32 devices in a mesh: dp: 8 (over z, y), fsdp: 4 (over x, core).
Axes of the slice: x: 2, y: 2, z: 4, core: 2. Of those that a mesh axis runs over, the one named last changes fastest.
Arguments:
- tokens: bfloat16 [16384, 768], P(('dp', 'fsdp')), may hold values from -6 to 6
- coordinates: int32 [2, 16384], P(None, ('dp', 'fsdp')), may hold values from 0 to 1000
- lengths: int32 [32], P(('dp', 'fsdp')), may hold values from 1 to 512, as said below
- cotangent: bfloat16 [16384, 768], P(('dp', 'fsdp')), may hold values from -6 to 6
- projector: bfloat16 [768, 2304], P(('dp', 'fsdp')), may hold values from -0.21875 to 0.21875
- intercept: bfloat16 [2304], P(('dp', 'fsdp')), may hold values from -1 to 1
- relative: bfloat16 [1536, 768], P(('dp', 'fsdp')), may hold values from -0.5 to 0.5
- combiner: bfloat16 [768, 768], P(('dp', 'fsdp')), may hold values from -1.75 to 1.75
- baseline: bfloat16 [768], P(('dp', 'fsdp')), may hold values from -1 to 1
- stretch: bfloat16 [768], P(('dp', 'fsdp')), may hold values from 0.5 to 1.5
- center: bfloat16 [768], P(('dp', 'fsdp')), may hold values from -1 to 1
- expander: bfloat16 [768, 3072], P(('dp', 'fsdp')), may hold values from -0.21875 to 0.21875
- uplift: bfloat16 [3072], P(('dp', 'fsdp')), may hold values from -1 to 1
- reducer: bfloat16 [3072, 768], P(('dp', 'fsdp')), may hold values from -0.109375 to 0.109375
- offset: bfloat16 [768], P(('dp', 'fsdp')), may hold values from -1 to 1
- rescale: bfloat16 [768], P(('dp', 'fsdp')), may hold values from 0.5 to 1.5
- recenter: bfloat16 [768], P(('dp', 'fsdp')), may hold values from -1 to 1
Outputs:
- activations: bfloat16 [16384, 768], P(('dp', 'fsdp'))
- token_gradient: bfloat16 [16384, 768], P(('dp', 'fsdp'))
- projector_gradient: float32 [768, 2304], P(('dp', 'fsdp'))
- intercept_gradient: float32 [2304], P(('dp', 'fsdp'))
- relative_gradient: float32 [1536, 768], P(('dp', 'fsdp'))
- combiner_gradient: float32 [768, 768], P(('dp', 'fsdp'))
- baseline_gradient: float32 [768], P(('dp', 'fsdp'))
- stretch_gradient: float32 [768], P(('dp', 'fsdp'))
- center_gradient: float32 [768], P(('dp', 'fsdp'))
- expander_gradient: float32 [768, 3072], P(('dp', 'fsdp'))
- uplift_gradient: float32 [3072], P(('dp', 'fsdp'))
- reducer_gradient: float32 [3072, 768], P(('dp', 'fsdp'))
- offset_gradient: float32 [768], P(('dp', 'fsdp'))
- rescale_gradient: float32 [768], P(('dp', 'fsdp'))
- recenter_gradient: float32 [768], P(('dp', 'fsdp'))
The draws below stay inside these ranges and needn't reach their ends.
Inputs may be any that keep to these rules, and one draw needn't show every extreme that they name: `lengths`: live tokens of each page; the first page is always full.
All inputs are finite; a program needn't handle non-finite values.
Results may differ from the reference program's by a relative error of at most 0.018.
Values may be sent and summed in bfloat16 or wider, within the bound.
A program may use at most 256 MiB of HBM per device.

```python
import jax
import jax.numpy as jnp
from jax import lax

D = 768
HEADS = 12
DH = 64
FF = 3072
FREQ = 192
PAGE = 512
GRID = 1000
PAGES = 32
TOKENS = 16384


def draw_lengths(key, part):
    subkeys = jax.random.split(key, 3)
    complete = jax.random.randint(subkeys[0], (PAGES,), 0, 2)
    divisor = jax.random.randint(subkeys[1], (PAGES,), 1, 9)
    surplus = jax.random.randint(subkeys[2], (PAGES,), 0, PAGE // 8 + 1)
    shorter = jnp.minimum(PAGE // divisor + surplus, PAGE)
    drawn = jnp.where(complete == 0, PAGE, shorter)
    return drawn.at[0].set(PAGE).astype(jnp.int32)


def place_ends(entries, rng, low, high):
    extent = entries.shape
    spot = [jax.random.randint(jax.random.fold_in(rng, axis), (), 0, extent[axis]) for axis in range(len(extent))]
    entries = entries.at[tuple(spot)].set(low)
    longest = extent.index(max(extent))
    spot[longest] = (spot[longest] + 1) % extent[longest]
    return entries.at[tuple(spot)].set(high)


def with_spikes(values, key, source, target, shards_of, factor):
    def block_of(axis_at):
        return (jnp.arange(values.shape[axis_at]) // (values.shape[axis_at] // shards_of)).reshape((-1,) + (1,) * (values.ndim - 1 - axis_at))

    first = jax.random.permutation(key, shards_of)[block_of(target)]
    second = (block_of(target) + shards_of // 2) % shards_of
    return jnp.where((block_of(source) == first) | (block_of(source) == second), factor * values, values)


def steps_of(own_key, extent, cuts, least, largest):
    def one(position, parts):
        steps = jax.random.uniform(jax.random.fold_in(jax.random.fold_in(own_key, 6), position), (parts,), jnp.float32, least / len(cuts), largest / len(cuts))
        return jnp.repeat(jnp.exp(steps), extent[position] // parts).reshape((-1,) + (1,) * (len(extent) - position - 1))

    factor_of = one(*cuts[0])
    for cut in cuts[1:]:
        factor_of = factor_of * one(*cut)
    return factor_of


def scatter_about(key, shape, scale, reach, cuts=(), kind=jnp.bfloat16):
    entries = jax.random.normal(key, shape, jnp.float32) * scale
    if len(cuts) > 0:
        entries = steps_of(key, shape, cuts, -0.22, 0.18) * entries
    return jnp.clip(entries, min=-reach, max=reach).astype(kind)


def bell_draw_with(own_key, dims, scale, reach, cuts, heavy, kind=jnp.bfloat16):
    entries = scale * jax.random.normal(own_key, dims, jnp.float32)
    if cuts:
        entries = entries * steps_of(own_key, dims, cuts, -0.22, 0.18)
    return jnp.clip(with_spikes(entries, jax.random.fold_in(own_key, 3), *heavy), -reach, reach).astype(kind)


def setup_inputs(seed: int = 0) -> dict:
    arg_keys = jax.random.split(jax.random.key(seed), 18)
    return {
        "tokens": bell_draw_with(arg_keys[0], (TOKENS, D), 1.0, 6.0, ((0, 32),), (0, 1, 32, 2.75)),
        "coordinates": place_ends(jax.random.randint(arg_keys[1], (2, TOKENS), 0, GRID + 1), jax.random.fold_in(arg_keys[1], 1), 0, GRID).astype(jnp.int32),
        "lengths": draw_lengths(jax.random.fold_in(arg_keys[17], 71), 0),
        "cotangent": bell_draw_with(arg_keys[3], (TOKENS, D), 1.0, 6.0, ((0, 32),), (0, 1, 32, 2.75)),
        "projector": scatter_about(arg_keys[4], (D, 3 * D), D ** -0.5, 0.21875, ((0, 32),)),
        "intercept": scatter_about(arg_keys[5], (3 * D,), 0.2, 1.0, ((0, 32),)),
        "relative": scatter_about(arg_keys[6], (8 * FREQ, D), (2 * DH) ** -0.5, 0.5, ((0, 32),)),
        "combiner": scatter_about(arg_keys[7], (D, D), (D // 64) ** -0.5, 1.75, ((0, 32),)),
        "baseline": scatter_about(arg_keys[8], (D,), 0.2, 1.0, ((0, 32),)),
        "stretch": jnp.clip(1.0 + 0.1 * jax.random.normal(arg_keys[9], (D,), jnp.float32), 0.5, 1.5).astype(jnp.bfloat16),
        "center": scatter_about(arg_keys[10], (D,), 0.2, 1.0, ((0, 32),)),
        "expander": scatter_about(arg_keys[11], (D, FF), D ** -0.5, 0.21875, ((0, 32),)),
        "uplift": scatter_about(arg_keys[12], (FF,), 0.2, 1.0, ((0, 32),)),
        "reducer": scatter_about(arg_keys[13], (FF, D), FF ** -0.5, 0.109375, ((0, 32),)),
        "offset": scatter_about(arg_keys[14], (D,), 0.2, 1.0, ((0, 32),)),
        "rescale": jnp.clip(1.0 + 0.1 * jax.random.normal(arg_keys[15], (D,), jnp.float32), 0.5, 1.5).astype(jnp.bfloat16),
        "recenter": scatter_about(arg_keys[16], (D,), 0.2, 1.0, ((0, 32),)),
    }


@jax.custom_vjp
def low(v):
    return lax.optimization_barrier(v.astype(jnp.bfloat16)).astype(jnp.float32)

@jax.custom_vjp
def low_back(v):
    return v

def low_keep(v):
    return (low(v), None)

def low_pass(kept, grad):
    return (grad,)

def back_keep(v):
    return (v, None)

def back_low(kept, grad):
    return (low(grad),)
low.defvjp(low_keep, low_pass)
low_back.defvjp(back_keep, back_low)
EPSILON = 1e-12
NEGATIVE = -1e+30
HIGHEST = lax.Precision.HIGHEST

def sinusoids(coordinates):
    steps_index = jnp.arange(FREQ, dtype=jnp.float32)
    frequency = jnp.exp(-jnp.log(10000.0) * steps_index / FREQ)
    angles = coordinates.astype(jnp.float32)[:, :, None] * frequency
    return jnp.concatenate([jnp.cos(angles[0]), jnp.sin(angles[0]), jnp.cos(angles[1]), jnp.sin(angles[1])], axis=1)

def rotate(weights, features):
    row_count, head_count = (weights.shape[0], weights.shape[1])
    halves = weights.reshape(row_count, head_count, 2, 2, FREQ)
    basis_view = features.reshape(row_count, 1, 2, 2, FREQ)
    cosine_part = basis_view[:, :, :, 0]
    sine_part = basis_view[:, :, :, 1]
    weight_sine = halves[:, :, :, 0]
    weight_cosine = halves[:, :, :, 1]
    leading = weight_sine * sine_part + weight_cosine * cosine_part
    trailing = weight_cosine * sine_part - weight_sine * cosine_part
    return jnp.stack([leading, trailing], axis=3).reshape(row_count, head_count, 4 * FREQ)

def normalize(hidden, scaling, shifting):
    center_part = hidden - lax.optimization_barrier(jnp.mean(hidden, axis=1, keepdims=True))
    variance = lax.optimization_barrier(jnp.mean(center_part * center_part, axis=1, keepdims=True))
    return center_part * lax.rsqrt(variance + EPSILON) * scaling + shifting

def page_attention(inputs, query_side, key_side):
    query_rows, key_rows, value_rows, features, length = inputs
    query_heads = query_rows.reshape(PAGE, HEADS, DH)
    key_heads = key_rows.reshape(PAGE, HEADS, DH)
    value_heads = value_rows.reshape(PAGE, HEADS, DH)
    query_weights = low_back(jnp.einsum('thn,fhn->thf', query_heads, query_side.reshape(4 * FREQ, HEADS, DH), precision=HIGHEST))
    key_weights = low_back(jnp.einsum('thn,fhn->thf', key_heads, key_side.reshape(4 * FREQ, HEADS, DH), precision=HIGHEST))
    left_terms = low(rotate(query_weights, features))
    right_terms = low(rotate(key_weights, features))
    shared = jnp.broadcast_to(features[:, None, :], (PAGE, HEADS, 4 * FREQ))
    query_cat = jnp.concatenate([left_terms, query_heads, shared], axis=2)
    key_cat = jnp.concatenate([shared, key_heads, right_terms], axis=2)
    scores = low_back(jnp.einsum('qhc,khc->hqk', query_cat, key_cat, precision=HIGHEST)) * (3.0 * DH) ** (-0.5)
    visible = jnp.arange(PAGE) < length
    scores = jnp.where(visible[None, None, :], scores, NEGATIVE)
    highest = lax.optimization_barrier(jnp.max(scores, axis=2, keepdims=True))
    powers = jnp.exp(scores - highest)
    weighting = low(powers / lax.optimization_barrier(jnp.sum(powers, axis=2, keepdims=True)))
    mixture = jnp.einsum('hqk,khn->qhn', weighting, value_heads, precision=HIGHEST)
    return mixture.reshape(PAGE, HEADS * DH)

def layer(tokens, features, lengths, projector, intercept, relative, combiner, baseline, stretch, center, expander, uplift, reducer, offset, rescale, recenter):
    model_width = tokens.shape[1]
    projected = jnp.dot(tokens, projector, precision=HIGHEST) + intercept
    query_rows = low(low_back(projected[:, :model_width]))
    key_rows = low(low_back(projected[:, model_width:2 * model_width]))
    value_rows = low(low_back(projected[:, 2 * model_width:]))
    query_side = relative[:4 * FREQ]
    key_side = relative[4 * FREQ:]
    page_count = lengths.shape[0]
    per_page = jax.checkpoint(page_attention)

    def one_page(inputs):
        return per_page(inputs, query_side, key_side)
    pages = (query_rows.reshape(page_count, PAGE, model_width), key_rows.reshape(page_count, PAGE, model_width), value_rows.reshape(page_count, PAGE, model_width), features.reshape(page_count, PAGE, 4 * FREQ), lengths)
    mixture = low(low_back(lax.map(one_page, pages).reshape(page_count * PAGE, model_width)))
    branch = low_back(jnp.dot(mixture, combiner, precision=HIGHEST) + baseline)
    first_out = normalize(tokens + branch, stretch, center)
    inner_sum = low_back(jnp.dot(low(first_out), expander, precision=HIGHEST) + uplift)
    activated = low(jax.nn.gelu(inner_sum, approximate=False))
    reduced = low_back(jnp.dot(activated, reducer, precision=HIGHEST) + offset)
    return normalize(first_out + reduced, rescale, recenter)

def reference(tokens, coordinates, lengths, cotangent, projector, intercept, relative, combiner, baseline, stretch, center, expander, uplift, reducer, offset, rescale, recenter):
    features = low(sinusoids(coordinates))
    params = [value.astype(jnp.float32) for value in (projector, intercept, relative, combiner, baseline, stretch, center, expander, uplift, reducer, offset, rescale, recenter)]

    def forward(inputs, *weights):
        return layer(inputs, features, lengths, *weights)
    result, pullback = jax.vjp(forward, tokens.astype(jnp.float32), *params)
    gradients = pullback(cotangent.astype(jnp.float32))
    return (result.astype(jnp.bfloat16), gradients[0].astype(jnp.bfloat16), gradients[1], gradients[2], gradients[3], gradients[4], gradients[5], gradients[6], gradients[7], gradients[8], gradients[9], gradients[10], gradients[11], gradients[12], gradients[13])
```

```python
import functools
from functools import partial

import jax
import jax.numpy as jnp
from jax import lax
from jax.experimental import pallas as pl
from jax.experimental.pallas import tpu as pltpu
from jax.sharding import PartitionSpec as P

HEADS = 12
DH = 64
FREQ = 192
PAGE = 512


EPSILON = 1e-12
NEGATIVE = -1e30


def sinusoids(coordinates):
    steps_index = jnp.arange(FREQ, dtype=jnp.float32)
    frequency = jnp.exp(-jnp.log(10000.0) * steps_index / FREQ)
    angles = coordinates.astype(jnp.float32)[:, :, None] * frequency
    return jnp.concatenate(
        [jnp.cos(angles[0]), jnp.sin(angles[0]), jnp.cos(angles[1]), jnp.sin(angles[1])], axis=1
    )


def rotate(weights, features):
    row_count, head_count = (weights.shape[0], weights.shape[1])
    halves = weights.reshape(row_count, head_count, 2, 2, FREQ)
    basis_view = features.reshape(row_count, 1, 2, 2, FREQ)
    cosine_part = basis_view[:, :, :, 0]
    sine_part = basis_view[:, :, :, 1]
    weight_sine = halves[:, :, :, 0]
    weight_cosine = halves[:, :, :, 1]
    leading = weight_sine * sine_part + weight_cosine * cosine_part
    trailing = weight_cosine * sine_part - weight_sine * cosine_part
    return jnp.stack([leading, trailing], axis=3).reshape(row_count, head_count, 4 * FREQ)


def rotate_back(upstream, features):
    row_count, head_count = (upstream.shape[0], upstream.shape[1])
    halves = upstream.reshape(row_count, head_count, 2, 2, FREQ)
    basis_view = features.reshape(row_count, 1, 2, 2, FREQ)
    cosine_part = basis_view[:, :, :, 0]
    sine_part = basis_view[:, :, :, 1]
    leading = halves[:, :, :, 0]
    trailing = halves[:, :, :, 1]
    sine_back = leading * sine_part - trailing * cosine_part
    cosine_back = leading * cosine_part + trailing * sine_part
    return jnp.stack([sine_back, cosine_back], axis=3).reshape(row_count, head_count, 4 * FREQ)


def normalize(hidden, scaling, shifting):
    center_part = hidden - jnp.mean(hidden, axis=1, keepdims=True)
    inverse = lax.rsqrt(jnp.mean(center_part * center_part, axis=1, keepdims=True) + EPSILON)
    normed = center_part * inverse
    return (normed * scaling + shifting, normed, inverse)


def normalize_back(upstream, normed, inverse, scaling):
    scaled = upstream * scaling
    return inverse * (
        scaled
        - jnp.mean(scaled, axis=1, keepdims=True)
        - normed * jnp.mean(scaled * normed, axis=1, keepdims=True)
    )


def encode(query_rows, key_rows, features, query_side, key_side):
    row_count = query_rows.shape[0]
    query_heads = query_rows.reshape(row_count, HEADS, DH)
    key_heads = key_rows.reshape(row_count, HEADS, DH)
    query_weights = jnp.einsum(
        "thn,fhn->thf",
        query_heads,
        query_side.reshape(4 * FREQ, HEADS, DH),
        preferred_element_type=jnp.float32,
    )
    key_weights = jnp.einsum(
        "thn,fhn->thf",
        key_heads,
        key_side.reshape(4 * FREQ, HEADS, DH),
        preferred_element_type=jnp.float32,
    )
    wide_features = features.astype(jnp.float32)
    left_terms = rotate(query_weights, wide_features).astype(jnp.bfloat16)
    right_terms = rotate(key_weights, wide_features).astype(jnp.bfloat16)
    shared = jnp.broadcast_to(features[:, None, :], (row_count, HEADS, 4 * FREQ))
    query_cat = jnp.concatenate([left_terms, query_heads, shared], axis=2)
    key_cat = jnp.concatenate([shared, key_heads, right_terms], axis=2)
    return (query_cat, key_cat)


def page_scores(query_cat, key_cat, length):
    scores = jnp.einsum("qhc,khc->hqk", query_cat, key_cat, preferred_element_type=jnp.float32) * (
        3.0 * DH
    ) ** (-0.5)
    visible = jnp.arange(key_cat.shape[0]) < length
    return jnp.where(visible[None, None, :], scores, NEGATIVE)


def page_forward(inputs, query_side, key_side):
    query_rows, key_rows, value_rows, features, length = inputs
    row_count = value_rows.shape[0]
    query_cat, key_cat = encode(query_rows, key_rows, features, query_side, key_side)
    scores = page_scores(query_cat, key_cat, length)
    highest = jnp.max(scores, axis=2, keepdims=True)
    powers = jnp.exp(scores - highest)
    totals = jnp.sum(powers, axis=2, keepdims=True)
    weighting = (powers / totals).astype(jnp.bfloat16)
    mixture = jnp.einsum(
        "hqk,khn->qhn",
        weighting,
        value_rows.reshape(row_count, HEADS, DH),
        preferred_element_type=jnp.float32,
    )
    return (
        mixture.reshape(row_count, HEADS * DH).astype(jnp.bfloat16),
        (highest + jnp.log(totals))[:, :, 0],
    )


def page_backward(accumulated, inputs, query_side, key_side):
    query_rows, key_rows, value_rows, features, length, log_total, mixture_back = inputs
    row_count = query_rows.shape[0]
    query_cat, key_cat = encode(query_rows, key_rows, features, query_side, key_side)
    scores = page_scores(query_cat, key_cat, length)
    weighting = jnp.exp(scores - log_total[:, :, None])
    value_heads = value_rows.reshape(row_count, HEADS, DH)
    back_heads = mixture_back.reshape(row_count, HEADS, DH)
    weighting_back = jnp.einsum(
        "qhn,khn->hqk", back_heads, value_heads, preferred_element_type=jnp.float32
    )
    centered = weighting_back - jnp.sum(weighting * weighting_back, axis=2, keepdims=True)
    score_back = (weighting * centered * (3.0 * DH) ** (-0.5)).astype(jnp.bfloat16)
    value_back = jnp.einsum(
        "hqk,qhn->khn",
        weighting.astype(jnp.bfloat16),
        back_heads,
        preferred_element_type=jnp.float32,
    )
    query_part = jnp.einsum(
        "hqk,khc->qhc",
        score_back,
        key_cat[:, :, : 4 * FREQ + DH],
        preferred_element_type=jnp.float32,
    )
    key_part = jnp.einsum(
        "hqk,qhc->khc", score_back, query_cat[:, :, 4 * FREQ :], preferred_element_type=jnp.float32
    )
    wide_features = features.astype(jnp.float32)
    query_weight_back = rotate_back(query_part[:, :, : 4 * FREQ], wide_features).astype(
        jnp.bfloat16
    )
    key_weight_back = rotate_back(key_part[:, :, DH:], wide_features).astype(jnp.bfloat16)
    query_table = query_side.reshape(4 * FREQ, HEADS, DH)
    key_table = key_side.reshape(4 * FREQ, HEADS, DH)
    query_back = query_part[:, :, 4 * FREQ :] + jnp.einsum(
        "thf,fhn->thn", query_weight_back, query_table, preferred_element_type=jnp.float32
    )
    key_back = key_part[:, :, :DH] + jnp.einsum(
        "thf,fhn->thn", key_weight_back, key_table, preferred_element_type=jnp.float32
    )
    query_heads = query_rows.reshape(row_count, HEADS, DH)
    key_heads = key_rows.reshape(row_count, HEADS, DH)
    query_total = accumulated[0] + jnp.einsum(
        "thf,thn->fhn", query_weight_back, query_heads, preferred_element_type=jnp.float32
    )
    key_total = accumulated[1] + jnp.einsum(
        "thf,thn->fhn", key_weight_back, key_heads, preferred_element_type=jnp.float32
    )
    outputs = (
        query_back.reshape(row_count, HEADS * DH).astype(jnp.bfloat16),
        key_back.reshape(row_count, HEADS * DH).astype(jnp.bfloat16),
        value_back.reshape(row_count, HEADS * DH).astype(jnp.bfloat16),
    )
    return ((query_total, key_total), outputs)


MESH = pl.DeviceIdType.MESH
NZ, NY, NX, NC = 4, 2, 2, 2


class Place:
    def __init__(self):
        d = lax.axis_index("dp")
        f = lax.axis_index("fsdp")
        self.z, self.y = d // NY, d % NY
        self.x, self.c = f // NC, f % NC
        z, y, x, c = self.z, self.y, self.x, self.c
        self.y1, self.x1 = y + (1 - c) * (1 - 2 * y), x + c * (1 - 2 * x)
        self.y2, self.x2 = y + c * (1 - 2 * y), x + (1 - c) * (1 - 2 * x)
        self.first = (z * NY + self.y1, self.x1 * NC + c)
        self.second = (z * NY + self.y2, self.x2 * NC + c)
        self.sibling = (z * NY + y, x * NC + 1 - c)

    def along_z(self, z):
        return (z * NY + self.y, self.x * NC + self.c)

    def peers(self):
        return [self.first, self.second, self.sibling] + [self.along_z((self.z + s) % NZ) for s in (1, 2, 3)]


def enter(place):
    barrier = pltpu.get_barrier_semaphore()
    peers = place.peers()
    for peer in peers:
        pl.semaphore_signal(barrier, inc=1, device_id=peer, device_id_type=MESH)
    pl.semaphore_wait(barrier, len(peers))


def gather_kernel(n, *refs):
    shards, full = refs[:n], refs[n : 2 * n]
    local, send, recv = refs[2 * n :]
    p = Place()
    z, y, x, c = p.z, p.y, p.x, p.c
    enter(p)

    def remote(w, src, dst, s, r, device):
        return pltpu.make_async_remote_copy(
            src_ref=src, dst_ref=dst, send_sem=send.at[w, s], recv_sem=recv.at[w, r], device_id=device, device_id_type=MESH
        )

    def block(w, by, bx, bc):
        return full[w].at[:, by, bx, bc]

    started = []

    def go(copy):
        copy.start()
        started.append(copy)

    own = []
    for w in range(n):
        cp = pltpu.make_async_copy(shards[w], full[w].at[z, y, x, c], local.at[w])
        cp.start()
        own.append(cp)
        for s in (1, 2, 3):
            go(remote(w, shards[w], full[w].at[z, y, x, c], s - 1, z, p.along_z((z + s) % NZ)))

    def arrived(w, ref, r):
        remote(w, ref, ref, 0, r, p.sibling).wait_recv()

    def stage_a(w):
        own[w].wait()
        for s in (1, 2, 3):
            zs = (z + s) % NZ
            arrived(w, full[w].at[zs, y, x, c], zs)
        a = block(w, y, x, c)
        go(remote(w, a, a, 3, 4, p.first))
        go(remote(w, a, a, 4, 5, p.second))
        go(remote(w, a, a, 5, 7, p.sibling))

    def stage_b(w):
        b = block(w, p.y1, p.x1, c)
        arrived(w, b, 4)
        go(remote(w, b, b, 6, 6, p.second))
        go(remote(w, b, b, 7, 8, p.sibling))

    def stage_c(w):
        b = block(w, p.y2, p.x2, c)
        arrived(w, b, 5)
        go(remote(w, b, b, 8, 9, p.sibling))
        b = block(w, 1 - y, 1 - x, c)
        arrived(w, b, 6)
        go(remote(w, b, b, 9, 10, p.sibling))

    def stage_d(w):
        for r in range(7, 11):
            arrived(w, block(w, y, x, 1 - c), r)

    for step in range(n + 3):
        if step < n:
            stage_a(step)
        if 0 <= step - 1 < n:
            stage_b(step - 1)
        if 0 <= step - 2 < n:
            stage_c(step - 2)
        if 0 <= step - 3 < n:
            stage_d(step - 3)
    for copy in started:
        copy.wait_send()


def gather_all(shards, cid):
    n = len(shards)
    outs = [jax.ShapeDtypeStruct((NZ, NY, NX, NC) + s.shape, s.dtype) for s in shards]
    full = pl.pallas_call(
        functools.partial(gather_kernel, n),
        out_shape=outs,
        in_specs=[pl.BlockSpec(memory_space=pl.ANY)] * n,
        out_specs=[pl.BlockSpec(memory_space=pl.ANY)] * n,
        scratch_shapes=[
            pltpu.SemaphoreType.DMA((n,)),
            pltpu.SemaphoreType.DMA((n, 10)),
            pltpu.SemaphoreType.DMA((n, 11)),
        ],
        compiler_params=pltpu.CompilerParams(collective_id=cid, has_side_effects=True),
        name="gather_all",
    )(*shards)
    return [f.reshape((32 * s.shape[0],) + s.shape[1:]) for f, s in zip(full, shards)]


def add_into(dst, a, b, rows, cols):
    dst[...] = (a[...].astype(jnp.float32) + b[...].astype(jnp.float32)).astype(dst.dtype)


def scatter_kernel(n, *refs):
    grads, outs = refs[:n], refs[n : 2 * n]
    held = refs[2 * n : 3 * n]
    second = refs[3 * n : 4 * n]
    firsts = refs[4 * n : 5 * n]
    alongs = refs[5 * n : 6 * n]
    send, recv = refs[6 * n :]
    p = Place()
    z, y, x, c = p.z, p.y, p.x, p.c
    enter(p)
    started = []

    def remote(w, src, dst, s, r, device):
        return pltpu.make_async_remote_copy(
            src_ref=src, dst_ref=dst, send_sem=send.at[w, s], recv_sem=recv.at[w, r], device_id=device, device_id_type=MESH
        )

    def go(copy):
        copy.start()
        started.append(copy)

    def arrived(w, ref, r):
        remote(w, ref, ref, 0, r, p.sibling).wait_recv()

    for w in range(n):
        go(remote(w, grads[w].at[:, :, :, 1 - c], held[w], 0, 0, p.sibling))

    def accumulate(w, by, bx, extra):
        @pl.loop(0, NZ)
        def _(k):
            held[w][k, by, bx] = (held[w][k, by, bx].astype(jnp.float32) + extra(k).astype(jnp.float32)).astype(jnp.bfloat16)

    def stage_s(w):
        arrived(w, held[w], 0)
        for by, bx in ((1 - y, 1 - x), (p.y2, p.x2), (p.y1, p.x1), (y, x)):
            accumulate(w, by, bx, lambda k: grads[w][k, by, bx, c])
            if by is not p.y1 and by is not y:
                pass
        go(remote(w, held[w].at[:, 1 - y, 1 - x], second[w].at[0], 1, 1, p.second))
        go(remote(w, held[w].at[:, p.y2, p.x2], second[w].at[1], 2, 2, p.second))

    def stage_x(w):
        arrived(w, second[w].at[0], 1)
        accumulate(w, p.y1, p.x1, lambda k: second[w][0, k])
        go(remote(w, held[w].at[:, p.y1, p.x1], firsts[w], 3, 3, p.first))
        arrived(w, second[w].at[1], 2)
        accumulate(w, y, x, lambda k: second[w][1, k])

    def stage_f(w):
        arrived(w, firsts[w], 3)
        accumulate(w, y, x, lambda k: firsts[w][k])
        for s in (1, 2, 3):
            zt = (z + s) % NZ
            go(remote(w, held[w].at[zt, y, x], alongs[w].at[z], 3 + s, 4 + z, p.along_z(zt)))

    def stage_z(w):
        total = held[w][z, y, x].astype(jnp.float32)
        for s in (1, 2, 3):
            zs = (z + s) % NZ
            arrived(w, alongs[w].at[zs], 4 + zs)
            total += alongs[w][zs].astype(jnp.float32)
        outs[w][...] = total

    for step in range(n + 3):
        if step < n:
            stage_s(step)
        if 0 <= step - 1 < n:
            stage_x(step - 1)
        if 0 <= step - 2 < n:
            stage_f(step - 2)
        if 0 <= step - 3 < n:
            stage_z(step - 3)
    for copy in started:
        copy.wait_send()


def scatter_all(grads, cid):
    n = len(grads)
    shards = [(g.shape[0] // 32, g.shape[1]) for g in grads]
    views = [g.reshape((NZ, NY, NX, NC) + s) for g, s in zip(grads, shards)]
    vm = pl.BlockSpec(memory_space=pltpu.VMEM)
    return pl.pallas_call(
        functools.partial(scatter_kernel, n),
        out_shape=[jax.ShapeDtypeStruct(s, jnp.float32) for s in shards],
        in_specs=[vm] * n,
        out_specs=[vm] * n,
        scratch_shapes=[pltpu.VMEM((NZ, NY, NX) + s, jnp.bfloat16) for s in shards]
        + [pltpu.VMEM((2, NZ) + s, jnp.bfloat16) for s in shards]
        + [pltpu.VMEM((NZ,) + s, jnp.bfloat16) for s in shards]
        + [pltpu.VMEM((NZ,) + s, jnp.bfloat16) for s in shards]
        + [pltpu.SemaphoreType.DMA((n, 7)), pltpu.SemaphoreType.DMA((n, 8))],
        compiler_params=pltpu.CompilerParams(collective_id=cid, has_side_effects=True, vmem_limit_bytes=60 << 20),
        name="scatter_all",
    )(*views)

LANES = 384


def widths(vectors):
    return [v.shape[0] for v in vectors]


def collect(matrices, vectors, remote):
    if not remote:
        gather = lambda v: lax.all_gather(v, ("dp", "fsdp"), axis=0, tiled=True)
        packed = jnp.concatenate(vectors)
        rows = gather(packed[None, :])
        full = [gather(m) for m in matrices]
        parts = []
        at = 0
        for w in widths(vectors):
            parts.append(rows[:, at : at + w].reshape(-1))
            at += w
        return (*full, parts)
    packed = jnp.concatenate(vectors)
    packed = jnp.zeros((8, LANES), jnp.bfloat16).at[0, : packed.shape[0]].set(packed)
    gathered = gather_all(list(matrices) + [packed], 0)
    rows = gathered[-1].reshape(32, 8, LANES)[:, 0]
    parts = []
    at = 0
    for w in widths(vectors):
        parts.append(rows[:, at : at + w].reshape(-1))
        at += w
    return (*gathered[:-1], parts)


def spread(changes, vectors, remote):
    if not remote:
        def both(v):
            v = lax.psum_scatter(v, "dp", scatter_dimension=0, tiled=True)
            v = lax.psum_scatter(v.astype(jnp.bfloat16), "fsdp", scatter_dimension=0, tiled=True)
            return v.astype(jnp.float32)

        return (*[both(c) for c in changes], [both(v) for v in vectors])
    sizes = [v.shape[0] // 32 for v in vectors]
    packed = jnp.concatenate([v.reshape(32, -1) for v in vectors], axis=1).astype(jnp.bfloat16)
    packed = jnp.zeros((32, 8, LANES), jnp.bfloat16).at[:, 0, : packed.shape[1]].set(packed).reshape(256, LANES)
    grads = [changes[i].astype(jnp.bfloat16) for i in (4, 3, 2, 1, 0)] + [packed]
    out = scatter_all(grads, 1)
    row = out[-1][0]
    parts = []
    at = 0
    for w in sizes:
        parts.append(row[at : at + w])
        at += w
    return (*[out[i] for i in (4, 3, 2, 1, 0)], parts)


def local(
    tokens,
    coordinates,
    lengths,
    cotangent,
    projector,
    intercept,
    relative,
    combiner,
    baseline,
    stretch,
    center,
    expander,
    uplift,
    reducer,
    offset,
    rescale,
    recenter,
    remote,
):
    model_width = tokens.shape[1]
    page_count = lengths.shape[0]
    vectors = (intercept, uplift, baseline, stretch, center, offset, rescale, recenter)
    matrices = (projector, relative, combiner, expander, reducer)
    (
        full_projector, full_relative, full_combiner, full_expander, full_reducer,
        (full_intercept, full_uplift, full_baseline, full_stretch, full_center, full_offset, full_rescale, full_recenter),
    ) = collect(matrices, vectors, remote)
    features = sinusoids(coordinates).astype(jnp.bfloat16)
    projected = jnp.dot(
        tokens, full_projector, preferred_element_type=jnp.float32
    ) + full_intercept.astype(jnp.float32)
    query_rows = projected[:, :model_width].astype(jnp.bfloat16)
    key_rows = projected[:, model_width : 2 * model_width].astype(jnp.bfloat16)
    value_rows = projected[:, 2 * model_width :].astype(jnp.bfloat16)
    page_view = (
        query_rows.reshape(page_count, PAGE, model_width),
        key_rows.reshape(page_count, PAGE, model_width),
        value_rows.reshape(page_count, PAGE, model_width),
        features.reshape(page_count, PAGE, 4 * FREQ),
    )
    mixture, log_totals = lax.map(
        partial(
            page_forward, query_side=full_relative[: 4 * FREQ], key_side=full_relative[4 * FREQ :]
        ),
        page_view + (lengths,),
    )
    mixture = mixture.reshape(page_count * PAGE, model_width)
    branch = jnp.dot(
        mixture, full_combiner, preferred_element_type=jnp.float32
    ) + full_baseline.astype(jnp.float32)
    first_out, first_normed, first_inverse = normalize(
        tokens.astype(jnp.float32) + branch,
        full_stretch.astype(jnp.float32),
        full_center.astype(jnp.float32),
    )
    first_low = first_out.astype(jnp.bfloat16)
    inner_sum = jnp.dot(
        first_low, full_expander, preferred_element_type=jnp.float32
    ) + full_uplift.astype(jnp.float32)
    activated = jax.nn.gelu(inner_sum, approximate=False).astype(jnp.bfloat16)
    second_sum = (
        first_out
        + jnp.dot(activated, full_reducer, preferred_element_type=jnp.float32)
        + full_offset.astype(jnp.float32)
    )
    result, second_normed, second_inverse = normalize(
        second_sum, full_rescale.astype(jnp.float32), full_recenter.astype(jnp.float32)
    )
    back_projector, back_relative, back_combiner, back_stretch = full_projector, full_relative, full_combiner, full_stretch
    back_expander, back_reducer, back_rescale = full_expander, full_reducer, full_rescale
    upstream = cotangent.astype(jnp.float32)
    rescale_change = jnp.sum(upstream * second_normed, axis=0)
    recenter_change = jnp.sum(upstream, axis=0)
    second_back = normalize_back(
        upstream, second_normed, second_inverse, back_rescale.astype(jnp.float32)
    )
    reduced_back = second_back.astype(jnp.bfloat16)
    offset_change = jnp.sum(reduced_back.astype(jnp.float32), axis=0)
    reducer_change = jnp.einsum(
        "tf,td->fd", activated, reduced_back, preferred_element_type=jnp.float32
    )
    activated_back = jnp.einsum(
        "td,fd->tf", reduced_back, back_reducer, preferred_element_type=jnp.float32
    )
    gelu_pullback = jax.vjp(partial(jax.nn.gelu, approximate=False), inner_sum)[1]
    inner_back = gelu_pullback(activated_back)[0].astype(jnp.bfloat16)
    uplift_change = jnp.sum(inner_back.astype(jnp.float32), axis=0)
    expander_change = jnp.einsum(
        "td,tf->df", first_low, inner_back, preferred_element_type=jnp.float32
    )
    first_back = second_back + jnp.einsum(
        "tf,df->td", inner_back, back_expander, preferred_element_type=jnp.float32
    )
    stretch_change = jnp.sum(first_back * first_normed, axis=0)
    center_change = jnp.sum(first_back, axis=0)
    sum_back = normalize_back(
        first_back, first_normed, first_inverse, back_stretch.astype(jnp.float32)
    )
    branch_back = sum_back.astype(jnp.bfloat16)
    baseline_change = jnp.sum(branch_back.astype(jnp.float32), axis=0)
    combiner_change = jnp.einsum(
        "td,te->de", mixture, branch_back, preferred_element_type=jnp.float32
    )
    mixture_back = jnp.einsum(
        "te,de->td", branch_back, back_combiner, preferred_element_type=jnp.float32
    ).astype(jnp.bfloat16)
    empty_table = jnp.zeros((4 * FREQ, HEADS, DH), jnp.float32)
    side_totals, page_grads = lax.scan(
        partial(
            page_backward, query_side=back_relative[: 4 * FREQ], key_side=back_relative[4 * FREQ :]
        ),
        (empty_table, empty_table),
        page_view + (lengths, log_totals, mixture_back.reshape(page_count, PAGE, model_width)),
    )
    relative_change = jnp.concatenate(
        [
            side_totals[0].reshape(4 * FREQ, model_width),
            side_totals[1].reshape(4 * FREQ, model_width),
        ],
        axis=0,
    )
    projected_back = jnp.concatenate([page_grads[0], page_grads[1], page_grads[2]], axis=2).reshape(
        page_count * PAGE, 3 * model_width
    )
    intercept_change = jnp.sum(projected_back.astype(jnp.float32), axis=0)
    projector_change = jnp.einsum(
        "td,te->de", tokens, projected_back, preferred_element_type=jnp.float32
    )
    token_change = (
        sum_back
        + jnp.einsum(
            "te,de->td", projected_back, back_projector, preferred_element_type=jnp.float32
        )
    ).astype(jnp.bfloat16)
    (
        projector_share, relative_share, combiner_share, expander_share, reducer_share,
        (intercept_share, uplift_share, baseline_share, stretch_share, center_share, offset_share, rescale_share, recenter_share),
    ) = spread(
        (projector_change, relative_change, combiner_change, expander_change, reducer_change),
        (intercept_change, uplift_change, baseline_change, stretch_change, center_change, offset_change, rescale_change, recenter_change),
        remote,
    )
    return (
        result.astype(jnp.bfloat16),
        token_change,
        projector_share,
        intercept_share,
        relative_share,
        combiner_share,
        baseline_share,
        stretch_share,
        center_share,
        expander_share,
        uplift_share,
        reducer_share,
        offset_share,
        rescale_share,
        recenter_share,
    )


def solution(mesh):
    placed = (
        P(("dp", "fsdp"), None),
        P(None, ("dp", "fsdp")),
        P(("dp", "fsdp")),
        P(("dp", "fsdp"), None),
        P(("dp", "fsdp"), None),
        P(("dp", "fsdp")),
        P(("dp", "fsdp"), None),
        P(("dp", "fsdp"), None),
        P(("dp", "fsdp")),
        P(("dp", "fsdp")),
        P(("dp", "fsdp")),
        P(("dp", "fsdp"), None),
        P(("dp", "fsdp")),
        P(("dp", "fsdp"), None),
        P(("dp", "fsdp")),
        P(("dp", "fsdp")),
        P(("dp", "fsdp")),
    )
    return jax.shard_map(
        partial(local, remote=tuple(mesh.shape.values()) == (NZ * NY, NX * NC)),
        mesh=mesh,
        in_specs=placed,
        out_specs=(
            P(("dp", "fsdp"), None),
            P(("dp", "fsdp"), None),
            P(("dp", "fsdp"), None),
            P(("dp", "fsdp")),
            P(("dp", "fsdp"), None),
            P(("dp", "fsdp"), None),
            P(("dp", "fsdp")),
            P(("dp", "fsdp")),
            P(("dp", "fsdp")),
            P(("dp", "fsdp"), None),
            P(("dp", "fsdp")),
            P(("dp", "fsdp"), None),
            P(("dp", "fsdp")),
            P(("dp", "fsdp")),
            P(("dp", "fsdp")),
        ),
        check_vma=False,
    )
```

```python
import functools
import types

import jax
import jax.numpy as jnp
from jax import lax
from jax.experimental import pallas as pl
from jax.experimental.pallas import tpu as pltpu
from jax.sharding import PartitionSpec as P

MESH = pl.DeviceIdType.MESH
NZ, NY, NX, NC = 4, 2, 2, 2


class Place:
    def __init__(self):
        d = lax.axis_index("dp")
        f = lax.axis_index("fsdp")
        self.z, self.y = d // NY, d % NY
        self.x, self.c = f // NC, f % NC
        z, y, x, c = self.z, self.y, self.x, self.c
        self.y1, self.x1 = y + (1 - c) * (1 - 2 * y), x + c * (1 - 2 * x)
        self.y2, self.x2 = y + c * (1 - 2 * y), x + (1 - c) * (1 - 2 * x)
        self.first = (z * NY + self.y1, self.x1 * NC + c)
        self.second = (z * NY + self.y2, self.x2 * NC + c)
        self.sibling = (z * NY + y, x * NC + 1 - c)

    def along_z(self, z):
        return (z * NY + self.y, self.x * NC + self.c)

    def peers(self):
        return [self.first, self.second, self.sibling] + [self.along_z((self.z + s) % NZ) for s in (1, 2, 3)]


def enter(place):
    barrier = pltpu.get_barrier_semaphore()
    peers = place.peers()
    for peer in peers:
        pl.semaphore_signal(barrier, inc=1, device_id=peer, device_id_type=MESH)
    pl.semaphore_wait(barrier, len(peers))


def gather_kernel(n, *refs):
    shards, full = refs[:n], refs[n : 2 * n]
    local, send, recv = refs[2 * n :]
    p = Place()
    z, y, x, c = p.z, p.y, p.x, p.c
    enter(p)

    def remote(w, src, dst, s, r, device):
        return pltpu.make_async_remote_copy(
            src_ref=src, dst_ref=dst, send_sem=send.at[w, s], recv_sem=recv.at[w, r], device_id=device, device_id_type=MESH
        )

    def block(w, by, bx, bc):
        return full[w].at[:, by, bx, bc]

    started = []

    def go(copy):
        copy.start()
        started.append(copy)

    own = []
    for w in range(n):
        cp = pltpu.make_async_copy(shards[w], full[w].at[z, y, x, c], local.at[w])
        cp.start()
        own.append(cp)
        for s in (1, 2, 3):
            go(remote(w, shards[w], full[w].at[z, y, x, c], s - 1, z, p.along_z((z + s) % NZ)))

    def arrived(w, ref, r):
        remote(w, ref, ref, 0, r, p.sibling).wait_recv()

    def stage_a(w):
        own[w].wait()
        for s in (1, 2, 3):
            zs = (z + s) % NZ
            arrived(w, full[w].at[zs, y, x, c], zs)
        a = block(w, y, x, c)
        go(remote(w, a, a, 3, 4, p.first))
        go(remote(w, a, a, 4, 5, p.second))
        go(remote(w, a, a, 5, 7, p.sibling))

    def stage_b(w):
        b = block(w, p.y1, p.x1, c)
        arrived(w, b, 4)
        go(remote(w, b, b, 6, 6, p.second))
        go(remote(w, b, b, 7, 8, p.sibling))

    def stage_c(w):
        b = block(w, p.y2, p.x2, c)
        arrived(w, b, 5)
        go(remote(w, b, b, 8, 9, p.sibling))
        b = block(w, 1 - y, 1 - x, c)
        arrived(w, b, 6)
        go(remote(w, b, b, 9, 10, p.sibling))

    def stage_d(w):
        for r in range(7, 11):
            arrived(w, block(w, y, x, 1 - c), r)

    for step in range(n + 3):
        if step < n:
            stage_a(step)
        if 0 <= step - 1 < n:
            stage_b(step - 1)
        if 0 <= step - 2 < n:
            stage_c(step - 2)
        if 0 <= step - 3 < n:
            stage_d(step - 3)
    for copy in started:
        copy.wait_send()


def gather_all(shards, cid):
    n = len(shards)
    outs = [jax.ShapeDtypeStruct((NZ, NY, NX, NC) + s.shape, s.dtype) for s in shards]
    full = pl.pallas_call(
        functools.partial(gather_kernel, n),
        out_shape=outs,
        in_specs=[pl.BlockSpec(memory_space=pl.ANY)] * n,
        out_specs=[pl.BlockSpec(memory_space=pl.ANY)] * n,
        scratch_shapes=[
            pltpu.SemaphoreType.DMA((n,)),
            pltpu.SemaphoreType.DMA((n, 10)),
            pltpu.SemaphoreType.DMA((n, 11)),
        ],
        compiler_params=pltpu.CompilerParams(collective_id=cid, has_side_effects=True),
        name="gather_all",
    )(*shards)
    return [f.reshape((32 * s.shape[0],) + s.shape[1:]) for f, s in zip(full, shards)]


def add_into(dst, a, b, rows, cols):
    dst[...] = (a[...].astype(jnp.float32) + b[...].astype(jnp.float32)).astype(dst.dtype)


def scatter_kernel(n, *refs):
    grads, outs = refs[:n], refs[n : 2 * n]
    held = refs[2 * n : 3 * n]
    second = refs[3 * n : 4 * n]
    firsts = refs[4 * n : 5 * n]
    alongs = refs[5 * n : 6 * n]
    send, recv = refs[6 * n :]
    p = Place()
    z, y, x, c = p.z, p.y, p.x, p.c
    enter(p)
    started = []

    def remote(w, src, dst, s, r, device):
        return pltpu.make_async_remote_copy(
            src_ref=src, dst_ref=dst, send_sem=send.at[w, s], recv_sem=recv.at[w, r], device_id=device, device_id_type=MESH
        )

    def go(copy):
        copy.start()
        started.append(copy)

    def arrived(w, ref, r):
        remote(w, ref, ref, 0, r, p.sibling).wait_recv()

    for w in range(n):
        go(remote(w, grads[w].at[:, :, :, 1 - c], held[w], 0, 0, p.sibling))

    def accumulate(w, by, bx, extra):
        @pl.loop(0, NZ)
        def _(k):
            held[w][k, by, bx] = (held[w][k, by, bx].astype(jnp.float32) + extra(k).astype(jnp.float32)).astype(jnp.bfloat16)

    def stage_s(w):
        arrived(w, held[w], 0)
        for by, bx in ((1 - y, 1 - x), (p.y2, p.x2), (p.y1, p.x1), (y, x)):
            accumulate(w, by, bx, lambda k: grads[w][k, by, bx, c])
            if by is not p.y1 and by is not y:
                pass
        go(remote(w, held[w].at[:, 1 - y, 1 - x], second[w].at[0], 1, 1, p.second))
        go(remote(w, held[w].at[:, p.y2, p.x2], second[w].at[1], 2, 2, p.second))

    def stage_x(w):
        arrived(w, second[w].at[0], 1)
        accumulate(w, p.y1, p.x1, lambda k: second[w][0, k])
        go(remote(w, held[w].at[:, p.y1, p.x1], firsts[w], 3, 3, p.first))
        arrived(w, second[w].at[1], 2)
        accumulate(w, y, x, lambda k: second[w][1, k])

    def stage_f(w):
        arrived(w, firsts[w], 3)
        accumulate(w, y, x, lambda k: firsts[w][k])
        for s in (1, 2, 3):
            zt = (z + s) % NZ
            go(remote(w, held[w].at[zt, y, x], alongs[w].at[z], 3 + s, 4 + z, p.along_z(zt)))

    def stage_z(w):
        total = held[w][z, y, x].astype(jnp.float32)
        for s in (1, 2, 3):
            zs = (z + s) % NZ
            arrived(w, alongs[w].at[zs], 4 + zs)
            total += alongs[w][zs].astype(jnp.float32)
        outs[w][...] = total

    for step in range(n + 3):
        if step < n:
            stage_s(step)
        if 0 <= step - 1 < n:
            stage_x(step - 1)
        if 0 <= step - 2 < n:
            stage_f(step - 2)
        if 0 <= step - 3 < n:
            stage_z(step - 3)
    for copy in started:
        copy.wait_send()


def scatter_all(grads, cid):
    n = len(grads)
    shards = [(g.shape[0] // 32, g.shape[1]) for g in grads]
    views = [g.reshape((NZ, NY, NX, NC) + s) for g, s in zip(grads, shards)]
    vm = pl.BlockSpec(memory_space=pltpu.VMEM)
    return pl.pallas_call(
        functools.partial(scatter_kernel, n),
        out_shape=[jax.ShapeDtypeStruct(s, jnp.float32) for s in shards],
        in_specs=[vm] * n,
        out_specs=[vm] * n,
        scratch_shapes=[pltpu.VMEM((NZ, NY, NX) + s, jnp.bfloat16) for s in shards]
        + [pltpu.VMEM((2, NZ) + s, jnp.bfloat16) for s in shards]
        + [pltpu.VMEM((NZ,) + s, jnp.bfloat16) for s in shards]
        + [pltpu.VMEM((NZ,) + s, jnp.bfloat16) for s in shards]
        + [pltpu.SemaphoreType.DMA((n, 7)), pltpu.SemaphoreType.DMA((n, 8))],
        compiler_params=pltpu.CompilerParams(collective_id=cid, has_side_effects=True, vmem_limit_bytes=60 << 20),
        name="scatter_all",
    )(*views)


PAGE = 512
D = 768
FF = 3072
HALF = 384
PAIRS = 6
SCALE = 192.0 ** -0.5
EPSILON = 1e-12
NEGATIVE = -1e30
BF = jnp.bfloat16
F32 = jnp.float32
ROWS = 128
PIECE = 256


def nn(a, b):
    return jnp.dot(a, b, preferred_element_type=F32)


def nt(a, b):
    return lax.dot_general(a, b, (((1,), (1,)), ((), ())), preferred_element_type=F32)


def span(i, size):
    return pl.ds(pl.multiple_of(i * size, size), size)


def own_lanes(e, rows):
    lane = lax.broadcasted_iota(jnp.int32, (rows, 128), 1)
    return lane < 64 if e == 0 else lane >= 64


def only(e, v):
    return jnp.where(own_lanes(e, v.shape[0]), v, jnp.zeros_like(v))


def only_rows(e, v):
    row = lax.broadcasted_iota(jnp.int32, v.shape, 0)
    return jnp.where(row < 64 if e == 0 else row >= 64, v, jnp.zeros_like(v))


def project(tokens, projector, intercept, qkv):
    @pl.loop(0, 9)
    def _(n):
        cols = span(n, PIECE)
        qkv[:, cols] = (nn(tokens[...], projector[:, cols]) + intercept[:, cols]).astype(BF)


def table(relative, side, half, cols):
    return relative[2 * side : 2 * side + 2, half, :, :, :, cols].reshape(HALF, 128)


def turn(weights_of, feats, out, at, rows):
    ws, wc = weights_of
    c = feats[rows, :HALF].astype(F32)
    s = feats[rows, HALF:].astype(F32)
    out[rows, at : at + HALF] = (ws * s + wc * c).astype(BF)
    out[rows, at + HALF : at + 2 * HALF] = (wc * s - ws * c).astype(BF)


def attend_setup(feats, left, right):
    left[:, D + 128 :] = feats[...]
    right[:, :D] = feats[...]


def attend_pair(p, qkv, relative, feats, live, left, right, probs, mixture):
    lanes = span(p, 128)
    q2 = qkv[:, lanes]
    k2 = qkv[:, span(p + PAIRS, 128)]
    v2 = qkv[:, span(p + 2 * PAIRS, 128)]
    for e in (0, 1):
        left[:, D : D + 128] = only(e, q2)
        right[:, D : D + 128] = only(e, k2)

        every = slice(None)
        q = left[:, D : D + 128]
        k = right[:, D : D + 128]
        turn((nt(q, table(relative, 0, 0, lanes)), nt(q, table(relative, 0, 1, lanes))), feats, left, 0, every)
        turn((nt(k, table(relative, 1, 0, lanes)), nt(k, table(relative, 1, 1, lanes))), feats, right, D + 128, every)
        scores = nt(left[...], right[...]) * SCALE
        key = lax.broadcasted_iota(jnp.int32, scores.shape, 1)
        scores = jnp.where(key < live, scores, NEGATIVE)
        powers = jnp.exp(scores - jnp.max(scores, axis=1, keepdims=True))
        share = (powers / jnp.sum(powers, axis=1, keepdims=True)).astype(BF)
        probs[2 * p + e] = share
        part = nn(share, only(e, v2))
        if e == 0:
            mixture[:, lanes] = part.astype(BF)
        else:
            mixture[:, lanes] = jnp.where(own_lanes(1, PAGE), part.astype(BF), mixture[:, lanes])


def mean(v):
    return jnp.sum(v, axis=1, keepdims=True) * (1.0 / D)


def first_norm(tokens, mixture, combiner, vec, hold, n1, r1, low):
    @pl.loop(0, 3)
    def _(n):
        cols = span(n, PIECE)
        hold[:, cols] = nn(mixture[...], combiner[:, cols])

    @pl.loop(0, PAGE // 32)
    def _(i):
        rows = span(i, 32)
        v = tokens[rows, :].astype(F32) + hold[rows, :] + vec.baseline[...]
        v = v - mean(v)
        r = lax.rsqrt(mean(v * v) + EPSILON)
        v = v * r
        n1[rows, :] = v
        r1[rows, :] = jnp.broadcast_to(r, (32, 128))
        low[rows, :] = (v * vec.stretch[...] + vec.center[...]).astype(BF)


def feed(low, expander, uplift, activated, slope):
    @pl.loop(0, FF // PIECE)
    def _(n):
        cols = span(n, PIECE)

        v = nn(low[...], expander[:, cols]) + uplift[:, cols]
        half = 0.5 * lax.erf(v * (0.5 ** 0.5)) + 0.5
        activated[:, cols] = (v * half).astype(BF)
        slope[:, cols] = (half + v * (jnp.exp(v * v * -0.5) * 0.3989422804014327)).astype(BF)


def second_norm(n1, cotangent, activated, reducer, vec, hold, reduced_back, second_back, result, sums):
    @pl.loop(0, 3)
    def _(n):
        cols = span(n, PIECE)
        hold[:, cols] = nn(activated[...], reducer[:, cols])

    zero = jnp.zeros((8, D), F32)

    def fold(v):
        return jnp.sum(v.reshape(4, 8, D), axis=0)

    def body(i, carry):
        rescale_sum, recenter_sum, offset_sum = carry
        rows = span(i, 32)
        v = (n1[rows, :] * vec.stretch[...] + vec.center[...]) + hold[rows, :] + vec.offset[...]
        v = v - mean(v)
        r = lax.rsqrt(mean(v * v) + EPSILON)
        v = v * r
        result[rows, :] = (v * vec.rescale[...] + vec.recenter[...]).astype(BF)
        g = cotangent[rows, :].astype(F32)
        u = g * vec.rescale[...]
        back = r * (u - mean(u) - v * mean(u * v))
        second_back[rows, :] = back
        low = back.astype(BF)
        reduced_back[rows, :] = low
        return (rescale_sum + fold(g * v), recenter_sum + fold(g), offset_sum + fold(low.astype(F32)))

    a, b, c = lax.fori_loop(0, PAGE // 32, body, (zero, zero, zero))
    for k, v in ((SUM_RESCALE, a), (SUM_RECENTER, b), (SUM_OFFSET, c)):
        sums[k : k + 1, :] = jnp.sum(v, axis=0, keepdims=True)


SUM_BASELINE, SUM_STRETCH, SUM_CENTER, SUM_OFFSET, SUM_RESCALE, SUM_RECENTER = range(6)


def feed_back(low_t, activated, slope, reduced_back, reducer, expander, grad_reducer, grad_expander, uplift_sum, total):
    @pl.loop(0, FF // PIECE)
    def _(n):
        cols = span(n, PIECE)
        grad_reducer[cols, :] = nn(activated[:, cols].T, reduced_back[...]).astype(BF)
        inner = (nt(reduced_back[...], reducer[cols, :]) * slope[:, cols].astype(F32)).astype(BF)
        uplift_sum[:, cols] = jnp.sum(inner.astype(F32), axis=0, keepdims=True)
        grad_expander[:, cols] = nn(low_t[...], inner).astype(BF)
        total[...] += nt(inner, expander[:, cols])


def first_back(total, n1, r1, vec, branch_back, sums):
    zero = jnp.zeros((8, D), F32)

    def fold(v):
        return jnp.sum(v.reshape(4, 8, D), axis=0)

    def body(i, carry):
        stretch_sum, center_sum, baseline_sum = carry
        rows = span(i, 32)
        b = total[rows, :]
        v = n1[rows, :]
        u = b * vec.stretch[...]
        back = r1[rows, :1] * (u - mean(u) - v * mean(u * v))
        total[rows, :] = back
        low = back.astype(BF)
        branch_back[rows, :] = low
        return (stretch_sum + fold(b * v), center_sum + fold(b), baseline_sum + fold(low.astype(F32)))

    a, b, c = lax.fori_loop(0, PAGE // 32, body, (zero, zero, zero))
    for k, v in ((SUM_STRETCH, a), (SUM_CENTER, b), (SUM_BASELINE, c)):
        sums[k : k + 1, :] = jnp.sum(v, axis=0, keepdims=True)


def branch_grads(mixture, branch_back, combiner, grad_combiner, mixture_back):
    @pl.loop(0, 3)
    def _(n):
        cols = span(n, PIECE)
        grad_combiner[cols, :] = nn(mixture[:, cols].T, branch_back[...]).astype(BF)
        mixture_back[:, cols] = nt(branch_back[...], combiner[cols, :]).astype(BF)


def back_setup(feats, top, bottom):
    for k in range(6):
        block = feats[:, k * 128 : (k + 1) * 128].T
        top[k * 128 : (k + 1) * 128, :] = block
        bottom[k * 128 : (k + 1) * 128, :] = block


def unturn(g, t, cols, out):
    @pl.loop(0, HALF // 64)
    def _(i):
        a = span(i, 64)
        b = pl.ds(pl.multiple_of(HALF + i * 64, 64), 64)
        c = t[a, :].astype(F32)
        s = t[b, :].astype(F32)
        g1 = g[a, :]
        g2 = g[b, :]
        out[a, :] = (g1 * s - g2 * c).astype(BF)
        out[b, :] = (g1 * c + g2 * s).astype(BF)


def back_pair(p, qkv, mixture_back, probs_of, relative, top, bottom, score_back, lifted, turned, grad_relative, projected_back):
    lanes = span(p, 128)
    q2 = qkv[:, lanes]
    k2 = qkv[:, span(p + PAIRS, 128)]
    v2 = qkv[:, span(p + 2 * PAIRS, 128)]
    m2 = mixture_back[:, lanes]
    qt, kt, mt = q2.T, k2.T, m2.T
    tables = [[table(relative, side, half, lanes).T for half in (0, 1)] for side in (0, 1)]
    query_t = jnp.zeros((128, PAGE), F32)
    key_t = jnp.zeros((128, PAGE), F32)
    value_t = jnp.zeros((128, PAGE), F32)
    grad_q = jnp.zeros((D, 128), F32)
    grad_k = jnp.zeros((D, 128), F32)
    for e in (0, 1):
        probs = probs_of(e)
        me = only(e, m2)
        top[D:, :] = only_rows(e, kt)
        bottom[D:, :] = only_rows(e, qt)

        back = nt(me, v2)
        share = probs[...].astype(F32)
        score_back[...] = (share * (back - jnp.sum(share * back, axis=1, keepdims=True)) * SCALE).astype(BF)

        value_t += nn(only_rows(e, mt), probs[...])
        lifted[...] = nt(top[...], score_back[...])
        query_t += lifted[D:, :]
        unturn(lifted, top, None, turned)
        grad_q += nn(turned[...], only(e, q2))
        query_t += only_rows(e, nn(tables[0][0], turned[:HALF, :]) + nn(tables[0][1], turned[HALF:, :]))
        lifted[...] = nn(bottom[...], score_back[...])
        key_t += lifted[D:, :]
        unturn(lifted, top, None, turned)
        grad_k += nn(turned[...], only(e, k2))
        key_t += only_rows(e, nn(tables[1][0], turned[:HALF, :]) + nn(tables[1][1], turned[HALF:, :]))
    for side, g in ((0, grad_q), (1, grad_k)):
        for half in (0, 1):
            block = g[half * HALF : (half + 1) * HALF, :].astype(BF)
            grad_relative[2 * side : 2 * side + 2, half, :, :, :, lanes] = block.reshape(2, 2, 2, 48, 128)
    projected_back[:, lanes] = query_t.T.astype(BF)
    projected_back[:, span(p + PAIRS, 128)] = key_t.T.astype(BF)
    projected_back[:, span(p + 2 * PAIRS, 128)] = value_t.T.astype(BF)


def project_back(tokens, tokens_t, projected_back, projector, sum_back, grad_projector, intercept_sum, token_gradient):
    @pl.loop(0, 9)
    def _(n):
        cols = span(n, PIECE)
        b = projected_back[:, cols]
        intercept_sum[:, cols] = jnp.sum(b.astype(F32), axis=0, keepdims=True)
        grad_projector[:, cols] = nn(tokens_t[...], b).astype(BF)

    @pl.loop(0, 3)
    def _(n):
        cols = span(n, PIECE)
        token_gradient[:, cols] = (sum_back[:, cols] + nt(projected_back[...], projector[cols, :])).astype(BF)


VM = pl.BlockSpec(memory_space=pltpu.VMEM)
HB = pl.BlockSpec(memory_space=pl.ANY)
SM = pl.BlockSpec(memory_space=pltpu.SMEM)
BIG = 63 << 20
W_SHAPES = {"projector": (24, 2304), "relative": (48, 768), "combiner": (24, 768), "expander": (24, 3072), "reducer": (96, 768)}
VECTORS = ("intercept", "uplift", "baseline", "stretch", "center", "offset", "rescale", "recenter")


def flat(ref):
    return ref.reshape(32 * ref.shape[4], ref.shape[5])


def name_refs(groups, refs):
    out = []
    at = 0
    for g in groups:
        out.append(types.SimpleNamespace(**dict(zip(g, refs[at : at + len(g)]))))
        at += len(g)
    return out


def front_kernel(names, *refs):
    i, o, s = name_refs(names, refs)
    order = ("projector", "relative", "combiner", "expander", "reducer")
    loads = {}
    for k, w in enumerate(order):
        dst = flat(getattr(s, "w_" + w))
        loads[w] = pltpu.make_async_copy(getattr(i, w), dst, s.load.at[k])
        loads[w].start()
    live = i.lengths[0]
    vec = i
    attend_setup(i.feats, s.left, s.right)
    loads["projector"].wait()
    project(i.tokens, flat(s.w_projector), i.intercept, o.qkv)
    loads["relative"].wait()

    def probs_out(h):
        return pltpu.make_async_copy(s.probs.at[h], o.probs.at[h], s.save.at[h])

    @pl.loop(0, PAIRS)
    def _(p):
        attend_pair(p, o.qkv, s.w_relative, i.feats, live, s.left, s.right, s.probs, s.mixture)
        probs_out(2 * p).start()
        probs_out(2 * p + 1).start()

    loads["combiner"].wait()
    first_norm(i.tokens, s.mixture, flat(s.w_combiner), vec, s.hold, s.n1, s.r1, s.low)
    loads["expander"].wait()
    feed(s.low, flat(s.w_expander), i.uplift, s.activated, s.slope)
    loads["reducer"].wait()
    second_norm(s.n1, i.cotangent, s.activated, flat(s.w_reducer), vec, s.hold, s.reduced_back, o.sum_back, o.result, o.sums)
    for k in range(6):
        s.low_t[k * 128 : (k + 1) * 128, :] = s.low[:, k * 128 : (k + 1) * 128].T
    feed_back(s.low_t, s.activated, s.slope, s.reduced_back, flat(s.w_reducer), flat(s.w_expander), s.g_reducer, s.g_expander, o.uplift_sum, o.sum_back)
    stores = [pltpu.make_async_copy(s.g_reducer, o.g_reducer, s.load.at[0]), pltpu.make_async_copy(s.g_expander, o.g_expander, s.load.at[1])]
    for st in stores:
        st.start()
    first_back(o.sum_back, s.n1, s.r1, vec, s.reduced_back, o.sums)
    branch_grads(s.mixture, s.reduced_back, flat(s.w_combiner), s.g_combiner, o.mixture_back)
    stores.append(pltpu.make_async_copy(s.g_combiner, o.g_combiner, s.load.at[2]))
    stores[-1].start()
    for st in stores:
        st.wait()
    for h in range(12):
        probs_out(h).wait()


def call(kernel, ins, outs, scratch, name, **params):
    names = (tuple(ins), tuple(outs), tuple(scratch))
    got = pl.pallas_call(
        functools.partial(kernel, names),
        out_shape=[jax.ShapeDtypeStruct(s, d) for s, d, _ in outs.values()],
        in_specs=[sp for _, sp in ins.values()],
        out_specs=[sp for _, _, sp in outs.values()],
        scratch_shapes=list(scratch.values()),
        compiler_params=pltpu.CompilerParams(vmem_limit_bytes=BIG, **params),
        name=name,
    )(*[a for a, _ in ins.values()])
    return types.SimpleNamespace(**dict(zip(outs, got)))


def buf(*shape, dtype=BF):
    return pltpu.VMEM(shape, dtype)


def weight_bufs(names):
    return {"w_" + n: buf(4, 2, 2, 2, *W_SHAPES[n]) for n in names}


def front(tokens, feats, lengths, cotangent, weights, vectors):
    ins = {"tokens": (tokens, VM), "feats": (feats, VM), "lengths": (lengths, SM), "cotangent": (cotangent, VM)}
    ins.update({k: (v, HB) for k, v in weights.items()})
    ins.update({k: (v, VM) for k, v in vectors.items()})
    outs = {
        "result": ((PAGE, D), BF, VM),
        "qkv": ((PAGE, 3 * D), BF, VM),
        "probs": ((12, PAGE, PAGE), BF, HB),
        "mixture_back": ((PAGE, D), BF, VM),
        "sum_back": ((PAGE, D), F32, VM),
        "sums": ((8, D), F32, VM),
        "uplift_sum": ((1, FF), F32, VM),
        "g_combiner": ((D, D), BF, HB),
        "g_expander": ((D, FF), BF, HB),
        "g_reducer": ((FF, D), BF, HB),
    }
    scratch = weight_bufs(W_SHAPES)
    scratch.update(
        left=buf(PAGE, 1664), right=buf(PAGE, 1664), probs=buf(12, PAGE, PAGE), mixture=buf(PAGE, D),
        hold=buf(PAGE, D, dtype=F32), n1=buf(PAGE, D, dtype=F32), r1=buf(PAGE, 128, dtype=F32), low=buf(PAGE, D), low_t=buf(D, PAGE),
        activated=buf(PAGE, FF), slope=buf(PAGE, FF), reduced_back=buf(PAGE, D),
        g_reducer=buf(FF, D), g_expander=buf(D, FF), g_combiner=buf(D, D),
        load=pltpu.SemaphoreType.DMA((5,)), save=pltpu.SemaphoreType.DMA((12,)),
    )
    return call(front_kernel, ins, outs, scratch, "front")


def rear_kernel(names, *refs):
    i, o, s = name_refs(names, refs)
    loads = {}
    for k, w in enumerate(("relative", "projector")):
        loads[w] = pltpu.make_async_copy(getattr(i, w), flat(getattr(s, "w_" + w)), s.load.at[k])
        loads[w].start()

    def fetch(p, slot):
        return pltpu.make_async_copy(i.probs.at[pl.ds(2 * p, 2)], s.probs.at[slot], s.fetch.at[slot])

    fetch(0, 0).start()
    back_setup(i.feats, s.top, s.bottom)
    for k in range(6):
        s.tokens_t[k * 128 : (k + 1) * 128, :] = i.tokens[:, k * 128 : (k + 1) * 128].T
    loads["relative"].wait()

    @pl.loop(0, PAIRS)
    def _(p):
        slot = p % 2

        @pl.when(p + 1 < PAIRS)
        def _():
            fetch(p + 1, 1 - slot).start()

        fetch(p, slot).wait()
        back_pair(
            p, i.qkv, i.mixture_back, lambda e: s.probs.at[slot, e], s.w_relative, s.top, s.bottom, s.score_back, s.lifted, s.turned,
            s.g_relative, s.projected_back,
        )

    loads["projector"].wait()
    store = pltpu.make_async_copy(flat(s.g_relative), o.g_relative, s.load.at[0])
    store.start()
    project_back(i.tokens, s.tokens_t, s.projected_back, flat(s.w_projector), i.sum_back, s.g_projector, o.intercept_sum, o.token_gradient)
    last = pltpu.make_async_copy(s.g_projector, o.g_projector, s.load.at[1])
    last.start()
    last.wait()
    store.wait()


def rear(tokens, feats, kept, weights):
    ins = {"tokens": (tokens, VM), "feats": (feats, VM)}
    ins.update({k: (getattr(kept, k), VM) for k in ("qkv", "mixture_back", "sum_back")})
    ins["probs"] = (kept.probs, HB)
    ins.update({k: (weights[k], HB) for k in ("relative", "projector")})
    outs = {
        "token_gradient": ((PAGE, D), BF, VM),
        "intercept_sum": ((1, 3 * D), F32, VM),
        "g_relative": ((2 * D, D), BF, HB),
        "g_projector": ((D, 3 * D), BF, HB),
    }
    scratch = weight_bufs(("relative", "projector"))
    scratch.update(
        probs=buf(2, 2, PAGE, PAGE), top=buf(D + 128, PAGE), bottom=buf(D + 128, PAGE), score_back=buf(PAGE, PAGE),
        lifted=buf(D + 128, PAGE, dtype=F32), turned=buf(D, PAGE), tokens_t=buf(D, PAGE), projected_back=buf(PAGE, 3 * D),
        g_relative=buf(4, 2, 2, 2, 48, D), g_projector=buf(D, 3 * D),
        load=pltpu.SemaphoreType.DMA((2,)), fetch=pltpu.SemaphoreType.DMA((2,)),
    )
    return call(rear_kernel, ins, outs, scratch, "rear")


def make_feats(coordinates):
    step = jnp.arange(192, dtype=F32)
    frequency = jnp.exp(-jnp.log(10000.0) * step / 192)
    angles = coordinates.astype(F32)[:, :, None] * frequency
    return jnp.concatenate([jnp.cos(angles[0]), jnp.cos(angles[1]), jnp.sin(angles[0]), jnp.sin(angles[1])], axis=1).astype(BF)


LANES = 384
NAMES = ("projector", "relative", "combiner", "expander", "reducer")
BACKWARD = ("reducer", "expander", "combiner", "relative", "projector")


def whole_gather(v):
    return lax.all_gather(v, ("dp", "fsdp"), axis=0, tiled=True)


def whole_scatter(v):
    v = lax.psum_scatter(v.astype(F32), "dp", scatter_dimension=0, tiled=True)
    return lax.psum_scatter(v.astype(BF), "fsdp", scatter_dimension=0, tiled=True).astype(F32)


def cut(rows, sizes):
    parts = []
    at = 0
    for size in sizes:
        parts.append(rows[..., at : at + size])
        at += size
    return parts


def local(
    tokens, coordinates, lengths, cotangent, projector, intercept, relative, combiner, baseline,
    stretch, center, expander, uplift, reducer, offset, rescale, recenter, remote,
):
    vectors = (intercept, uplift, baseline, stretch, center, offset, rescale, recenter)
    matrices = (projector, relative, combiner, expander, reducer)
    sizes = [v.shape[0] for v in vectors]
    packed = jnp.concatenate(vectors)
    if remote:
        packed = jnp.pad(packed[None], ((0, 7), (0, LANES - packed.shape[0])))
        *full, rows = gather_all(list(matrices) + [packed], 0)
        rows = rows.reshape(32, 8, LANES)[:, 0]
    else:
        full = [whole_gather(m) for m in matrices]
        rows = whole_gather(packed[None])
    weights = dict(zip(NAMES, full))
    shared = {k: v.reshape(1, -1).astype(F32) for k, v in zip(VECTORS, cut(rows, sizes))}
    feats = make_feats(coordinates)
    f = front(tokens, feats, lengths, cotangent, weights, shared)
    r = rear(tokens, feats, f, weights)
    sums = [r.intercept_sum[0], f.uplift_sum[0]] + [f.sums[k] for k in range(6)]
    changes = (f.g_reducer, f.g_expander, f.g_combiner, r.g_relative, r.g_projector)
    count = D // 24 if remote else lax.axis_size(("dp", "fsdp"))
    stacked = jnp.concatenate([v.reshape(count, -1) for v in sums], axis=1)
    if remote:
        stacked = jnp.pad(stacked.astype(BF)[:, None], ((0, 0), (0, 7), (0, LANES - stacked.shape[1])))
        *shares, row = scatter_all(list(changes) + [stacked.reshape(-1, LANES)], 1)
        row = row[0]
    else:
        shares = [whole_scatter(c) for c in changes]
        row = whole_scatter(stacked)[0]
    share = dict(zip(BACKWARD, shares))
    small = dict(zip(VECTORS, cut(row, sizes)))
    return (
        f.result, r.token_gradient, share["projector"], small["intercept"], share["relative"], share["combiner"], small["baseline"],
        small["stretch"], small["center"], share["expander"], small["uplift"], share["reducer"], small["offset"], small["rescale"],
        small["recenter"],
    )


def solution(mesh):
    rows, line = P(("dp", "fsdp"), None), P(("dp", "fsdp"))
    remote = (mesh.shape["dp"], mesh.shape["fsdp"]) == (NZ * NY, NX * NC)
    return jax.shard_map(
        functools.partial(local, remote=remote),
        mesh=mesh,
        in_specs=(rows, P(None, ("dp", "fsdp")), line, rows, rows, line, rows, rows, line, line, line, rows, line, rows, line, line, line),
        out_specs=(rows, rows, rows, line, rows, rows, line, line, line, rows, line, rows, line, line, line),
        check_vma=False,
    )
```

```python
import functools
import types

import jax
import jax.numpy as jnp
import numpy as np
from jax import lax
from jax.experimental import pallas as pl
from jax.experimental.pallas import tpu as pltpu
from jax.sharding import PartitionSpec as P

MESH = pl.DeviceIdType.MESH
NZ, NY, NX, NC = 4, 2, 2, 2


class Place:
    def __init__(self):
        d = lax.axis_index("dp")
        f = lax.axis_index("fsdp")
        self.z, self.y = d // NY, d % NY
        self.x, self.c = f // NC, f % NC
        z, y, x, c = self.z, self.y, self.x, self.c
        self.y1, self.x1 = y + (1 - c) * (1 - 2 * y), x + c * (1 - 2 * x)
        self.y2, self.x2 = y + c * (1 - 2 * y), x + (1 - c) * (1 - 2 * x)
        self.yd, self.xd = 1 - y, 1 - x
        self.first = (z * NY + self.y1, self.x1 * NC + c)
        self.second = (z * NY + self.y2, self.x2 * NC + c)
        self.sibling = (z * NY + y, x * NC + 1 - c)

    def along_z(self, z):
        return (z * NY + self.y, self.x * NC + self.c)

    def peers(self):
        return [self.first, self.second, self.sibling] + [self.along_z((self.z + s) % NZ) for s in (1, 2, 3)]


def enter(place):
    barrier = pltpu.get_barrier_semaphore()
    peers = place.peers()
    for peer in peers:
        pl.semaphore_signal(barrier, inc=1, device_id=peer, device_id_type=MESH)
    pl.semaphore_wait(barrier, len(peers))


def gather_kernel(n, *refs):
    shards, full = refs[:n], refs[n : 2 * n]
    local, send, recv = refs[2 * n :]
    p = Place()
    z, y, x, c = p.z, p.y, p.x, p.c
    enter(p)

    def remote(w, src, dst, s, r, device):
        return pltpu.make_async_remote_copy(
            src_ref=src, dst_ref=dst, send_sem=send.at[w, s], recv_sem=recv.at[w, r], device_id=device, device_id_type=MESH
        )

    def block(w, by, bx, bc):
        return full[w].at[:, by, bx, bc]

    started = []

    def go(copy):
        copy.start()
        started.append(copy)

    own = []
    for w in range(n):
        cp = pltpu.make_async_copy(shards[w], full[w].at[z, y, x, c], local.at[w])
        cp.start()
        own.append(cp)
        for s in (1, 2, 3):
            go(remote(w, shards[w], full[w].at[z, y, x, c], s - 1, z, p.along_z((z + s) % NZ)))

    def arrived(w, ref, r):
        remote(w, ref, ref, 0, r, p.sibling).wait_recv()

    def stage_a(w):
        own[w].wait()
        for s in (1, 2, 3):
            zs = (z + s) % NZ
            arrived(w, full[w].at[zs, y, x, c], zs)
        a = block(w, y, x, c)
        go(remote(w, a, a, 3, 4, p.first))
        go(remote(w, a, a, 4, 5, p.second))
        go(remote(w, a, a, 5, 7, p.sibling))

    def stage_b(w):
        b = block(w, p.y1, p.x1, c)
        arrived(w, b, 4)
        go(remote(w, b, b, 6, 6, p.second))
        go(remote(w, b, b, 7, 8, p.sibling))

    def stage_c(w):
        b = block(w, p.y2, p.x2, c)
        arrived(w, b, 5)
        go(remote(w, b, b, 8, 9, p.sibling))
        b = block(w, 1 - y, 1 - x, c)
        arrived(w, b, 6)
        go(remote(w, b, b, 9, 10, p.sibling))

    def stage_d(w):
        for r in range(7, 11):
            arrived(w, block(w, y, x, 1 - c), r)

    for step in range(n + 3):
        if step < n:
            stage_a(step)
        if 0 <= step - 1 < n:
            stage_b(step - 1)
        if 0 <= step - 2 < n:
            stage_c(step - 2)
        if 0 <= step - 3 < n:
            stage_d(step - 3)
    for copy in started:
        copy.wait_send()


def gather_all(shards, cid):
    n = len(shards)
    outs = [jax.ShapeDtypeStruct((NZ, NY, NX, NC) + s.shape, s.dtype) for s in shards]
    full = pl.pallas_call(
        functools.partial(gather_kernel, n),
        out_shape=outs,
        in_specs=[pl.BlockSpec(memory_space=pl.ANY)] * n,
        out_specs=[pl.BlockSpec(memory_space=pl.ANY)] * n,
        scratch_shapes=[
            pltpu.SemaphoreType.DMA((n,)),
            pltpu.SemaphoreType.DMA((n, 10)),
            pltpu.SemaphoreType.DMA((n, 11)),
        ],
        compiler_params=pltpu.CompilerParams(collective_id=cid, has_side_effects=True),
        name="gather_all",
    )(*shards)
    return [f.reshape((32 * s.shape[0],) + s.shape[1:]) for f, s in zip(full, shards)]


def add_into(dst, a, b, rows, cols):
    dst[...] = (a[...].astype(jnp.float32) + b[...].astype(jnp.float32)).astype(dst.dtype)


def scatter_kernel(n, *refs):
    grads, outs = refs[:n], refs[n : 2 * n]
    held = refs[2 * n : 3 * n]
    second = refs[3 * n : 4 * n]
    firsts = refs[4 * n : 5 * n]
    alongs = refs[5 * n : 6 * n]
    send, recv = refs[6 * n :]
    p = Place()
    z, y, x, c = p.z, p.y, p.x, p.c
    enter(p)
    started = []

    def remote(w, src, dst, s, r, device):
        return pltpu.make_async_remote_copy(
            src_ref=src, dst_ref=dst, send_sem=send.at[w, s], recv_sem=recv.at[w, r], device_id=device, device_id_type=MESH
        )

    def go(copy):
        copy.start()
        started.append(copy)

    def arrived(w, ref, r):
        remote(w, ref, ref, 0, r, p.sibling).wait_recv()

    for w in range(n):
        go(remote(w, grads[w].at[:, :, :, 1 - c], held[w], 0, 0, p.sibling))

    def accumulate(w, by, bx, extra):
        @pl.loop(0, NZ)
        def _(k):
            held[w][k, by, bx] = (held[w][k, by, bx].astype(jnp.float32) + extra(k).astype(jnp.float32)).astype(jnp.bfloat16)

    def stage_s(w):
        arrived(w, held[w], 0)
        for by, bx in ((1 - y, 1 - x), (p.y2, p.x2), (p.y1, p.x1), (y, x)):
            accumulate(w, by, bx, lambda k: grads[w][k, by, bx, c])
            if by is not p.y1 and by is not y:
                pass
        go(remote(w, held[w].at[:, 1 - y, 1 - x], second[w].at[0], 1, 1, p.second))
        go(remote(w, held[w].at[:, p.y2, p.x2], second[w].at[1], 2, 2, p.second))

    def stage_x(w):
        arrived(w, second[w].at[0], 1)
        accumulate(w, p.y1, p.x1, lambda k: second[w][0, k])
        go(remote(w, held[w].at[:, p.y1, p.x1], firsts[w], 3, 3, p.first))
        arrived(w, second[w].at[1], 2)
        accumulate(w, y, x, lambda k: second[w][1, k])

    def stage_f(w):
        arrived(w, firsts[w], 3)
        accumulate(w, y, x, lambda k: firsts[w][k])
        for s in (1, 2, 3):
            zt = (z + s) % NZ
            go(remote(w, held[w].at[zt, y, x], alongs[w].at[z], 3 + s, 4 + z, p.along_z(zt)))

    def stage_z(w):
        total = held[w][z, y, x].astype(jnp.float32)
        for s in (1, 2, 3):
            zs = (z + s) % NZ
            arrived(w, alongs[w].at[zs], 4 + zs)
            total += alongs[w][zs].astype(jnp.float32)
        outs[w][...] = total

    for step in range(n + 3):
        if step < n:
            stage_s(step)
        if 0 <= step - 1 < n:
            stage_x(step - 1)
        if 0 <= step - 2 < n:
            stage_f(step - 2)
        if 0 <= step - 3 < n:
            stage_z(step - 3)
    for copy in started:
        copy.wait_send()


def scatter_all(grads, cid):
    n = len(grads)
    shards = [(g.shape[0] // 32, g.shape[1]) for g in grads]
    views = [g.reshape((NZ, NY, NX, NC) + s) for g, s in zip(grads, shards)]
    vm = pl.BlockSpec(memory_space=pltpu.VMEM)
    return pl.pallas_call(
        functools.partial(scatter_kernel, n),
        out_shape=[jax.ShapeDtypeStruct(s, jnp.float32) for s in shards],
        in_specs=[vm] * n,
        out_specs=[vm] * n,
        scratch_shapes=[pltpu.VMEM((NZ, NY, NX) + s, jnp.bfloat16) for s in shards]
        + [pltpu.VMEM((2, NZ) + s, jnp.bfloat16) for s in shards]
        + [pltpu.VMEM((NZ,) + s, jnp.bfloat16) for s in shards]
        + [pltpu.VMEM((NZ,) + s, jnp.bfloat16) for s in shards]
        + [pltpu.SemaphoreType.DMA((n, 7)), pltpu.SemaphoreType.DMA((n, 8))],
        compiler_params=pltpu.CompilerParams(collective_id=cid, has_side_effects=True, vmem_limit_bytes=60 << 20),
        name="scatter_all",
    )(*views)


PAGE = 512
D = 768
FF = 3072
HALF = 384
PAIRS = 6
SCALE = 192.0 ** -0.5
EPSILON = 1e-12
NEGATIVE = -1e30
BF = jnp.bfloat16
F32 = jnp.float32
ROWS = 128
PIECE = 256


def nn(a, b):
    return jnp.dot(a, b, preferred_element_type=F32)


def nt(a, b):
    return lax.dot_general(a, b, (((1,), (1,)), ((), ())), preferred_element_type=F32)


def span(i, size):
    return pl.ds(pl.multiple_of(i * size, size), size)


def own_lanes(e, rows):
    lane = lax.broadcasted_iota(jnp.int32, (rows, 128), 1)
    return lane < 64 if e == 0 else lane >= 64


def only(e, v):
    return jnp.where(own_lanes(e, v.shape[0]), v, jnp.zeros_like(v))


def only_rows(e, v):
    row = lax.broadcasted_iota(jnp.int32, v.shape, 0)
    return jnp.where(row < 64 if e == 0 else row >= 64, v, jnp.zeros_like(v))


def project(tokens, projector, intercept, qkv):
    @pl.loop(0, 9)
    def _(n):
        cols = span(n, PIECE)
        qkv[:, cols] = (nn(tokens[...], projector[:, cols]) + intercept[:, cols]).astype(BF)


def table(relative, side, half, cols):
    return relative[2 * side : 2 * side + 2, half * 192 : (half + 1) * 192, cols].reshape(HALF, 128)


def turn(weights_of, feats, out, at, rows):
    ws, wc = weights_of
    c = feats[rows, :HALF].astype(F32)
    s = feats[rows, HALF:].astype(F32)
    out[rows, at : at + HALF] = (ws * s + wc * c).astype(BF)
    out[rows, at + HALF : at + 2 * HALF] = (wc * s - ws * c).astype(BF)


def attend_setup(feats, left, right):
    left[:, D + 128 :] = feats[...]
    right[:, :D] = feats[...]


def attend_pair(p, qkv, relative, feats, live, left, right, probs, mixture):
    lanes = span(p, 128)
    q2 = qkv[:, lanes]
    k2 = qkv[:, span(p + PAIRS, 128)]
    v2 = qkv[:, span(p + 2 * PAIRS, 128)]
    for e in (0, 1):
        left[:, D : D + 128] = only(e, q2)
        right[:, D : D + 128] = only(e, k2)

        every = slice(None)
        q = left[:, D : D + 128]
        k = right[:, D : D + 128]
        turn((nt(q, table(relative, 0, 0, lanes)), nt(q, table(relative, 0, 1, lanes))), feats, left, 0, every)
        turn((nt(k, table(relative, 1, 0, lanes)), nt(k, table(relative, 1, 1, lanes))), feats, right, D + 128, every)
        scores = nt(left[...], right[...]) * SCALE
        key = lax.broadcasted_iota(jnp.int32, scores.shape, 1)
        scores = jnp.where(key < live, scores, NEGATIVE)
        powers = jnp.exp(scores - jnp.max(scores, axis=1, keepdims=True))
        share = (powers / jnp.sum(powers, axis=1, keepdims=True)).astype(BF)
        probs[2 * p + e] = share
        part = nn(share, only(e, v2))
        if e == 0:
            mixture[:, lanes] = part.astype(BF)
        else:
            mixture[:, lanes] = jnp.where(own_lanes(1, PAGE), part.astype(BF), mixture[:, lanes])


def mean(v):
    return jnp.sum(v, axis=1, keepdims=True) * (1.0 / D)


def first_norm(tokens, mixture, combiner, vec, hold, n1, r1, low):
    @pl.loop(0, 3)
    def _(n):
        cols = span(n, PIECE)
        hold[:, cols] = nn(mixture[...], combiner[:, cols])

    @pl.loop(0, PAGE // 32)
    def _(i):
        rows = span(i, 32)
        v = tokens[rows, :].astype(F32) + hold[rows, :] + vec.baseline[...]
        v = v - mean(v)
        r = lax.rsqrt(mean(v * v) + EPSILON)
        v = v * r
        n1[rows, :] = v
        r1[rows, :] = jnp.broadcast_to(r, (32, 128))
        low[rows, :] = (v * vec.stretch[...] + vec.center[...]).astype(BF)


def feed(low, expander, uplift, activated, slope):
    @pl.loop(0, FF // PIECE)
    def _(n):
        cols = span(n, PIECE)

        v = nn(low[...], expander[:, cols]) + uplift[:, cols]
        half = 0.5 * lax.erf(v * (0.5 ** 0.5)) + 0.5
        activated[:, cols] = (v * half).astype(BF)
        slope[:, cols] = (half + v * (jnp.exp(v * v * -0.5) * 0.3989422804014327)).astype(BF)


def second_norm(n1, cotangent, activated, reducer, vec, hold, reduced_back, second_back, result, sums):
    @pl.loop(0, 3)
    def _(n):
        cols = span(n, PIECE)
        hold[:, cols] = nn(activated[...], reducer[:, cols])

    zero = jnp.zeros((8, D), F32)

    def fold(v):
        return jnp.sum(v.reshape(4, 8, D), axis=0)

    def body(i, carry):
        rescale_sum, recenter_sum, offset_sum = carry
        rows = span(i, 32)
        v = (n1[rows, :] * vec.stretch[...] + vec.center[...]) + hold[rows, :] + vec.offset[...]
        v = v - mean(v)
        r = lax.rsqrt(mean(v * v) + EPSILON)
        v = v * r
        result[rows, :] = (v * vec.rescale[...] + vec.recenter[...]).astype(BF)
        g = cotangent[rows, :].astype(F32)
        u = g * vec.rescale[...]
        back = r * (u - mean(u) - v * mean(u * v))
        second_back[rows, :] = back
        low = back.astype(BF)
        reduced_back[rows, :] = low
        return (rescale_sum + fold(g * v), recenter_sum + fold(g), offset_sum + fold(low.astype(F32)))

    a, b, c = lax.fori_loop(0, PAGE // 32, body, (zero, zero, zero))
    for k, v in ((SUM_RESCALE, a), (SUM_RECENTER, b), (SUM_OFFSET, c)):
        sums[k : k + 1, :] = jnp.sum(v, axis=0, keepdims=True)


SUM_BASELINE, SUM_STRETCH, SUM_CENTER, SUM_OFFSET, SUM_RESCALE, SUM_RECENTER = range(6)


def feed_back(low_t, activated, slope, reduced_back, reducer, expander, grad_reducer, grad_expander, uplift_sum, total):
    @pl.loop(0, FF // PIECE)
    def _(n):
        cols = span(n, PIECE)
        grad_reducer[cols, :] = nn(activated[:, cols].T, reduced_back[...]).astype(BF)
        inner = (nt(reduced_back[...], reducer[cols, :]) * slope[:, cols].astype(F32)).astype(BF)
        uplift_sum[:, cols] = jnp.sum(inner.astype(F32), axis=0, keepdims=True)
        grad_expander[:, cols] = nn(low_t[...], inner).astype(BF)
        total[...] += nt(inner, expander[:, cols])


def first_back(total, n1, r1, vec, branch_back, sums):
    zero = jnp.zeros((8, D), F32)

    def fold(v):
        return jnp.sum(v.reshape(4, 8, D), axis=0)

    def body(i, carry):
        stretch_sum, center_sum, baseline_sum = carry
        rows = span(i, 32)
        b = total[rows, :]
        v = n1[rows, :]
        u = b * vec.stretch[...]
        back = r1[rows, :1] * (u - mean(u) - v * mean(u * v))
        total[rows, :] = back
        low = back.astype(BF)
        branch_back[rows, :] = low
        return (stretch_sum + fold(b * v), center_sum + fold(b), baseline_sum + fold(low.astype(F32)))

    a, b, c = lax.fori_loop(0, PAGE // 32, body, (zero, zero, zero))
    for k, v in ((SUM_STRETCH, a), (SUM_CENTER, b), (SUM_BASELINE, c)):
        sums[k : k + 1, :] = jnp.sum(v, axis=0, keepdims=True)


def branch_grads(mixture, branch_back, combiner, grad_combiner, mixture_back):
    @pl.loop(0, 3)
    def _(n):
        cols = span(n, PIECE)
        grad_combiner[cols, :] = nn(mixture[:, cols].T, branch_back[...]).astype(BF)
        mixture_back[:, cols] = nt(branch_back[...], combiner[cols, :]).astype(BF)


def back_setup(feats, top, bottom):
    for k in range(6):
        block = feats[:, k * 128 : (k + 1) * 128].T
        top[k * 128 : (k + 1) * 128, :] = block
        bottom[k * 128 : (k + 1) * 128, :] = block


def unturn(g, t, cols, out):
    @pl.loop(0, HALF // 64)
    def _(i):
        a = span(i, 64)
        b = pl.ds(pl.multiple_of(HALF + i * 64, 64), 64)
        c = t[a, :].astype(F32)
        s = t[b, :].astype(F32)
        g1 = g[a, :]
        g2 = g[b, :]
        out[a, :] = (g1 * s - g2 * c).astype(BF)
        out[b, :] = (g1 * c + g2 * s).astype(BF)


def back_pair(p, qkv, mixture_back, probs_of, relative, top, bottom, score_back, lifted, turned, grad_relative, projected_back):
    lanes = span(p, 128)
    q2 = qkv[:, lanes]
    k2 = qkv[:, span(p + PAIRS, 128)]
    v2 = qkv[:, span(p + 2 * PAIRS, 128)]
    m2 = mixture_back[:, lanes]
    qt, kt, mt = q2.T, k2.T, m2.T
    tables = [[table(relative, side, half, lanes).T for half in (0, 1)] for side in (0, 1)]
    query_t = jnp.zeros((128, PAGE), F32)
    key_t = jnp.zeros((128, PAGE), F32)
    value_t = jnp.zeros((128, PAGE), F32)
    grad_q = jnp.zeros((D, 128), F32)
    grad_k = jnp.zeros((D, 128), F32)
    for e in (0, 1):
        probs = probs_of(e)
        me = only(e, m2)
        top[D:, :] = only_rows(e, kt)
        bottom[D:, :] = only_rows(e, qt)

        back = nt(me, v2)
        share = probs[...].astype(F32)
        score_back[...] = (share * (back - jnp.sum(share * back, axis=1, keepdims=True)) * SCALE).astype(BF)

        value_t += nn(only_rows(e, mt), probs[...])
        lifted[...] = nt(top[...], score_back[...])
        query_t += lifted[D:, :]
        unturn(lifted, top, None, turned)
        grad_q += nn(turned[...], only(e, q2))
        query_t += only_rows(e, nn(tables[0][0], turned[:HALF, :]) + nn(tables[0][1], turned[HALF:, :]))
        lifted[...] = nn(bottom[...], score_back[...])
        key_t += lifted[D:, :]
        unturn(lifted, top, None, turned)
        grad_k += nn(turned[...], only(e, k2))
        key_t += only_rows(e, nn(tables[1][0], turned[:HALF, :]) + nn(tables[1][1], turned[HALF:, :]))
    for side, g in ((0, grad_q), (1, grad_k)):
        for half in (0, 1):
            block = g[half * HALF : (half + 1) * HALF, :].astype(BF)
            grad_relative[2 * side : 2 * side + 2, half * 192 : (half + 1) * 192, lanes] = block.reshape(2, 192, 128)
    projected_back[:, lanes] = query_t.T.astype(BF)
    projected_back[:, span(p + PAIRS, 128)] = key_t.T.astype(BF)
    projected_back[:, span(p + 2 * PAIRS, 128)] = value_t.T.astype(BF)


def project_back(tokens, tokens_t, projected_back, projector, sum_back, grad_projector, intercept_sum, token_gradient):
    @pl.loop(0, 9)
    def _(n):
        cols = span(n, PIECE)
        b = projected_back[:, cols]
        intercept_sum[:, cols] = jnp.sum(b.astype(F32), axis=0, keepdims=True)
        grad_projector[:, cols] = nn(tokens_t[...], b).astype(BF)

    @pl.loop(0, 3)
    def _(n):
        cols = span(n, PIECE)
        token_gradient[:, cols] = (sum_back[:, cols] + nt(projected_back[...], projector[cols, :])).astype(BF)


VM = pl.BlockSpec(memory_space=pltpu.VMEM)
HB = pl.BlockSpec(memory_space=pl.ANY)
SM = pl.BlockSpec(memory_space=pltpu.SMEM)
BIG = 63 << 20
W_SHAPES = {"projector": (24, 2304), "relative": (48, 768), "combiner": (24, 768), "expander": (24, 3072), "reducer": (96, 768)}
VECTORS = ("intercept", "uplift", "baseline", "stretch", "center", "offset", "rescale", "recenter")


def flat(ref):
    return ref.reshape(ref.shape[0] * ref.shape[1], ref.shape[2])


def name_refs(groups, refs):
    out = []
    at = 0
    for g in groups:
        out.append(types.SimpleNamespace(**dict(zip(g, refs[at : at + len(g)]))))
        at += len(g)
    return out


def front_kernel(names, *refs):
    i, o, s = name_refs(names, refs)
    order = ("projector", "relative", "combiner", "expander", "reducer")
    loads = {}
    for k, w in enumerate(order):
        dst = flat(getattr(s, "w_" + w))
        loads[w] = pltpu.make_async_copy(getattr(i, w), dst, s.load.at[k])
        loads[w].start()
    live = i.lengths[0]
    vec = i
    attend_setup(i.feats, s.left, s.right)
    loads["projector"].wait()
    project(i.tokens, flat(s.w_projector), i.intercept, o.qkv)
    loads["relative"].wait()

    def probs_out(h):
        return pltpu.make_async_copy(s.probs.at[h], o.probs.at[h], s.save.at[h])

    @pl.loop(0, PAIRS)
    def _(p):
        attend_pair(p, o.qkv, s.w_relative, i.feats, live, s.left, s.right, s.probs, s.mixture)
        probs_out(2 * p).start()
        probs_out(2 * p + 1).start()

    loads["combiner"].wait()
    first_norm(i.tokens, s.mixture, flat(s.w_combiner), vec, s.hold, s.n1, s.r1, s.low)
    loads["expander"].wait()
    feed(s.low, flat(s.w_expander), i.uplift, s.activated, s.slope)
    loads["reducer"].wait()
    second_norm(s.n1, i.cotangent, s.activated, flat(s.w_reducer), vec, s.hold, s.reduced_back, o.sum_back, o.result, o.sums)
    for k in range(6):
        s.low_t[k * 128 : (k + 1) * 128, :] = s.low[:, k * 128 : (k + 1) * 128].T
    feed_back(s.low_t, s.activated, s.slope, s.reduced_back, flat(s.w_reducer), flat(s.w_expander), s.g_reducer, s.g_expander, o.uplift_sum, o.sum_back)
    stores = [pltpu.make_async_copy(s.g_reducer, o.g_reducer, s.load.at[0]), pltpu.make_async_copy(s.g_expander, o.g_expander, s.load.at[1])]
    for st in stores:
        st.start()
    first_back(o.sum_back, s.n1, s.r1, vec, s.reduced_back, o.sums)
    branch_grads(s.mixture, s.reduced_back, flat(s.w_combiner), s.g_combiner, o.mixture_back)
    stores.append(pltpu.make_async_copy(s.g_combiner, o.g_combiner, s.load.at[2]))
    stores[-1].start()
    for st in stores:
        st.wait()
    for h in range(12):
        probs_out(h).wait()


def call(kernel, ins, outs, scratch, name, **params):
    names = (tuple(ins), tuple(outs), tuple(scratch))
    got = pl.pallas_call(
        functools.partial(kernel, names),
        out_shape=[jax.ShapeDtypeStruct(s, d) for s, d, _ in outs.values()],
        in_specs=[sp for _, sp in ins.values()],
        out_specs=[sp for _, _, sp in outs.values()],
        scratch_shapes=list(scratch.values()),
        compiler_params=pltpu.CompilerParams(vmem_limit_bytes=BIG, **params),
        name=name,
    )(*[a for a, _ in ins.values()])
    return types.SimpleNamespace(**dict(zip(outs, got)))


def buf(*shape, dtype=BF):
    return pltpu.VMEM(shape, dtype)


def weight_bufs(names):
    return {"w_" + n: buf(4, 8 * W_SHAPES[n][0], W_SHAPES[n][1]) for n in names}


def front(tokens, feats, lengths, cotangent, weights, vectors):
    ins = {"tokens": (tokens, VM), "feats": (feats, VM), "lengths": (lengths, SM), "cotangent": (cotangent, VM)}
    ins.update({k: (v, HB) for k, v in weights.items()})
    ins.update({k: (v, VM) for k, v in vectors.items()})
    outs = {
        "result": ((PAGE, D), BF, VM),
        "qkv": ((PAGE, 3 * D), BF, VM),
        "probs": ((12, PAGE, PAGE), BF, HB),
        "mixture_back": ((PAGE, D), BF, VM),
        "sum_back": ((PAGE, D), F32, VM),
        "sums": ((8, D), F32, VM),
        "uplift_sum": ((1, FF), F32, VM),
        "g_combiner": ((D, D), BF, HB),
        "g_expander": ((D, FF), BF, HB),
        "g_reducer": ((FF, D), BF, HB),
    }
    scratch = weight_bufs(W_SHAPES)
    scratch.update(
        left=buf(PAGE, 1664), right=buf(PAGE, 1664), probs=buf(12, PAGE, PAGE), mixture=buf(PAGE, D),
        hold=buf(PAGE, D, dtype=F32), n1=buf(PAGE, D, dtype=F32), r1=buf(PAGE, 128, dtype=F32), low=buf(PAGE, D), low_t=buf(D, PAGE),
        activated=buf(PAGE, FF), slope=buf(PAGE, FF), reduced_back=buf(PAGE, D),
        g_reducer=buf(FF, D), g_expander=buf(D, FF), g_combiner=buf(D, D),
        load=pltpu.SemaphoreType.DMA((5,)), save=pltpu.SemaphoreType.DMA((12,)),
    )
    return call(front_kernel, ins, outs, scratch, "front")


def rear_kernel(names, *refs):
    i, o, s = name_refs(names, refs)
    loads = {}
    for k, w in enumerate(("relative", "projector")):
        loads[w] = pltpu.make_async_copy(getattr(i, w), flat(getattr(s, "w_" + w)), s.load.at[k])
        loads[w].start()

    def fetch(p, slot):
        return pltpu.make_async_copy(i.probs.at[pl.ds(2 * p, 2)], s.probs.at[slot], s.fetch.at[slot])

    fetch(0, 0).start()
    back_setup(i.feats, s.top, s.bottom)
    for k in range(6):
        s.tokens_t[k * 128 : (k + 1) * 128, :] = i.tokens[:, k * 128 : (k + 1) * 128].T
    loads["relative"].wait()

    @pl.loop(0, PAIRS)
    def _(p):
        slot = p % 2

        @pl.when(p + 1 < PAIRS)
        def _():
            fetch(p + 1, 1 - slot).start()

        fetch(p, slot).wait()
        back_pair(
            p, i.qkv, i.mixture_back, lambda e: s.probs.at[slot, e], s.w_relative, s.top, s.bottom, s.score_back, s.lifted, s.turned,
            s.g_relative, s.projected_back,
        )

    loads["projector"].wait()
    store = pltpu.make_async_copy(flat(s.g_relative), o.g_relative, s.load.at[0])
    store.start()
    project_back(i.tokens, s.tokens_t, s.projected_back, flat(s.w_projector), i.sum_back, s.g_projector, o.intercept_sum, o.token_gradient)
    last = pltpu.make_async_copy(s.g_projector, o.g_projector, s.load.at[1])
    last.start()
    last.wait()
    store.wait()


def rear(tokens, feats, kept, weights):
    ins = {"tokens": (tokens, VM), "feats": (feats, VM)}
    ins.update({k: (getattr(kept, k), VM) for k in ("qkv", "mixture_back", "sum_back")})
    ins["probs"] = (kept.probs, HB)
    ins.update({k: (weights[k], HB) for k in ("relative", "projector")})
    outs = {
        "token_gradient": ((PAGE, D), BF, VM),
        "intercept_sum": ((1, 3 * D), F32, VM),
        "g_relative": ((2 * D, D), BF, HB),
        "g_projector": ((D, 3 * D), BF, HB),
    }
    scratch = weight_bufs(("relative", "projector"))
    scratch.update(
        probs=buf(2, 2, PAGE, PAGE), top=buf(D + 128, PAGE), bottom=buf(D + 128, PAGE), score_back=buf(PAGE, PAGE),
        lifted=buf(D + 128, PAGE, dtype=F32), turned=buf(D, PAGE), tokens_t=buf(D, PAGE), projected_back=buf(PAGE, 3 * D),
        g_relative=buf(4, HALF, D), g_projector=buf(D, 3 * D),
        load=pltpu.SemaphoreType.DMA((2,)), fetch=pltpu.SemaphoreType.DMA((2,)),
    )
    return call(rear_kernel, ins, outs, scratch, "rear")


def make_feats(coordinates):
    step = jnp.arange(192, dtype=F32)
    frequency = jnp.exp(-jnp.log(10000.0) * step / 192)
    angles = coordinates.astype(F32)[:, :, None] * frequency
    return jnp.concatenate([jnp.cos(angles[0]), jnp.cos(angles[1]), jnp.sin(angles[0]), jnp.sin(angles[1])], axis=1).astype(BF)


ORDER = ("small", "projector", "relative", "combiner", "expander", "reducer")
COUNTS = {"intercept": 72, "uplift": 96, "baseline": 24, "stretch": 24, "center": 24, "offset": 24, "rescale": 24, "recenter": 24}


class Gather:
    def __init__(self, place, shards, full, local, send, recv):
        self.p, self.shards, self.full = place, shards, full
        self.local, self.send, self.recv = local, send, recv
        self.sent = []

    def remote(self, w, src, dst, s, r, device):
        return pltpu.make_async_remote_copy(
            src_ref=src, dst_ref=dst, send_sem=self.send.at[w, s], recv_sem=self.recv.at[w, r], device_id=device, device_id_type=MESH
        )

    def go(self, make):
        self.remote(*make()).start()
        self.sent.append(make)

    def arrived(self, w, ref, r):
        self.remote(w, ref, ref, 0, r, self.p.sibling).wait_recv()

    def begin(self):
        p = self.p
        for w in range(len(self.shards)):
            pltpu.make_async_copy(self.shards[w], self.own(w, p.z), self.local.at[w]).start()
            for s in (1, 2, 3):
                self.go(lambda w=w, s=s: (w, self.shards[w], self.own(w, p.z), s - 1, p.z, p.along_z((p.z + s) % NZ)))

    def rows(self, w, y, x, c):
        count = self.shards[w].shape[0]
        return pl.ds(pl.multiple_of(((y * NX + x) * NC + c) * count, 8), count)

    def own(self, w, z):
        p = self.p
        return self.full[w].at[z, self.rows(w, p.y, p.x, p.c)]

    def block(self, w, at):
        p = self.p
        y, x = {"own": (p.y, p.x), "first": (p.y1, p.x1), "second": (p.y2, p.x2), "across": (p.yd, p.xd)}[at]
        return self.full[w].at[:, self.rows(w, y, x, p.c)]

    def pass_on(self, w, at, *moves):
        for s, r, device in moves:
            self.go(lambda s=s, r=r, device=device: (w, self.block(w, at), self.block(w, at), s, r, device))

    def a(self, w):
        p = self.p
        pltpu.make_async_copy(self.shards[w], self.own(w, p.z), self.local.at[w]).wait()
        for s in (1, 2, 3):
            zs = (p.z + s) % NZ
            self.arrived(w, self.own(w, zs), zs)
        self.pass_on(w, "own", (3, 4, p.first), (4, 5, p.second), (5, 7, p.sibling))

    def b(self, w):
        p = self.p
        self.arrived(w, self.block(w, "first"), 4)
        self.pass_on(w, "first", (6, 6, p.second), (7, 8, p.sibling))

    def c(self, w):
        p = self.p
        self.arrived(w, self.block(w, "second"), 5)
        self.pass_on(w, "second", (8, 9, p.sibling))
        self.arrived(w, self.block(w, "across"), 6)
        self.pass_on(w, "across", (9, 10, p.sibling))

    def d(self, w):
        for r in range(7, 11):
            self.arrived(w, self.block(w, "own"), r)

    def end(self):
        for make in self.sent:
            self.remote(*make()).wait_send()


def ramp(n, width):
    quotient = jnp.floor((lax.broadcasted_iota(jnp.int32, (32, n), 1).astype(F32) + 0.5) * (1.0 / width)).astype(jnp.int32)
    mine = quotient == lax.broadcasted_iota(jnp.int32, (32, n), 0)
    col = lax.broadcasted_iota(jnp.int32, (128, n), 1)
    rest = col - jnp.floor((col.astype(F32) + 0.5) * (1.0 / width)).astype(jnp.int32) * width
    pick = jnp.where(rest == lax.broadcasted_iota(jnp.int32, (128, n), 0), 1.0, 0.0).astype(BF)
    return mine, pick


def widen(packs, vec, wide):
    k = 0
    for name, ref in (("intercept", wide.intercept), ("uplift", wide.uplift)):
        n = 32 * COUNTS[name]
        mine, pick = ramp(n, COUNTS[name])
        rows = packs[pl.ds(k, 32, stride=8), :].astype(BF)
        ref[...] = jnp.sum(jnp.where(mine, nn(rows, pick), 0.0), axis=0, keepdims=True)
        k += 1
    mine, pick = ramp(D, 24)
    for j in range(6):
        rows = packs[pl.ds(k + j, 32, stride=8), :].astype(BF)
        vec[j : j + 1, :] = jnp.sum(jnp.where(mine, nn(rows, pick), 0.0), axis=0, keepdims=True)


def narrow(rows, intercept_sum, uplift_sum, packs):
    def one(k, v, mine, pick):
        v = jnp.where(mine, v, 0.0)
        high = v.astype(BF)
        packs[pl.ds(k, 32, stride=8), :] = nt(high, pick) + nt((v - high.astype(F32)).astype(BF), pick)

    one(0, intercept_sum, *ramp(32 * 72, 72))
    one(1, uplift_sum, *ramp(32 * 96, 96))
    wide = ramp(D, 24)
    for j in range(6):
        one(2 + j, rows[j : j + 1, :], *wide)


def sinusoids(frequency, coordinates, feats_t, feats):
    for c in (0, 1):
        angles = frequency[...] * coordinates[c : c + 1, :].astype(F32)
        feats_t[c * 192 : (c + 1) * 192, :] = jnp.cos(angles).astype(BF)
        feats_t[HALF + c * 192 : HALF + (c + 1) * 192, :] = jnp.sin(angles).astype(BF)
    for k in range(6):
        feats[:, k * 128 : (k + 1) * 128] = feats_t[k * 128 : (k + 1) * 128, :].T


FREQUENCY = np.exp(-np.log(10000.0) * np.arange(192) / 192).astype(np.float32)[:, None]
VEC_ROWS = VECTORS[2:]


def fused_front_kernel(names, *refs):
    i, o, s = name_refs(names, refs)
    p = Place()
    enter(p)
    s.pack[...] = jnp.zeros((8, 128), F32)
    for k, v in enumerate(VECTORS):
        n = COUNTS[v]
        s.pack[k : k + 1, 0:n] = getattr(i, v)[...].astype(F32).reshape(1, n)
    shards = [s.pack] + [getattr(i, w) for w in ORDER[1:]]
    full = [s.packs] + [getattr(s, "w_" + w) for w in ORDER[1:]]
    g = Gather(p, shards, full, s.local, s.send, s.recv)
    g.begin()
    live = i.lengths[0]
    vec = types.SimpleNamespace(**{v: s.vec.at[k : k + 1] for k, v in enumerate(VEC_ROWS)})
    sinusoids(i.frequency, i.coordinates, o.feats_t, o.feats)
    g.a(0)
    g.a(1); g.b(0)
    g.a(2); g.b(1); g.c(0)
    g.a(3); g.b(2); g.c(1); g.d(0)
    widen(s.packs.reshape(256, 128), s.vec, types.SimpleNamespace(intercept=s.intercept, uplift=s.uplift))
    g.a(4); g.b(3); g.c(2); g.d(1)
    project(i.tokens, flat(s.w_projector), s.intercept, o.qkv)
    attend_setup(o.feats, s.left, s.right)
    g.a(5); g.b(4); g.c(3); g.d(2)

    def probs_out(h):
        return pltpu.make_async_copy(s.probs.at[h], o.probs.at[h], s.save.at[h])

    @pl.loop(0, PAIRS)
    def _(q):
        attend_pair(q, o.qkv, s.w_relative, o.feats, live, s.left, s.right, s.probs, s.mixture)
        probs_out(2 * q).start()
        probs_out(2 * q + 1).start()

        @pl.when(q == 1)
        def _():
            g.d(3)

        @pl.when(q == 3)
        def _():
            g.b(5)

        @pl.when(q == 5)
        def _():
            g.c(4)

    first_norm(i.tokens, s.mixture, flat(s.w_combiner), vec, s.hold, s.n1, s.r1, s.low)
    g.d(4)
    feed(s.low, flat(s.w_expander), s.uplift, s.activated, s.slope)
    g.c(5)
    for k in range(6):
        s.low_t[k * 128 : (k + 1) * 128, :] = s.low[:, k * 128 : (k + 1) * 128].T
    g.d(5)
    second_norm(s.n1, i.cotangent, s.activated, flat(s.w_reducer), vec, s.hold, s.reduced_back, o.sum_back, o.result, o.sums)
    feed_back(s.low_t, s.activated, s.slope, s.reduced_back, flat(s.w_reducer), flat(s.w_expander), s.g_reducer, s.g_expander, o.uplift_sum, o.sum_back)
    stores = [pltpu.make_async_copy(s.g_reducer, o.g_reducer, s.load.at[0]), pltpu.make_async_copy(s.g_expander, o.g_expander, s.load.at[1])]
    for st in stores:
        st.start()
    first_back(o.sum_back, s.n1, s.r1, vec, s.reduced_back, o.sums)
    branch_grads(s.mixture, s.reduced_back, flat(s.w_combiner), s.g_combiner, o.mixture_back)
    stores.append(pltpu.make_async_copy(s.g_combiner, o.g_combiner, s.load.at[2]))
    stores[-1].start()
    loads = [pltpu.make_async_copy(flat(s.w_projector), o.projector, s.load.at[3]), pltpu.make_async_copy(flat(s.w_relative), o.relative, s.load.at[4])]
    for st in loads:
        st.start()
    for st in stores + loads:
        st.wait()
    for h in range(12):
        probs_out(h).wait()
    g.end()


def fused_front(tokens, coordinates, lengths, cotangent, shards, vectors):
    ins = {"tokens": (tokens, VM), "coordinates": (coordinates, VM), "lengths": (lengths, SM), "cotangent": (cotangent, VM)}
    ins["frequency"] = (jnp.asarray(FREQUENCY), VM)
    ins.update({k: (shards[k], HB) for k in ORDER[1:]})
    ins.update({k: (v, VM) for k, v in vectors.items()})
    outs = {
        "result": ((PAGE, D), BF, VM),
        "qkv": ((PAGE, 3 * D), BF, VM),
        "feats": ((PAGE, D), BF, VM),
        "feats_t": ((D, PAGE), BF, VM),
        "probs": ((12, PAGE, PAGE), BF, HB),
        "mixture_back": ((PAGE, D), BF, VM),
        "sum_back": ((PAGE, D), F32, VM),
        "sums": ((8, D), F32, VM),
        "uplift_sum": ((1, FF), F32, VM),
        "g_combiner": ((D, D), BF, HB),
        "g_expander": ((D, FF), BF, HB),
        "g_reducer": ((FF, D), BF, HB),
        "projector": ((D, 3 * D), BF, HB),
        "relative": ((2 * D, D), BF, HB),
    }
    scratch = weight_bufs(W_SHAPES)
    scratch.update(
        left=buf(PAGE, 1664), right=buf(PAGE, 1664), probs=buf(12, PAGE, PAGE), mixture=buf(PAGE, D),
        hold=buf(PAGE, D, dtype=F32), n1=buf(PAGE, D, dtype=F32), r1=buf(PAGE, 128, dtype=F32), low=buf(PAGE, D), low_t=buf(D, PAGE),
        activated=buf(PAGE, FF), slope=buf(PAGE, FF), reduced_back=buf(PAGE, D),
        g_reducer=buf(FF, D), g_expander=buf(D, FF), g_combiner=buf(D, D),
        pack=buf(8, 128, dtype=F32), packs=buf(4, 64, 128, dtype=F32), vec=buf(8, D, dtype=F32),
        intercept=buf(1, 3 * D, dtype=F32), uplift=buf(1, FF, dtype=F32),
        load=pltpu.SemaphoreType.DMA((5,)), save=pltpu.SemaphoreType.DMA((12,)),
        local=pltpu.SemaphoreType.DMA((6,)), send=pltpu.SemaphoreType.DMA((6, 10)), recv=pltpu.SemaphoreType.DMA((6, 11)),
    )
    return call(fused_front_kernel, ins, outs, scratch, "fused_front", collective_id=0, has_side_effects=True)


LANES = 384
NAMES = ("projector", "relative", "combiner", "expander", "reducer")
BACKWARD = ("reducer", "expander", "combiner", "relative", "projector")


def whole_gather(v):
    return lax.all_gather(v, ("dp", "fsdp"), axis=0, tiled=True)


def whole_scatter(v):
    v = lax.psum_scatter(v.astype(F32), "dp", scatter_dimension=0, tiled=True)
    return lax.psum_scatter(v.astype(BF), "fsdp", scatter_dimension=0, tiled=True).astype(F32)


def cut(rows, sizes):
    parts = []
    at = 0
    for size in sizes:
        parts.append(rows[..., at : at + size])
        at += size
    return parts


def local(
    tokens, coordinates, lengths, cotangent, projector, intercept, relative, combiner, baseline,
    stretch, center, expander, uplift, reducer, offset, rescale, recenter, remote,
):
    vectors = (intercept, uplift, baseline, stretch, center, offset, rescale, recenter)
    matrices = (projector, relative, combiner, expander, reducer)
    sizes = [v.shape[0] for v in vectors]
    if remote:
        f = fused_front(tokens, coordinates, lengths, cotangent, dict(zip(NAMES, matrices)), dict(zip(VECTORS, vectors)))
        feats = f.feats
        weights = {"projector": f.projector, "relative": f.relative}
    else:
        rows = whole_gather(jnp.concatenate(vectors)[None])
        weights = {k: whole_gather(m) for k, m in zip(NAMES, matrices)}
        shared = {k: v.reshape(1, -1).astype(F32) for k, v in zip(VECTORS, cut(rows, sizes))}
        feats = make_feats(coordinates)
        f = front(tokens, feats, lengths, cotangent, weights, shared)
    r = rear(tokens, feats, f, weights)
    sums = [r.intercept_sum[0], f.uplift_sum[0]] + [f.sums[k] for k in range(6)]
    changes = (f.g_reducer, f.g_expander, f.g_combiner, r.g_relative, r.g_projector)
    count = D // 24 if remote else lax.axis_size(("dp", "fsdp"))
    stacked = jnp.concatenate([v.reshape(count, -1) for v in sums], axis=1)
    if remote:
        stacked = jnp.pad(stacked.astype(BF)[:, None], ((0, 0), (0, 7), (0, LANES - stacked.shape[1])))
        *shares, row = scatter_all(list(changes) + [stacked.reshape(-1, LANES)], 1)
        row = row[0]
    else:
        shares = [whole_scatter(c) for c in changes]
        row = whole_scatter(stacked)[0]
    share = dict(zip(BACKWARD, shares))
    small = dict(zip(VECTORS, cut(row, sizes)))
    return (
        f.result, r.token_gradient, share["projector"], small["intercept"], share["relative"], share["combiner"], small["baseline"],
        small["stretch"], small["center"], share["expander"], small["uplift"], share["reducer"], small["offset"], small["rescale"],
        small["recenter"],
    )


def solution(mesh):
    rows, line = P(("dp", "fsdp"), None), P(("dp", "fsdp"))
    remote = (mesh.shape["dp"], mesh.shape["fsdp"]) == (NZ * NY, NX * NC)
    return jax.shard_map(
        functools.partial(local, remote=remote),
        mesh=mesh,
        in_specs=(rows, P(None, ("dp", "fsdp")), line, rows, rows, line, rows, rows, line, line, line, rows, line, rows, line, line, line),
        out_specs=(rows, rows, rows, line, rows, rows, line, line, line, rows, line, rows, line, line, line),
        check_vma=False,
    )
```

```python
import functools
import types

import jax
import jax.numpy as jnp
import numpy as np
from jax import lax
from jax.experimental import pallas as pl
from jax.experimental.pallas import tpu as pltpu
from jax.sharding import PartitionSpec as P

MESH = pl.DeviceIdType.MESH
NZ, NY, NX, NC = 4, 2, 2, 2


PAGE = 512
D = 768
FF = 3072
HALF = 384
PAIRS = 6
SCALE = 192.0 ** -0.5
EPSILON = 1e-12
NEGATIVE = -1e30
BF = jnp.bfloat16
F32 = jnp.float32
PIECE = 256
SUM_BASELINE, SUM_STRETCH, SUM_CENTER, SUM_OFFSET, SUM_RESCALE, SUM_RECENTER = range(6)
VM = pl.BlockSpec(memory_space=pltpu.VMEM)
HB = pl.BlockSpec(memory_space=pl.ANY)
SM = pl.BlockSpec(memory_space=pltpu.SMEM)
BIG = 63 << 20
W_SHAPES = {"projector": (24, 2304), "relative": (48, 768), "combiner": (24, 768), "expander": (24, 3072), "reducer": (96, 768)}
VECTORS = ("intercept", "uplift", "baseline", "stretch", "center", "offset", "rescale", "recenter")
ORDER = ("small", "projector", "relative", "combiner", "expander", "reducer")
COUNTS = {"intercept": 72, "uplift": 96, "baseline": 24, "stretch": 24, "center": 24, "offset": 24, "rescale": 24, "recenter": 24}
FREQUENCY = np.exp(-np.log(10000.0) * np.arange(192) / 192).astype(np.float32)[:, None]
VEC_ROWS = VECTORS[2:]


class Place:
    def __init__(self):
        d = lax.axis_index("dp")
        f = lax.axis_index("fsdp")
        self.z, self.y = d // NY, d % NY
        self.x, self.c = f // NC, f % NC
        z, y, x, c = self.z, self.y, self.x, self.c
        self.y1, self.x1 = y + (1 - c) * (1 - 2 * y), x + c * (1 - 2 * x)
        self.y2, self.x2 = y + c * (1 - 2 * y), x + (1 - c) * (1 - 2 * x)
        self.yd, self.xd = 1 - y, 1 - x
        self.first = (z * NY + self.y1, self.x1 * NC + c)
        self.second = (z * NY + self.y2, self.x2 * NC + c)
        self.sibling = (z * NY + y, x * NC + 1 - c)

    def along_z(self, z):
        return (z * NY + self.y, self.x * NC + self.c)

    def peers(self):
        return [self.first, self.second, self.sibling] + [self.along_z((self.z + s) % NZ) for s in (1, 2, 3)]


def enter(place):
    barrier = pltpu.get_barrier_semaphore()
    peers = place.peers()
    for peer in peers:
        pl.semaphore_signal(barrier, inc=1, device_id=peer, device_id_type=MESH)
    pl.semaphore_wait(barrier, len(peers))


def nn(a, b):
    return jnp.dot(a, b, preferred_element_type=F32)


def nt(a, b):
    return lax.dot_general(a, b, (((1,), (1,)), ((), ())), preferred_element_type=F32)


def span(i, size):
    return pl.ds(pl.multiple_of(i * size, size), size)


def own_lanes(e, rows):
    lane = lax.broadcasted_iota(jnp.int32, (rows, 128), 1)
    return lane < 64 if e == 0 else lane >= 64


def only(e, v):
    return jnp.where(own_lanes(e, v.shape[0]), v, jnp.zeros_like(v))


def only_rows(e, v):
    row = lax.broadcasted_iota(jnp.int32, v.shape, 0)
    return jnp.where(row < 64 if e == 0 else row >= 64, v, jnp.zeros_like(v))


def project(tokens, projector, intercept, qkv):
    @pl.loop(0, 9)
    def _(n):
        cols = span(n, PIECE)
        qkv[:, cols] = (nn(tokens[...], projector[:, cols]) + intercept[:, cols]).astype(BF)


def table(relative, side, half, cols):
    return relative[2 * side : 2 * side + 2, half * 192 : (half + 1) * 192, cols].reshape(HALF, 128)


def turn(weights_of, feats, out, at, rows):
    ws, wc = weights_of
    c = feats[rows, :HALF].astype(F32)
    s = feats[rows, HALF:].astype(F32)
    out[rows, at : at + HALF] = (ws * s + wc * c).astype(BF)
    out[rows, at + HALF : at + 2 * HALF] = (wc * s - ws * c).astype(BF)


def mean(v):
    return jnp.sum(v, axis=1, keepdims=True) * (1.0 / D)


def first_norm(tokens, mixture, combiner, vec, hold, n1, r1, low):
    @pl.loop(0, 3)
    def _(n):
        cols = span(n, PIECE)
        hold[:, cols] = nn(mixture[...], combiner[:, cols])

    @pl.loop(0, PAGE // 32)
    def _(i):
        rows = span(i, 32)
        v = tokens[rows, :].astype(F32) + hold[rows, :] + vec.baseline[...]
        v = v - mean(v)
        r = lax.rsqrt(mean(v * v) + EPSILON)
        v = v * r
        n1[rows, :] = v
        r1[rows, :] = jnp.broadcast_to(r, (32, 128))
        low[rows, :] = (v * vec.stretch[...] + vec.center[...]).astype(BF)


def second_norm(n1, cotangent, vec, hold, reduced_back, second_back, result, sums):
    zero = jnp.zeros((8, D), F32)

    def fold(v):
        return jnp.sum(v.reshape(4, 8, D), axis=0)

    def body(i, carry):
        rescale_sum, recenter_sum, offset_sum = carry
        rows = span(i, 32)
        v = (n1[rows, :] * vec.stretch[...] + vec.center[...]) + hold[rows, :] + vec.offset[...]
        v = v - mean(v)
        r = lax.rsqrt(mean(v * v) + EPSILON)
        v = v * r
        g = cotangent[rows, :].astype(F32)
        result[rows, :] = (v * vec.rescale[...] + vec.recenter[...]).astype(BF)
        u = g * vec.rescale[...]
        back = r * (u - mean(u) - v * mean(u * v))
        second_back[rows, :] = back
        low = back.astype(BF)
        reduced_back[rows, :] = low
        return (rescale_sum + fold(g * v), recenter_sum + fold(g), offset_sum + fold(low.astype(F32)))

    a, b, c = lax.fori_loop(0, PAGE // 32, body, (zero, zero, zero))
    for k, v in ((SUM_RESCALE, a), (SUM_RECENTER, b), (SUM_OFFSET, c)):
        sums[k : k + 1, :] = jnp.sum(v, axis=0, keepdims=True)


def first_back(total, n1, r1, vec, branch_back, sums):
    zero = jnp.zeros((8, D), F32)

    def fold(v):
        return jnp.sum(v.reshape(4, 8, D), axis=0)

    def body(i, carry):
        stretch_sum, center_sum, baseline_sum = carry
        rows = span(i, 32)
        b = total[rows, :]
        v = n1[rows, :]
        u = b * vec.stretch[...]
        back = r1[rows, :1] * (u - mean(u) - v * mean(u * v))
        total[rows, :] = back
        low = back.astype(BF)
        branch_back[rows, :] = low
        return (stretch_sum + fold(b * v), center_sum + fold(b), baseline_sum + fold(low.astype(F32)))

    a, b, c = lax.fori_loop(0, PAGE // 32, body, (zero, zero, zero))
    for k, v in ((SUM_STRETCH, a), (SUM_CENTER, b), (SUM_BASELINE, c)):
        sums[k : k + 1, :] = jnp.sum(v, axis=0, keepdims=True)


def branch_grads(mixture, branch_back, combiner, grad_combiner, mixture_back):
    @pl.loop(0, 3)
    def _(n):
        cols = span(n, PIECE)
        grad_combiner[cols, :] = nn(mixture[:, cols].T, branch_back[...]).astype(BF)
        mixture_back[:, cols] = nt(branch_back[...], combiner[cols, :]).astype(BF)


def back_setup(feats, top, bottom):
    for k in range(6):
        block = feats[:, k * 128 : (k + 1) * 128].T
        top[k * 128 : (k + 1) * 128, :] = block
        bottom[k * 128 : (k + 1) * 128, :] = block


def unturn(g, t, cols, out):
    @pl.loop(0, HALF // 64)
    def _(i):
        a = span(i, 64)
        b = pl.ds(pl.multiple_of(HALF + i * 64, 64), 64)
        c = t[a, :].astype(F32)
        s = t[b, :].astype(F32)
        g1 = g[a, :]
        g2 = g[b, :]
        out[a, :] = (g1 * s - g2 * c).astype(BF)
        out[b, :] = (g1 * c + g2 * s).astype(BF)


def flat(ref):
    return ref.reshape(ref.shape[0] * ref.shape[1], ref.shape[2])


def name_refs(groups, refs):
    out = []
    at = 0
    for g in groups:
        out.append(types.SimpleNamespace(**dict(zip(g, refs[at : at + len(g)]))))
        at += len(g)
    return out


def call(kernel, ins, outs, scratch, name, **params):
    names = (tuple(ins), tuple(outs), tuple(scratch))
    got = pl.pallas_call(
        functools.partial(kernel, names),
        out_shape=[jax.ShapeDtypeStruct(s, d) for s, d, _ in outs.values()],
        in_specs=[sp for _, sp in ins.values()],
        out_specs=[sp for _, _, sp in outs.values()],
        scratch_shapes=list(scratch.values()),
        compiler_params=pltpu.CompilerParams(vmem_limit_bytes=BIG, **params),
        name=name,
    )(*[a for a, _ in ins.values()])
    return types.SimpleNamespace(**dict(zip(outs, got)))


def buf(*shape, dtype=BF):
    return pltpu.VMEM(shape, dtype)


class Gather:
    def __init__(self, place, shards, full, local, send, recv):
        self.p, self.shards, self.full = place, shards, full
        self.local, self.send, self.recv = local, send, recv
        self.sent = []

    def remote(self, w, src, dst, s, r, device):
        return pltpu.make_async_remote_copy(
            src_ref=src, dst_ref=dst, send_sem=self.send.at[w, s], recv_sem=self.recv.at[w, r], device_id=device, device_id_type=MESH
        )

    def go(self, make):
        self.remote(*make()).start()
        self.sent.append(make)

    def arrived(self, w, ref, r):
        self.remote(w, ref, ref, 0, r, self.p.sibling).wait_recv()

    def begin(self):
        p = self.p
        for w in range(len(self.shards)):
            pltpu.make_async_copy(self.shards[w], self.own(w, p.z), self.local.at[w]).start()
            for s in (1, 2, 3):
                self.go(lambda w=w, s=s: (w, self.shards[w], self.own(w, p.z), s - 1, p.z, p.along_z((p.z + s) % NZ)))

    def rows(self, w, y, x, c):
        count = self.shards[w].shape[0]
        return pl.ds(pl.multiple_of(((y * NX + x) * NC + c) * count, 8), count)

    def own(self, w, z):
        p = self.p
        return self.full[w].at[z, self.rows(w, p.y, p.x, p.c)]

    def block(self, w, at):
        p = self.p
        y, x = {"own": (p.y, p.x), "first": (p.y1, p.x1), "second": (p.y2, p.x2), "across": (p.yd, p.xd)}[at]
        return self.full[w].at[:, self.rows(w, y, x, p.c)]

    def pass_on(self, w, at, *moves):
        for s, r, device in moves:
            self.go(lambda s=s, r=r, device=device: (w, self.block(w, at), self.block(w, at), s, r, device))

    def a(self, w):
        p = self.p
        pltpu.make_async_copy(self.shards[w], self.own(w, p.z), self.local.at[w]).wait()
        for s in (1, 2, 3):
            zs = (p.z + s) % NZ
            self.arrived(w, self.own(w, zs), zs)
        self.pass_on(w, "own", (3, 4, p.first), (4, 5, p.second), (5, 7, p.sibling))

    def b(self, w):
        p = self.p
        self.arrived(w, self.block(w, "first"), 4)
        self.pass_on(w, "first", (6, 6, p.second), (7, 8, p.sibling))

    def c(self, w):
        p = self.p
        self.arrived(w, self.block(w, "second"), 5)
        self.pass_on(w, "second", (8, 9, p.sibling))
        self.arrived(w, self.block(w, "across"), 6)
        self.pass_on(w, "across", (9, 10, p.sibling))

    def d(self, w):
        for r in range(7, 11):
            self.arrived(w, self.block(w, "own"), r)

    def end(self):
        for make in self.sent:
            self.remote(*make()).wait_send()


def ramp(start, width):
    col = lax.broadcasted_iota(jnp.int32, (32, D), 1) + start
    mine = jnp.floor((col.astype(F32) + 0.5) * (1.0 / width)).astype(jnp.int32) == lax.broadcasted_iota(jnp.int32, (32, D), 0)
    col = lax.broadcasted_iota(jnp.int32, (128, D), 1) + start
    rest = col - jnp.floor((col.astype(F32) + 0.5) * (1.0 / width)).astype(jnp.int32) * width
    pick = jnp.where(rest == lax.broadcasted_iota(jnp.int32, (128, D), 0), 1.0, 0.0).astype(BF)
    return mine, pick


def widen(packs, vec, wide):
    k = 0
    for name, ref in (("intercept", wide.intercept), ("uplift", wide.uplift)):
        rows = packs[pl.ds(k, 32, stride=8), :].astype(BF)
        for start in range(0, 32 * COUNTS[name], D):
            mine, pick = ramp(start, COUNTS[name])
            ref[:, start : start + D] = jnp.sum(jnp.where(mine, nn(rows, pick), 0.0), axis=0, keepdims=True)
        k += 1
    mine, pick = ramp(0, 24)
    for j in range(6):
        rows = packs[pl.ds(k + j, 32, stride=8), :].astype(BF)
        vec[j : j + 1, :] = jnp.sum(jnp.where(mine, nn(rows, pick), 0.0), axis=0, keepdims=True)


def narrow(sums, intercept_sum, uplift_sum, packs):
    def one(v, mine, pick):
        v = jnp.where(mine, v, 0.0)
        high = v.astype(BF)
        return nt(high, pick) + nt((v - high.astype(F32)).astype(BF), pick)

    for k, (name, ref) in enumerate((("intercept", intercept_sum), ("uplift", uplift_sum))):
        total = jnp.zeros((32, 128), F32)
        for start in range(0, 32 * COUNTS[name], D):
            total += one(ref[:, start : start + D], *ramp(start, COUNTS[name]))
        packs[pl.ds(k, 32, stride=8), :] = total
    mine, pick = ramp(0, 24)
    for j in range(6):
        packs[pl.ds(2 + j, 32, stride=8), :] = one(sums[j : j + 1, :], mine, pick)


def sinusoids(frequency, coordinates, feats_t, feats):
    for c in (0, 1):
        angles = frequency[...] * coordinates[c : c + 1, :].astype(F32)
        feats_t[c * 192 : (c + 1) * 192, :] = jnp.cos(angles).astype(BF)
        feats_t[HALF + c * 192 : HALF + (c + 1) * 192, :] = jnp.sin(angles).astype(BF)
    for k in range(6):
        feats[:, k * 128 : (k + 1) * 128] = feats_t[k * 128 : (k + 1) * 128, :].T


class Scatter:
    ROLES = ("own", "first", "second", "across")

    def __init__(self, place, counts, grads, blocks, outs, send, recv):
        self.p, self.counts, self.grads, self.blocks, self.outs = place, counts, grads, blocks, outs
        self.send, self.recv = send, recv
        self.sent = []

    def remote(self, w, src, dst, s, r, device):
        return pltpu.make_async_remote_copy(
            src_ref=src, dst_ref=dst, send_sem=self.send.at[w, s], recv_sem=self.recv.at[w, r], device_id=device, device_id_type=MESH
        )

    def go(self, make):
        self.remote(*make()).start()
        self.sent.append(make)

    def arrived(self, w, ref, r):
        self.remote(w, ref, ref, 0, r, self.p.sibling).wait_recv()

    def at(self, role):
        p = self.p
        return {"own": (p.y, p.x), "first": (p.y1, p.x1), "second": (p.y2, p.x2), "across": (p.yd, p.xd)}[role]

    def part(self, w, y, x, c):
        count = self.counts[w]
        return self.grads[w].at[:, pl.ds(pl.multiple_of(((y * NX + x) * NC + c) * count, 8), count)]

    def begin(self, w):
        theirs = {"own": "own", "first": "second", "second": "first", "across": "across"}
        for b in (3, 2, 1, 0):
            role = theirs[self.ROLES[b]]
            self.go(lambda b=b, role=role: (w, self.part(w, *self.at(role), 1 - self.p.c), self.blocks[w](b), b, b, self.p.sibling))

    def add(self, w, b, other):
        mine = self.blocks[w](b)

        @pl.loop(0, NZ)
        def _(k):
            mine[k] = (mine[k].astype(F32) + other[k].astype(F32)).astype(mine.dtype)

    def s(self, w):
        block = self.blocks[w]
        for b in (3, 2, 1, 0):
            self.arrived(w, block(b), b)
            self.add(w, b, self.part(w, *self.at(self.ROLES[b]), self.p.c))
            if b >= 2:
                self.go(lambda b=b: (w, block(b), block(7 - b), 7 - b, 7 - b, self.p.second))

    def x(self, w):
        block = self.blocks[w]
        self.arrived(w, block(4), 4)
        self.add(w, 1, block(4))
        self.go(lambda: (w, block(1), block(6), 6, 6, self.p.first))
        self.arrived(w, block(5), 5)
        self.add(w, 0, block(5))

    def f(self, w):
        p = self.p
        block = self.blocks[w]
        self.arrived(w, block(6), 6)
        self.add(w, 0, block(6))
        for s in (1, 2, 3):

            def make(s=s):
                zt = (p.z + s) % NZ
                return w, block(0).at[zt], block(7).at[p.z], 6 + s, 7 + p.z, p.along_z(zt)

            self.go(make)

    def z(self, w):
        p = self.p
        total = self.blocks[w](0)[p.z].astype(F32)
        for s in (1, 2, 3):
            zs = (p.z + s) % NZ
            self.arrived(w, self.blocks[w](7).at[zs], 7 + zs)
            total += self.blocks[w](7)[zs].astype(F32)
        self.outs[w][...] = total

    def end(self):
        for make in self.sent:
            self.remote(*make()).wait_send()


def pool_at(n):
    return pl.ds(pl.multiple_of((n >> 1) * 512, 512), 512), pl.ds(pl.multiple_of((n & 1) * PIECE, PIECE), PIECE)


def attend(p, qkv, relative, feats, live, left, right, slots, mixture):
    lanes = span(p, 128)
    q2 = qkv[:, lanes]
    k2 = qkv[:, span(p + PAIRS, 128)]
    v2 = qkv[:, span(p + 2 * PAIRS, 128)]
    every = slice(None)
    for e in (0, 1):
        q = only(e, q2)
        k = only(e, k2)
        turn((nt(q, table(relative, 0, 0, lanes)), nt(q, table(relative, 0, 1, lanes))), feats, left, 0, every)
        turn((nt(k, table(relative, 1, 0, lanes)), nt(k, table(relative, 1, 1, lanes))), feats, right, 0, every)
        scores = (nt(left[...], feats[...]) + nt(q, k2) + nt(feats[...], right[...])) * SCALE
        key = lax.broadcasted_iota(jnp.int32, scores.shape, 1)
        scores = jnp.where(key < live, scores, NEGATIVE)
        powers = jnp.exp(scores - jnp.max(scores, axis=1, keepdims=True))
        share = (powers / jnp.sum(powers, axis=1, keepdims=True)).astype(BF)
        slots[e][...] = share
        part = nn(share, only(e, v2))
        if e == 0:
            mixture[:, lanes] = part.astype(BF)
        else:
            mixture[:, lanes] = jnp.where(own_lanes(1, PAGE), part.astype(BF), mixture[:, lanes])


def feed_pool(low, expander, uplift, activated, slope):
    @pl.loop(0, FF // PIECE)
    def _(n):
        cols = span(n, PIECE)
        v = nn(low[...], expander[:, cols]) + uplift[:, cols]
        half = 0.5 * lax.erf(v * (0.5 ** 0.5)) + 0.5
        activated[pool_at(n)] = (v * half).astype(BF)
        slope[pool_at(n)] = (half + v * (jnp.exp(v * v * -0.5) * 0.3989422804014327)).astype(BF)


def reduce_pool(activated, reducer, hold):
    @pl.loop(0, 3)
    def _(n):
        cols = span(n, PIECE)
        total = nn(activated[0:512, :], reducer[0:512, cols])
        for j in range(1, 6):
            total += nn(activated[512 * j : 512 * (j + 1), :], reducer[512 * j : 512 * (j + 1), cols])
        hold[:, cols] = total


def reducer_gradient(activated, reduced_back, grad_reducer):
    @pl.loop(0, FF // PIECE)
    def _(n):
        grad_reducer[span(n, PIECE), :] = nn(activated[pool_at(n)].T, reduced_back[...]).astype(BF)


def expander_gradient(low_t, slope, reduced_back, reducer, expander, grad_expander, uplift_sum, total):
    @pl.loop(0, FF // PIECE)
    def _(n):
        cols = span(n, PIECE)
        inner = (nt(reduced_back[...], reducer[cols, :]) * slope[pool_at(n)].astype(F32)).astype(BF)
        uplift_sum[:, cols] = jnp.sum(inner.astype(F32), axis=0, keepdims=True)
        grad_expander[:, cols] = nn(low_t[...], inner).astype(BF)
        total[...] += nt(inner, expander[:, cols])


def attend_back(p, qkv, mixture_back, slots, ready, done, relative, top, bottom, score_back, two, turned, grad_relative, back_t):
    lanes = span(p, 128)
    q2 = qkv[:, lanes]
    k2 = qkv[:, span(p + PAIRS, 128)]
    v2 = qkv[:, span(p + 2 * PAIRS, 128)]
    m2 = mixture_back[:, lanes]
    qt, kt, mt = q2.T, k2.T, m2.T
    tables = [[table(relative, side, half, lanes).T for half in (0, 1)] for side in (0, 1)]
    query_t = jnp.zeros((128, PAGE), F32)
    key_t = jnp.zeros((128, PAGE), F32)
    value_t = jnp.zeros((128, PAGE), F32)
    lifted = two.at[0 : D + 128, 0:PAGE]

    def table_grad(e, side, t2):
        g = two.at[0:D, PAGE + 128 * side : PAGE + 128 * (side + 1)]
        if e == 0:
            g[...] = nn(turned[...], only(0, t2))
        else:
            for half in (0, 1):
                cut = slice(half * HALF, (half + 1) * HALF)
                block = (g[cut, :] + nn(turned[cut, :], only(1, t2))).astype(BF)
                grad_relative[2 * side : 2 * side + 2, half * 192 : (half + 1) * 192, lanes] = block.reshape(2, 192, 128)

    for e in (0, 1):
        me = only(e, m2)
        top[D:, :] = only_rows(e, kt)
        bottom[D:, :] = only_rows(e, qt)
        back = nt(me, v2)
        ready(e)
        share = slots[e][...].astype(F32)
        score_back[...] = (share * (back - jnp.sum(share * back, axis=1, keepdims=True)) * SCALE).astype(BF)
        value_t += nn(only_rows(e, mt), slots[e][...])
        done(e)
        lifted[...] = nt(top[...], score_back[...])
        query_t += lifted[D:, :]
        unturn(lifted, top, None, turned)
        table_grad(e, 0, q2)
        query_t += only_rows(e, nn(tables[0][0], turned[:HALF, :]) + nn(tables[0][1], turned[HALF:, :]))
        lifted[...] = nn(bottom[...], score_back[...])
        key_t += lifted[D:, :]
        unturn(lifted, top, None, turned)
        table_grad(e, 1, k2)
        key_t += only_rows(e, nn(tables[1][0], turned[:HALF, :]) + nn(tables[1][1], turned[HALF:, :]))
    back_t[lanes, :] = query_t.astype(BF)
    back_t[span(p + PAIRS, 128), :] = key_t.astype(BF)
    back_t[span(p + 2 * PAIRS, 128), :] = value_t.astype(BF)


def projector_gradient(tokens_t, back_t, grad_projector, intercept_sum):
    @pl.loop(0, 9)
    def _(n):
        cols = span(n, PIECE)
        b = back_t[cols, :]
        intercept_sum[:, cols] = nt(jnp.ones((8, PAGE), BF), b)[0:1, :]
        grad_projector[:, :, cols] = nt(tokens_t[...], b).astype(BF).reshape(4, 192, PIECE)


def token_gradient(projector, back_t, sum_back, out):
    @pl.loop(0, 3)
    def _(n):
        cols = span(n, PIECE)
        out[:, cols] = (sum_back[:, cols] + nn(projector[cols, :], back_t[...]).T).astype(BF)


def transposed(src, dst):
    for k in range(6):
        dst[k * 128 : (k + 1) * 128, :] = src[:, k * 128 : (k + 1) * 128].T


def layer_kernel(remote, names, *refs):
    i, o, s = name_refs(names, refs)
    full = [getattr(s, "w_" + w) for w in ORDER[1:]]
    shards = [getattr(i, w) for w in ORDER[1:]]
    take_tokens = pltpu.make_async_copy(i.tokens, s.mixture_back, s.load.at[0])
    take_cotangent = pltpu.make_async_copy(i.cotangent, s.cotangent, s.load.at[1])
    take_tokens.start()
    if remote:
        p = Place()
        enter(p)
        s.pack[...] = jnp.zeros((8, 128), F32)
        for k, v in enumerate(VECTORS):
            n = COUNTS[v]
            s.pack[k : k + 1, 0:n] = getattr(i, v)[...].astype(F32).reshape(1, n)
        g = Gather(p, [s.pack] + shards, [s.packs] + full, s.local, s.send, s.recv)
        g.begin()
        vec_ref, intercept, uplift = s.vec, s.intercept, s.uplift
    else:
        takes = [pltpu.make_async_copy(a, flat(b), s.load.at[2 + k]) for k, (a, b) in enumerate(zip(shards, full))]
        for t in takes:
            t.start()
        vec_ref, intercept, uplift = i.vec, i.intercept, i.uplift
    w = types.SimpleNamespace(**{n: flat(ref) for n, ref in zip(ORDER[1:], full)})
    vec = types.SimpleNamespace(**{v: vec_ref.at[k : k + 1] for k, v in enumerate(VEC_ROWS)})
    live = i.lengths[0]
    wide = s.wide.reshape(3 * PAGE, D)
    low, mixture, reduced_back = (wide.at[k * PAGE : (k + 1) * PAGE] for k in range(3))
    n1, hold = s.two.at[0:PAGE], s.two.at[PAGE : 2 * PAGE]
    left, right = flat(s.g_reducer).at[0:PAGE], flat(s.g_reducer).at[PAGE : 2 * PAGE]
    activated, slope = s.activated, s.slope

    sinusoids(i.frequency, i.coordinates, s.low_t, s.feats)
    if remote:
        g.a(0)
        g.a(1); g.b(0)
        g.a(2); g.b(1); g.c(0)
        g.a(3); g.b(2); g.c(1); g.d(0)
        widen(s.packs.reshape(256, 128), s.vec, types.SimpleNamespace(intercept=s.intercept, uplift=s.uplift))
        g.a(4); g.b(3); g.c(2); g.d(1)
        early = {1: [(g.d, 3)], 3: [(g.b, 5)], 5: [(g.c, 4)]}
    else:
        for t in takes:
            t.wait()
        early = {}
    take_tokens.wait()
    project(s.mixture_back, w.projector, intercept, s.qkv)
    if remote:
        g.a(5); g.b(4); g.c(3); g.d(2)

    slots = [s.low_t.at[0:PAGE], s.cotangent.at[:, 0:PAGE]]

    def keep(q, e):
        return pltpu.make_async_copy(slots[e], o.probs.at[2 * q + e], s.keep.at[e])

    def fetch(q, e):
        return pltpu.make_async_copy(o.probs.at[2 * q + e], slots[e], s.keep.at[e])

    def hooks(q, table_of):
        for k, steps in table_of.items():

            @pl.when(q == k)
            def _(steps=steps):
                for step, w in steps:
                    step(w)

    @pl.loop(0, PAIRS)
    def _(q):
        @pl.when(q >= 1)
        def _():
            keep(q - 1, 0).wait()
            keep(q - 1, 1).wait()

        attend(q, s.qkv, s.w_relative, s.feats, live, left, right, slots, mixture)
        keep(q, 0).start()
        keep(q, 1).start()
        hooks(q, early)

    keep(PAIRS - 1, 0).wait()
    keep(PAIRS - 1, 1).wait()
    take_cotangent.start()

    first_norm(s.mixture_back, mixture, w.combiner, vec, hold, n1, s.r1, low)
    if remote:
        g.d(4)
    feed_pool(low, w.expander, uplift, activated, slope)
    transposed(low, s.low_t)
    if remote:
        g.c(5)
        g.d(5)
    take_cotangent.wait()
    reduce_pool(activated, w.reducer, hold)
    second_norm(n1, s.cotangent, vec, hold, reduced_back, s.sum_back, s.cotangent, o.sums if not remote else s.sums)
    give_result = pltpu.make_async_copy(s.cotangent, o.result, s.load.at[1])
    give_result.start()
    sums, uplift_sum, intercept_sum = (s.sums, s.uplift, s.intercept) if remote else (o.sums, o.uplift_sum, o.intercept_sum)
    reducer_gradient(activated, reduced_back, flat(s.g_reducer))
    grads = [s.g_reducer, s.g_expander, s.g_combiner, s.w_reducer.at[:, 0:HALF], s.w_expander.at[:, :, 0 : 3 * D]]
    late = {}
    if remote:
        g.end()
        blocks = [
            lambda b: s.held_reducer.at[b] if b < 4 else s.wide.at[4 * b - 16 : 4 * b - 12],
            lambda b: s.held_expander.at[b],
            lambda b: s.w_expander.at[:, 24 * b : 24 * b + 24, 3 * D :],
            lambda b: s.w_reducer.at[:, HALF + 48 * b : HALF + 48 * b + 48],
            lambda b: s.held_projector.at[b],
            lambda b: s.held_small.at[b],
        ]
        outs = [o.reducer, o.expander, o.combiner, o.relative, o.projector, o.small]
        t = Scatter(p, [96, 24, 24, 48, 24, 8], grads + [s.packs], blocks, outs, s.send2, s.recv2)
        t.begin(0)
    else:
        gives = [pltpu.make_async_copy(a, b, s.give.at[k]) for k, (a, b) in enumerate(zip(grads, [o.reducer, o.expander, o.combiner, o.relative, o.projector]))]
        gives[0].start()
    expander_gradient(s.low_t, slope, reduced_back, w.reducer, w.expander, flat(s.g_expander), uplift_sum, s.sum_back)
    if remote:
        t.begin(1)
    else:
        gives[1].start()
    first_back(s.sum_back, n1, s.r1, vec, reduced_back, sums)
    branch_grads(mixture, reduced_back, w.combiner, flat(s.g_combiner), s.mixture_back)
    fetch(0, 0).start()
    give_result.wait()
    fetch(0, 1).start()
    if remote:
        for peer in p.peers():
            pl.semaphore_signal(s.ready, inc=1, device_id=peer, device_id_type=MESH)
        pl.semaphore_wait(s.ready, 6)
        t.begin(2)
        t.s(0)
        t.s(1)
        late = {0: [(t.s, 2)], 1: [(t.x, 0)], 2: [(t.f, 0)], 3: [(t.x, 1)], 4: [(t.f, 1), (t.x, 2), (t.z, 0)], 5: [(t.f, 2), (t.z, 1)]}
    else:
        gives[2].start()
    top, bottom = activated.at[0:896], activated.at[896:1792]
    turned, score_back = activated.at[1792:2560], activated.at[2560:3072]
    tokens_t, back_t = slope.at[0:D], slope.at[D:]
    back_setup(s.feats, top, bottom)
    again = pltpu.make_async_copy(i.tokens, s.feats, s.load.at[0])
    again.start()
    again.wait()
    transposed(s.feats, tokens_t)

    @pl.loop(0, PAIRS)
    def _(q):
        def done(e):
            @pl.when(q + 1 < PAIRS)
            def _():
                fetch(q + 1, e).start()

        attend_back(
            q, s.qkv, s.mixture_back, slots, lambda e: fetch(q, e).wait(), done, s.w_relative, top, bottom, score_back, s.two, turned, grads[3], back_t
        )
        hooks(q, late)

    if remote:
        t.begin(3)
    else:
        gives[3].start()
    projector_gradient(tokens_t, back_t, grads[4], intercept_sum)
    if remote:
        t.begin(4)
        narrow(s.sums, intercept_sum, uplift_sum, s.packs.reshape(256, 128))
        t.begin(5)
        t.s(3)
        t.s(4)
        t.s(5)
    else:
        gives[4].start()
    token_gradient(w.projector, back_t, s.sum_back, s.feats)
    give_tokens = pltpu.make_async_copy(s.feats, o.token_gradient, s.load.at[0])
    give_tokens.start()
    if remote:
        t.z(2)
        t.x(3); t.x(4); t.x(5)
        t.f(3); t.f(4); t.f(5)
        t.z(3); t.z(4); t.z(5)
        t.end()
    else:
        for c in gives:
            c.wait()
    give_tokens.wait()


def layer(tokens, coordinates, lengths, cotangent, weights, vectors, remote):
    ins = {"tokens": (tokens, HB), "coordinates": (coordinates, VM), "lengths": (lengths, SM), "cotangent": (cotangent, HB)}
    ins["frequency"] = (jnp.asarray(FREQUENCY), VM)
    ins.update({k: (weights[k], HB) for k in ORDER[1:]})
    ins.update({k: (v, VM) for k, v in vectors.items()})
    outs = {"result": ((PAGE, D), BF, HB), "token_gradient": ((PAGE, D), BF, HB), "probs": ((2 * PAIRS, PAGE, PAGE), BF, HB)}
    for k in ORDER[1:]:
        r, n = W_SHAPES[k]
        outs[k] = ((r, n), F32, VM) if remote else ((4, 8 * r, n), BF, HB)
    if remote:
        outs["small"] = ((8, 128), F32, VM)
    else:
        outs.update(sums=((8, D), F32, VM), uplift_sum=((1, FF), F32, VM), intercept_sum=((1, 3 * D), F32, VM))
    scratch = {"w_" + k: buf(4, 8 * r, n) for k, (r, n) in W_SHAPES.items()}
    scratch.update({"g_" + k: buf(4, 8 * W_SHAPES[k][0], W_SHAPES[k][1]) for k in ("combiner", "expander", "reducer")})
    scratch.update(
        feats=buf(PAGE, D), cotangent=buf(PAGE, D), qkv=buf(PAGE, 3 * D),
        wide=buf(16, 96, D), low_t=buf(D, PAGE), mixture_back=buf(PAGE, D), two=buf(2 * PAGE, D, dtype=F32),
        sum_back=buf(PAGE, D, dtype=F32), r1=buf(PAGE, 128, dtype=F32), activated=buf(FF, PAGE), slope=buf(FF, PAGE),
        load=pltpu.SemaphoreType.DMA((7,)), keep=pltpu.SemaphoreType.DMA((2,)),
    )
    extra = {}
    if remote:
        scratch.update(
            held_reducer=buf(4, 4, 96, D), held_expander=buf(8, 4, 24, FF), held_projector=buf(8, 4, 24, 3 * D),
            held_small=buf(8, 4, 8, 128, dtype=F32), pack=buf(8, 128, dtype=F32), packs=buf(4, 64, 128, dtype=F32),
            vec=buf(8, D, dtype=F32), intercept=buf(1, 3 * D, dtype=F32), uplift=buf(1, FF, dtype=F32), sums=buf(8, D, dtype=F32),
            local=pltpu.SemaphoreType.DMA((6,)), send=pltpu.SemaphoreType.DMA((6, 10)), recv=pltpu.SemaphoreType.DMA((6, 11)),
            send2=pltpu.SemaphoreType.DMA((6, 10)), recv2=pltpu.SemaphoreType.DMA((6, 11)), ready=pltpu.SemaphoreType.REGULAR,
        )
        extra = dict(collective_id=0, has_side_effects=True)
    else:
        scratch["give"] = pltpu.SemaphoreType.DMA((5,))
    return call(functools.partial(layer_kernel, remote), ins, outs, scratch, "layer", **extra)


def finish_kernel(*refs):
    n = len(VECTORS)
    mats, small = refs[0:5], refs[5]
    for a, b in zip(mats, refs[6:11]):
        b[...] = a[...]
    for k, v in enumerate(VECTORS):
        refs[11 + k][...] = small[k : k + 1, 0 : COUNTS[v]].reshape(COUNTS[v])


def finish(mats, small):
    outs = [jax.ShapeDtypeStruct(m.shape, F32) for m in mats] + [jax.ShapeDtypeStruct((COUNTS[v],), F32) for v in VECTORS]
    got = pl.pallas_call(finish_kernel, out_shape=outs, in_specs=[VM] * 6, out_specs=[VM] * len(outs), name="finish")(*mats, small)
    return got[:5], dict(zip(VECTORS, got[5:]))


def whole_gather(v):
    return lax.all_gather(v, ("dp", "fsdp"), axis=0, tiled=True)


def whole_scatter(v):
    v = lax.psum_scatter(v.astype(F32), "dp", scatter_dimension=0, tiled=True)
    return lax.psum_scatter(v.astype(BF), "fsdp", scatter_dimension=0, tiled=True).astype(F32)


def cut(rows, sizes):
    parts = []
    at = 0
    for size in sizes:
        parts.append(rows[..., at : at + size])
        at += size
    return parts


def local(
    tokens, coordinates, lengths, cotangent, projector, intercept, relative, combiner, baseline,
    stretch, center, expander, uplift, reducer, offset, rescale, recenter, remote,
):
    vectors = dict(zip(VECTORS, (intercept, uplift, baseline, stretch, center, offset, rescale, recenter)))
    weights = dict(zip(ORDER[1:], (projector, relative, combiner, expander, reducer)))
    if remote:
        f = layer(tokens, coordinates, lengths, cotangent, weights, vectors, True)
        mats, small = finish([getattr(f, k) for k in ORDER[1:]], f.small)
        share = dict(zip(ORDER[1:], mats))
    else:
        sizes = [v.shape[0] for v in vectors.values()]
        rows = whole_gather(jnp.concatenate(list(vectors.values()))[None])
        wide = {k: v.reshape(1, -1).astype(F32) for k, v in zip(VECTORS, cut(rows, sizes))}
        table_rows = jnp.concatenate([wide[k] for k in VEC_ROWS] + [jnp.zeros((2, D), F32)])
        full = {k: whole_gather(m) for k, m in weights.items()}
        f = layer(
            tokens, coordinates, lengths, cotangent, full, {"vec": table_rows, "intercept": wide["intercept"], "uplift": wide["uplift"]}, False
        )
        share = {k: whole_scatter(getattr(f, k).reshape(-1, W_SHAPES[k][1])) for k in ORDER[1:]}
        sums = [f.intercept_sum[0], f.uplift_sum[0]] + [f.sums[k] for k in range(6)]
        stacked = jnp.concatenate([v.reshape(rows.shape[0], -1) for v in sums], axis=1)
        small = dict(zip(VECTORS, cut(whole_scatter(stacked)[0], sizes)))
    return (
        f.result, f.token_gradient, share["projector"], small["intercept"], share["relative"], share["combiner"], small["baseline"],
        small["stretch"], small["center"], share["expander"], small["uplift"], share["reducer"], small["offset"], small["rescale"],
        small["recenter"],
    )


def solution(mesh):
    rows, line = P(("dp", "fsdp"), None), P(("dp", "fsdp"))
    remote = (mesh.shape["dp"], mesh.shape["fsdp"]) == (NZ * NY, NX * NC)
    return jax.shard_map(
        functools.partial(local, remote=remote),
        mesh=mesh,
        in_specs=(rows, P(None, ("dp", "fsdp")), line, rows, rows, line, rows, rows, line, line, line, rows, line, rows, line, line, line),
        out_specs=(rows, rows, rows, line, rows, rows, line, line, line, rows, line, rows, line, line, line),
        check_vma=False,
    )
```

```python
import functools
import types

import jax
import jax.numpy as jnp
import numpy as np
from jax import lax
from jax.experimental import pallas as pl
from jax.experimental.pallas import tpu as pltpu
from jax.sharding import PartitionSpec as P

MESH = pl.DeviceIdType.MESH
NZ, NY, NX, NC = 4, 2, 2, 2


PAGE = 512
D = 768
FF = 3072
HALF = 384
PAIRS = 6
SCALE = 192.0 ** -0.5
EPSILON = 1e-12
NEGATIVE = -1e30
BF = jnp.bfloat16
F32 = jnp.float32
PIECE = 256
SUM_BASELINE, SUM_STRETCH, SUM_CENTER, SUM_OFFSET, SUM_RESCALE, SUM_RECENTER = range(6)
VM = pl.BlockSpec(memory_space=pltpu.VMEM)
HB = pl.BlockSpec(memory_space=pl.ANY)
SM = pl.BlockSpec(memory_space=pltpu.SMEM)
BIG = 63 << 20
W_SHAPES = {"projector": (24, 2304), "relative": (48, 768), "combiner": (24, 768), "expander": (24, 3072), "reducer": (96, 768)}
VECTORS = ("intercept", "uplift", "baseline", "stretch", "center", "offset", "rescale", "recenter")
ORDER = ("small", "projector", "relative", "combiner", "expander", "reducer")
COUNTS = {"intercept": 72, "uplift": 96, "baseline": 24, "stretch": 24, "center": 24, "offset": 24, "rescale": 24, "recenter": 24}
FREQUENCY = np.exp(-np.log(10000.0) * np.arange(192) / 192).astype(np.float32)[:, None]
VEC_ROWS = VECTORS[2:]


class Place:
    def __init__(self):
        d = lax.axis_index("dp")
        f = lax.axis_index("fsdp")
        self.z, self.y = d // NY, d % NY
        self.x, self.c = f // NC, f % NC
        z, y, x, c = self.z, self.y, self.x, self.c
        self.y1, self.x1 = y + (1 - c) * (1 - 2 * y), x + c * (1 - 2 * x)
        self.y2, self.x2 = y + c * (1 - 2 * y), x + (1 - c) * (1 - 2 * x)
        self.yd, self.xd = 1 - y, 1 - x
        self.first = (z * NY + self.y1, self.x1 * NC + c)
        self.second = (z * NY + self.y2, self.x2 * NC + c)
        self.sibling = (z * NY + y, x * NC + 1 - c)

    def along_z(self, z):
        return (z * NY + self.y, self.x * NC + self.c)

    def peers(self):
        return [self.first, self.second, self.sibling] + [self.along_z((self.z + s) % NZ) for s in (1, 2, 3)]


def enter(place):
    barrier = pltpu.get_barrier_semaphore()
    peers = place.peers()
    for peer in peers:
        pl.semaphore_signal(barrier, inc=1, device_id=peer, device_id_type=MESH)
    pl.semaphore_wait(barrier, len(peers))


def nn(a, b):
    return jnp.dot(a, b, preferred_element_type=F32)


def nt(a, b):
    return lax.dot_general(a, b, (((1,), (1,)), ((), ())), preferred_element_type=F32)


def span(i, size):
    return pl.ds(pl.multiple_of(i * size, size), size)


def own_lanes(e, rows):
    lane = lax.broadcasted_iota(jnp.int32, (rows, 128), 1)
    return lane < 64 if e == 0 else lane >= 64


def only(e, v):
    return jnp.where(own_lanes(e, v.shape[0]), v, jnp.zeros_like(v))


def only_rows(e, v):
    row = lax.broadcasted_iota(jnp.int32, v.shape, 0)
    return jnp.where(row < 64 if e == 0 else row >= 64, v, jnp.zeros_like(v))


def project(tokens, projector, intercept, qkv):
    @pl.loop(0, 9)
    def _(n):
        cols = span(n, PIECE)
        qkv[:, cols] = (nn(tokens[...], projector[:, cols]) + intercept[:, cols]).astype(BF)


def table(relative, side, half, cols):
    return relative[2 * side : 2 * side + 2, half * 192 : (half + 1) * 192, cols].reshape(HALF, 128)


def turn(weights_of, feats, out, at, rows):
    ws, wc = weights_of
    c = feats[rows, :HALF].astype(F32)
    s = feats[rows, HALF:].astype(F32)
    out[rows, at : at + HALF] = (ws * s + wc * c).astype(BF)
    out[rows, at + HALF : at + 2 * HALF] = (wc * s - ws * c).astype(BF)


def mean(v):
    return jnp.sum(v, axis=1, keepdims=True) * (1.0 / D)


def first_norm(tokens, mixture, combiner, vec, hold, n1, r1, low):
    @pl.loop(0, 3)
    def _(n):
        cols = span(n, PIECE)
        hold[:, cols] = nn(mixture[...], combiner[:, cols])

    @pl.loop(0, PAGE // 32)
    def _(i):
        rows = span(i, 32)
        v = tokens[rows, :].astype(F32) + hold[rows, :] + vec.baseline[...]
        v = v - mean(v)
        r = lax.rsqrt(mean(v * v) + EPSILON)
        v = v * r
        n1[rows, :] = v
        r1[rows, :] = jnp.broadcast_to(r, (32, 128))
        low[rows, :] = (v * vec.stretch[...] + vec.center[...]).astype(BF)


def second_norm(n1, cotangent, vec, hold, reduced_back, second_back, result, sums):
    zero = jnp.zeros((8, D), F32)

    def fold(v):
        return jnp.sum(v.reshape(4, 8, D), axis=0)

    def body(i, carry):
        rescale_sum, recenter_sum, offset_sum = carry
        rows = span(i, 32)
        v = (n1[rows, :] * vec.stretch[...] + vec.center[...]) + hold[rows, :] + vec.offset[...]
        v = v - mean(v)
        r = lax.rsqrt(mean(v * v) + EPSILON)
        v = v * r
        g = cotangent[rows, :].astype(F32)
        result[rows, :] = (v * vec.rescale[...] + vec.recenter[...]).astype(BF)
        u = g * vec.rescale[...]
        back = r * (u - mean(u) - v * mean(u * v))
        second_back[rows, :] = back
        low = back.astype(BF)
        reduced_back[rows, :] = low
        return (rescale_sum + fold(g * v), recenter_sum + fold(g), offset_sum + fold(low.astype(F32)))

    a, b, c = lax.fori_loop(0, PAGE // 32, body, (zero, zero, zero))
    for k, v in ((SUM_RESCALE, a), (SUM_RECENTER, b), (SUM_OFFSET, c)):
        sums[k : k + 1, :] = jnp.sum(v, axis=0, keepdims=True)


def first_back(total, n1, r1, vec, branch_back, sums):
    zero = jnp.zeros((8, D), F32)

    def fold(v):
        return jnp.sum(v.reshape(4, 8, D), axis=0)

    def body(i, carry):
        stretch_sum, center_sum, baseline_sum = carry
        rows = span(i, 32)
        b = total[rows, :]
        v = n1[rows, :]
        u = b * vec.stretch[...]
        back = r1[rows, :1] * (u - mean(u) - v * mean(u * v))
        total[rows, :] = back
        low = back.astype(BF)
        branch_back[rows, :] = low
        return (stretch_sum + fold(b * v), center_sum + fold(b), baseline_sum + fold(low.astype(F32)))

    a, b, c = lax.fori_loop(0, PAGE // 32, body, (zero, zero, zero))
    for k, v in ((SUM_STRETCH, a), (SUM_CENTER, b), (SUM_BASELINE, c)):
        sums[k : k + 1, :] = jnp.sum(v, axis=0, keepdims=True)


def branch_grads(mixture, branch_back, combiner, grad_combiner, mixture_back):
    @pl.loop(0, 3)
    def _(n):
        cols = span(n, PIECE)
        grad_combiner[cols, :] = nn(mixture[:, cols].T, branch_back[...]).astype(BF)
        mixture_back[:, cols] = nt(branch_back[...], combiner[cols, :]).astype(BF)


def back_setup(feats, top, bottom):
    for k in range(6):
        block = feats[:, k * 128 : (k + 1) * 128].T
        top[k * 128 : (k + 1) * 128, :] = block
        bottom[k * 128 : (k + 1) * 128, :] = block


def unturn(g, t, cols, out):
    @pl.loop(0, HALF // 64)
    def _(i):
        a = span(i, 64)
        b = pl.ds(pl.multiple_of(HALF + i * 64, 64), 64)
        c = t[a, :].astype(F32)
        s = t[b, :].astype(F32)
        g1 = g[a, :]
        g2 = g[b, :]
        out[a, :] = (g1 * s - g2 * c).astype(BF)
        out[b, :] = (g1 * c + g2 * s).astype(BF)


def flat(ref):
    return ref.reshape(ref.shape[0] * ref.shape[1], ref.shape[2])


def name_refs(groups, refs):
    out = []
    at = 0
    for g in groups:
        out.append(types.SimpleNamespace(**dict(zip(g, refs[at : at + len(g)]))))
        at += len(g)
    return out


def call(kernel, ins, outs, scratch, name, **params):
    names = (tuple(ins), tuple(outs), tuple(scratch))
    got = pl.pallas_call(
        functools.partial(kernel, names),
        out_shape=[jax.ShapeDtypeStruct(s, d) for s, d, _ in outs.values()],
        in_specs=[sp for _, sp in ins.values()],
        out_specs=[sp for _, _, sp in outs.values()],
        scratch_shapes=list(scratch.values()),
        compiler_params=pltpu.CompilerParams(vmem_limit_bytes=BIG, **params),
        name=name,
    )(*[a for a, _ in ins.values()])
    return types.SimpleNamespace(**dict(zip(outs, got)))


def buf(*shape, dtype=BF):
    return pltpu.VMEM(shape, dtype)


class Gather:
    def __init__(self, place, shards, full, local, send, recv):
        self.p, self.shards, self.full = place, shards, full
        self.local, self.send, self.recv = local, send, recv
        self.sent = []

    def remote(self, w, src, dst, s, r, device):
        return pltpu.make_async_remote_copy(
            src_ref=src, dst_ref=dst, send_sem=self.send.at[w, s], recv_sem=self.recv.at[w, r], device_id=device, device_id_type=MESH
        )

    def go(self, make):
        self.remote(*make()).start()
        self.sent.append(make)

    def arrived(self, w, ref, r):
        self.remote(w, ref, ref, 0, r, self.p.sibling).wait_recv()

    def begin(self):
        p = self.p
        for w in range(len(self.shards)):
            pltpu.make_async_copy(self.shards[w], self.own(w, p.z), self.local.at[w]).start()
            for s in (1, 2, 3):
                self.go(lambda w=w, s=s: (w, self.shards[w], self.own(w, p.z), s - 1, p.z, p.along_z((p.z + s) % NZ)))

    def rows(self, w, y, x, c):
        count = self.shards[w].shape[0]
        return pl.ds(pl.multiple_of(((y * NX + x) * NC + c) * count, 8), count)

    def own(self, w, z):
        p = self.p
        return self.full[w].at[z, self.rows(w, p.y, p.x, p.c)]

    def block(self, w, at):
        p = self.p
        y, x = {"own": (p.y, p.x), "first": (p.y1, p.x1), "second": (p.y2, p.x2), "across": (p.yd, p.xd)}[at]
        return self.full[w].at[:, self.rows(w, y, x, p.c)]

    def pass_on(self, w, at, *moves):
        for s, r, device in moves:
            self.go(lambda s=s, r=r, device=device: (w, self.block(w, at), self.block(w, at), s, r, device))

    def a(self, w):
        p = self.p
        pltpu.make_async_copy(self.shards[w], self.own(w, p.z), self.local.at[w]).wait()
        for s in (1, 2, 3):
            zs = (p.z + s) % NZ
            self.arrived(w, self.own(w, zs), zs)
        self.pass_on(w, "own", (3, 4, p.first), (4, 5, p.second), (5, 7, p.sibling))

    def b(self, w):
        p = self.p
        self.arrived(w, self.block(w, "first"), 4)
        self.pass_on(w, "first", (6, 6, p.second), (7, 8, p.sibling))

    def c(self, w):
        p = self.p
        self.arrived(w, self.block(w, "second"), 5)
        self.pass_on(w, "second", (8, 9, p.sibling))
        self.arrived(w, self.block(w, "across"), 6)
        self.pass_on(w, "across", (9, 10, p.sibling))

    def d(self, w):
        for r in range(7, 11):
            self.arrived(w, self.block(w, "own"), r)

    def end(self):
        for make in self.sent:
            self.remote(*make()).wait_send()


class Gather2(Gather):
    def shard(self, w, at, z):
        p = self.p
        y, x = {"own": (p.y, p.x), "first": (p.y1, p.x1), "second": (p.y2, p.x2), "across": (p.yd, p.xd)}[at]
        return self.full[w].at[z, self.rows(w, y, x, p.c)]

    def level(self, k):
        return (self.p.z + k) % NZ

    def spread(self, w, k, source=None):
        p = self.p
        for j, (r, device) in enumerate(((4, p.first), (8, p.second), (16, p.sibling))):

            def make(j=j, r=r, device=device):
                z = self.level(k)
                ref = self.shard(w, "own", z)
                return w, ref if source is None else source, ref, 3 + 3 * k + j, r + z, device

            self.go(make)

    def begin(self, early=None):
        p = self.p
        n = len(self.shards)
        for w in range(n):
            pltpu.make_async_copy(self.shards[w], self.own(w, p.z), self.local.at[w]).start()
            for s in (1, 2, 3):
                self.go(lambda w=w, s=s: (w, self.shards[w], self.own(w, p.z), s - 1, p.z, p.along_z((p.z + s) % NZ)))
            self.spread(w, 0, self.shards[w])

    def a(self, w):
        pltpu.make_async_copy(self.shards[w], self.own(w, self.p.z), self.local.at[w]).wait()
        for k in (1, 2, 3):
            self.arrived(w, self.shard(w, "own", self.level(k)), self.level(k))
            self.spread(w, k)

    def b(self, w):
        p = self.p
        for k in range(NZ):
            self.arrived(w, self.shard(w, "first", self.level(k)), 4 + self.level(k))
            for j, (r, device) in enumerate(((12, p.second), (20, p.sibling))):

                def make(k=k, j=j, r=r, device=device):
                    z = self.level(k)
                    ref = self.shard(w, "first", z)
                    return w, ref, ref, 15 + 2 * k + j, r + z, device

                self.go(make)

    def hand(self, w, at, slot, r, s):
        for k in range(NZ):
            self.arrived(w, self.shard(w, at, self.level(k)), r + self.level(k))

            def make(k=k):
                z = self.level(k)
                ref = self.shard(w, at, z)
                return w, ref, ref, s + k, slot + z, self.p.sibling

            self.go(make)

    def c(self, w):
        self.hand(w, "second", 24, 8, 23)

    def e(self, w):
        self.hand(w, "across", 28, 12, 27)

    def d(self, w):
        for r in range(16, 32):
            self.arrived(w, self.own(w, 0), r)


def ramp(start, width):
    col = lax.broadcasted_iota(jnp.int32, (32, D), 1) + start
    mine = jnp.floor((col.astype(F32) + 0.5) * (1.0 / width)).astype(jnp.int32) == lax.broadcasted_iota(jnp.int32, (32, D), 0)
    col = lax.broadcasted_iota(jnp.int32, (128, D), 1) + start
    rest = col - jnp.floor((col.astype(F32) + 0.5) * (1.0 / width)).astype(jnp.int32) * width
    pick = jnp.where(rest == lax.broadcasted_iota(jnp.int32, (128, D), 0), 1.0, 0.0).astype(BF)
    return mine, pick


def widen(packs, vec, wide):
    k = 0
    for name, ref in (("intercept", wide.intercept), ("uplift", wide.uplift)):
        rows = packs[pl.ds(k, 32, stride=8), :].astype(BF)
        for start in range(0, 32 * COUNTS[name], D):
            mine, pick = ramp(start, COUNTS[name])
            ref[:, start : start + D] = jnp.sum(jnp.where(mine, nn(rows, pick), 0.0), axis=0, keepdims=True)
        k += 1
    mine, pick = ramp(0, 24)
    for j in range(6):
        rows = packs[pl.ds(k + j, 32, stride=8), :].astype(BF)
        vec[j : j + 1, :] = jnp.sum(jnp.where(mine, nn(rows, pick), 0.0), axis=0, keepdims=True)


def narrow(sums, intercept_sum, uplift_sum, packs):
    def one(v, mine, pick):
        v = jnp.where(mine, v, 0.0)
        high = v.astype(BF)
        return nt(high, pick) + nt((v - high.astype(F32)).astype(BF), pick)

    for k, (name, ref) in enumerate((("intercept", intercept_sum), ("uplift", uplift_sum))):
        total = jnp.zeros((32, 128), F32)
        for start in range(0, 32 * COUNTS[name], D):
            total += one(ref[:, start : start + D], *ramp(start, COUNTS[name]))
        packs[pl.ds(k, 32, stride=8), :] = total
    mine, pick = ramp(0, 24)
    for j in range(6):
        packs[pl.ds(2 + j, 32, stride=8), :] = one(sums[j : j + 1, :], mine, pick)


def sinusoids(frequency, coordinates, feats_t, feats):
    for c in (0, 1):
        angles = frequency[...] * coordinates[c : c + 1, :].astype(F32)
        feats_t[c * 192 : (c + 1) * 192, :] = jnp.cos(angles).astype(BF)
        feats_t[HALF + c * 192 : HALF + (c + 1) * 192, :] = jnp.sin(angles).astype(BF)
    for k in range(6):
        feats[:, k * 128 : (k + 1) * 128] = feats_t[k * 128 : (k + 1) * 128, :].T


class Scatter:
    ROLES = ("own", "first", "second", "across")

    def __init__(self, place, counts, grads, blocks, outs, send, recv):
        self.p, self.counts, self.grads, self.blocks, self.outs = place, counts, grads, blocks, outs
        self.send, self.recv = send, recv
        self.sent = []

    def remote(self, w, src, dst, s, r, device):
        return pltpu.make_async_remote_copy(
            src_ref=src, dst_ref=dst, send_sem=self.send.at[w, s], recv_sem=self.recv.at[w, r], device_id=device, device_id_type=MESH
        )

    def go(self, make):
        self.remote(*make()).start()
        self.sent.append(make)

    def arrived(self, w, ref, r):
        self.remote(w, ref, ref, 0, r, self.p.sibling).wait_recv()

    def at(self, role):
        p = self.p
        return {"own": (p.y, p.x), "first": (p.y1, p.x1), "second": (p.y2, p.x2), "across": (p.yd, p.xd)}[role]

    def part(self, w, y, x, c):
        count = self.counts[w]
        return self.grads[w].at[:, pl.ds(pl.multiple_of(((y * NX + x) * NC + c) * count, 8), count)]

    def begin(self, w):
        theirs = {"own": "own", "first": "second", "second": "first", "across": "across"}
        for b in (3, 2, 1, 0):
            role = theirs[self.ROLES[b]]
            self.go(lambda b=b, role=role: (w, self.part(w, *self.at(role), 1 - self.p.c), self.blocks[w](b), b, b, self.p.sibling))

    def add(self, w, b, other):
        mine = self.blocks[w](b)

        @pl.loop(0, NZ)
        def _(k):
            mine[k] = (mine[k].astype(F32) + other[k].astype(F32)).astype(mine.dtype)

    def s(self, w):
        block = self.blocks[w]
        for b in (3, 2, 1, 0):
            self.arrived(w, block(b), b)
            self.add(w, b, self.part(w, *self.at(self.ROLES[b]), self.p.c))
            if b >= 2:
                self.go(lambda b=b: (w, block(b), block(7 - b), 7 - b, 7 - b, self.p.second))

    def x(self, w):
        block = self.blocks[w]
        self.arrived(w, block(4), 4)
        self.add(w, 1, block(4))
        self.go(lambda: (w, block(1), block(6), 6, 6, self.p.first))
        self.arrived(w, block(5), 5)
        self.add(w, 0, block(5))

    def f(self, w):
        p = self.p
        block = self.blocks[w]
        self.arrived(w, block(6), 6)
        self.add(w, 0, block(6))
        for s in (1, 2, 3):

            def make(s=s):
                zt = (p.z + s) % NZ
                return w, block(0).at[zt], block(7).at[p.z], 6 + s, 7 + p.z, p.along_z(zt)

            self.go(make)

    def z(self, w):
        p = self.p
        total = self.blocks[w](0)[p.z].astype(F32)
        for s in (1, 2, 3):
            zs = (p.z + s) % NZ
            self.arrived(w, self.blocks[w](7).at[zs], 7 + zs)
            total += self.blocks[w](7)[zs].astype(F32)
        self.outs[w](total)

    def end(self):
        for make in self.sent:
            self.remote(*make()).wait_send()


def pool_at(n):
    return pl.ds(pl.multiple_of((n >> 1) * 512, 512), 512), pl.ds(pl.multiple_of((n & 1) * PIECE, PIECE), PIECE)


def attend(p, qkv, relative, feats, live, left, right, slots, mixture):
    lanes = span(p, 128)
    q2 = qkv[:, lanes]
    k2 = qkv[:, span(p + PAIRS, 128)]
    v2 = qkv[:, span(p + 2 * PAIRS, 128)]
    every = slice(None)
    for e in (0, 1):
        q = only(e, q2)
        k = only(e, k2)
        turn((nt(q, table(relative, 0, 0, lanes)), nt(q, table(relative, 0, 1, lanes))), feats, left, 0, every)
        turn((nt(k, table(relative, 1, 0, lanes)), nt(k, table(relative, 1, 1, lanes))), feats, right, 0, every)
        scores = (nt(left[...], feats[...]) + nt(q, k2) + nt(feats[...], right[...])) * SCALE
        key = lax.broadcasted_iota(jnp.int32, scores.shape, 1)
        scores = jnp.where(key < live, scores, NEGATIVE)
        powers = jnp.exp(scores - jnp.max(scores, axis=1, keepdims=True))
        share = (powers / jnp.sum(powers, axis=1, keepdims=True)).astype(BF)
        slots[e][...] = share
        part = nn(share, only(e, v2))
        if e == 0:
            mixture[:, lanes] = part.astype(BF)
        else:
            mixture[:, lanes] = jnp.where(own_lanes(1, PAGE), part.astype(BF), mixture[:, lanes])


def feed_pool(low, expander, uplift, activated, slope):
    @pl.loop(0, FF // PIECE)
    def _(n):
        cols = span(n, PIECE)
        v = nn(low[...], expander[:, cols]) + uplift[:, cols]
        half = 0.5 * lax.erf(v * (0.5 ** 0.5)) + 0.5
        activated[pool_at(n)] = (v * half).astype(BF)
        slope[pool_at(n)] = (half + v * (jnp.exp(v * v * -0.5) * 0.3989422804014327)).astype(BF)


def reduce_pool(activated, reducer, hold):
    @pl.loop(0, 3)
    def _(n):
        cols = span(n, PIECE)
        total = nn(activated[0:512, :], reducer[0:512, cols])
        for j in range(1, 6):
            total += nn(activated[512 * j : 512 * (j + 1), :], reducer[512 * j : 512 * (j + 1), cols])
        hold[:, cols] = total


def reducer_gradient(activated, reduced_back, grad_reducer):
    @pl.loop(0, FF // PIECE)
    def _(n):
        grad_reducer[span(n, PIECE), :] = nn(activated[pool_at(n)].T, reduced_back[...]).astype(BF)


def expander_gradient(low_t, slope, reduced_back, reducer, expander, grad_expander, uplift_sum, total, hook):
    @pl.loop(0, FF // PIECE)
    def _(n):
        cols = span(n, PIECE)
        inner = (nt(reduced_back[...], reducer[cols, :]) * slope[pool_at(n)].astype(F32)).astype(BF)
        slope[pool_at(n)] = inner
        uplift_sum[:, cols] = jnp.sum(inner.astype(F32), axis=0, keepdims=True)
        grad_expander[:, cols] = nn(low_t[...], inner).astype(BF)
        hook(n)

    @pl.loop(0, 3)
    def _(n):
        cols = span(n, PIECE)
        part = nt(slope[0:512, :], expander[cols, 0:512])
        for j in range(1, 6):
            part += nt(slope[512 * j : 512 * (j + 1), :], expander[cols, 512 * j : 512 * (j + 1)])
        total[:, cols] += part


def attend_back(p, qkv, mixture_back, slots, ready, done, relative, top, bottom, score_back, two, turned, grad_relative, back_t):
    lanes = span(p, 128)
    q2 = qkv[:, lanes]
    k2 = qkv[:, span(p + PAIRS, 128)]
    v2 = qkv[:, span(p + 2 * PAIRS, 128)]
    m2 = mixture_back[:, lanes]
    qt, kt, mt = q2.T, k2.T, m2.T
    tables = [[table(relative, side, half, lanes).T for half in (0, 1)] for side in (0, 1)]
    query_t = jnp.zeros((128, PAGE), F32)
    key_t = jnp.zeros((128, PAGE), F32)
    value_t = jnp.zeros((128, PAGE), F32)
    lifted = two.at[0 : D + 128, 0:PAGE]

    def table_grad(e, side, t2):
        g = two.at[0:D, PAGE + 128 * side : PAGE + 128 * (side + 1)]
        if e == 0:
            g[...] = nn(turned[...], only(0, t2))
        else:
            for half in (0, 1):
                cut = slice(half * HALF, (half + 1) * HALF)
                block = (g[cut, :] + nn(turned[cut, :], only(1, t2))).astype(BF)
                grad_relative[2 * side : 2 * side + 2, half * 192 : (half + 1) * 192, lanes] = block.reshape(2, 192, 128)

    for e in (0, 1):
        me = only(e, m2)
        top[D:, :] = only_rows(e, kt)
        bottom[D:, :] = only_rows(e, qt)
        back = nt(me, v2)
        ready(e)
        share = slots[e][...].astype(F32)
        score_back[...] = (share * (back - jnp.sum(share * back, axis=1, keepdims=True)) * SCALE).astype(BF)
        value_t += nn(only_rows(e, mt), slots[e][...])
        done(e)
        lifted[...] = nt(top[...], score_back[...])
        query_t += lifted[D:, :]
        unturn(lifted, top, None, turned)
        table_grad(e, 0, q2)
        query_t += only_rows(e, nn(tables[0][0], turned[:HALF, :]) + nn(tables[0][1], turned[HALF:, :]))
        lifted[...] = nn(bottom[...], score_back[...])
        key_t += lifted[D:, :]
        unturn(lifted, top, None, turned)
        table_grad(e, 1, k2)
        key_t += only_rows(e, nn(tables[1][0], turned[:HALF, :]) + nn(tables[1][1], turned[HALF:, :]))
    back_t[lanes, :] = query_t.astype(BF)
    back_t[span(p + PAIRS, 128), :] = key_t.astype(BF)
    back_t[span(p + 2 * PAIRS, 128), :] = value_t.astype(BF)


def projector_gradient(j, tokens_t, back_t, grad_projector, intercept_sum):
    @pl.loop(0, 3)
    def _(k):
        cols = pl.ds(pl.multiple_of(k * D + j * PIECE, PIECE), PIECE)
        b = back_t[cols, :]
        intercept_sum[:, cols] = nt(jnp.ones((8, PAGE), BF), b)[0:1, :]
        grad_projector[:, :, span(3 * j + k, PIECE)] = nt(tokens_t[...], b).astype(BF).reshape(4, 192, PIECE)


def token_gradient(projector, back_t, sum_back, out):
    @pl.loop(0, 3)
    def _(n):
        cols = span(n, PIECE)
        out[:, cols] = (sum_back[:, cols] + nn(projector[cols, :], back_t[...]).T).astype(BF)


def transposed(src, dst):
    for k in range(6):
        dst[k * 128 : (k + 1) * 128, :] = src[:, k * 128 : (k + 1) * 128].T


def layer_kernel(remote, names, *refs):
    i, o, s = name_refs(names, refs)
    full = [getattr(s, "w_" + w) for w in ORDER[1:]]
    shards = [getattr(i, w) for w in ORDER[1:]]
    take_tokens = pltpu.make_async_copy(i.tokens, s.mixture_back, s.load.at[0])
    take_cotangent = pltpu.make_async_copy(i.cotangent, s.cotangent, s.load.at[1])
    take_tokens.start()
    if remote:
        p = Place()
        enter(p)
        s.pack[...] = jnp.zeros((8, 128), F32)
        for k, v in enumerate(VECTORS):
            n = COUNTS[v]
            s.pack[k : k + 1, 0:n] = getattr(i, v)[...].astype(F32).reshape(1, n)
        g = Gather2(p, [s.pack] + shards, [s.packs] + full, s.local, s.send, s.recv)
        g.begin()
        vec_ref, intercept, uplift = s.vec, s.intercept, s.uplift
    else:
        takes = [pltpu.make_async_copy(a, flat(b), s.load.at[2 + k]) for k, (a, b) in enumerate(zip(shards, full))]
        for t in takes:
            t.start()
        vec_ref, intercept, uplift = i.vec, i.intercept, i.uplift
    w = types.SimpleNamespace(**{n: flat(ref) for n, ref in zip(ORDER[1:], full)})
    vec = types.SimpleNamespace(**{v: vec_ref.at[k : k + 1] for k, v in enumerate(VEC_ROWS)})
    live = i.lengths[0]
    wide = flat(s.wide)
    low, mixture, reduced_back = (wide.at[k * PAGE : (k + 1) * PAGE] for k in range(3))
    n1, hold = s.two.at[0:PAGE], s.two.at[PAGE : 2 * PAGE]
    left, right = flat(s.g_reducer).at[0:PAGE], flat(s.g_reducer).at[PAGE : 2 * PAGE]
    activated, slope = s.activated, s.slope

    sinusoids(i.frequency, i.coordinates, s.low_t, s.feats)
    if remote:
        g.a(0)
        g.a(1); g.b(0)
        g.a(2); g.b(1); g.c(0); g.e(0)
        g.a(3); g.b(2); g.c(1); g.e(1); g.d(0)
        widen(s.packs.reshape(256, 128), s.vec, types.SimpleNamespace(intercept=s.intercept, uplift=s.uplift))
        g.a(4); g.b(3); g.c(2); g.e(2); g.d(1)
        early = {0: [(g.c, 4)], 1: [(g.d, 3)], 2: [(g.b, 5)], 3: [(g.e, 4)], 4: [(g.c, 5)]}
    else:
        for t in takes:
            t.wait()
        early = {}
    take_tokens.wait()
    project(s.mixture_back, w.projector, intercept, s.qkv)
    if remote:
        g.a(5); g.b(4); g.c(3); g.e(3); g.d(2)

    slots = [s.low_t.at[0:PAGE], s.cotangent.at[:, 0:PAGE]]

    def keep(q, e):
        return pltpu.make_async_copy(slots[e], o.probs.at[2 * q + e], s.keep.at[e])

    def fetch(q, e):
        return pltpu.make_async_copy(o.probs.at[2 * q + e], slots[e], s.keep.at[e])

    def hooks(q, table_of):
        for k, steps in table_of.items():

            @pl.when(q == k)
            def _(steps=steps):
                run(steps)

    @pl.loop(0, PAIRS)
    def _(q):
        @pl.when(q >= 1)
        def _():
            keep(q - 1, 0).wait()
            keep(q - 1, 1).wait()

        attend(q, s.qkv, s.w_relative, s.feats, live, left, right, slots, mixture)
        keep(q, 0).start()
        keep(q, 1).start()
        hooks(q, early)

    keep(PAIRS - 1, 0).wait()
    keep(PAIRS - 1, 1).wait()
    take_cotangent.start()

    first_norm(s.mixture_back, mixture, w.combiner, vec, hold, n1, s.r1, low)
    if remote:
        g.e(5)
        g.d(4)
    feed_pool(low, w.expander, uplift, activated, slope)
    transposed(low, s.low_t)
    if remote:
        g.d(5)
    take_cotangent.wait()
    reduce_pool(activated, w.reducer, hold)
    second_norm(n1, s.cotangent, vec, hold, reduced_back, s.sum_back, s.cotangent, o.sums if not remote else s.sums)
    give_result = pltpu.make_async_copy(s.cotangent, o.result, s.load.at[1])
    give_result.start()
    sums, uplift_sum, intercept_sum = (s.sums, s.uplift, s.intercept) if remote else (o.sums, o.uplift_sum, o.intercept_sum)
    reducer_gradient(activated, reduced_back, flat(s.g_reducer))
    grad_relative = s.w_reducer.at[:, 0:HALF]
    grad_projector = s.w_expander.at[:, :, 0 : 3 * D]
    if remote:
        g.end()

        def whole(ref):
            def put(v):
                ref[...] = v

            return put

        def relative_part(j):
            def put(v):
                o.relative[:, j * PIECE : (j + 1) * PIECE] = v

            return put

        def projector_part(j):
            def put(v):
                for k in range(3):
                    o.projector[:, k * D + j * PIECE : k * D + (j + 1) * PIECE] = v[:, k * PIECE : (k + 1) * PIECE]

            return put

        counts = [96, 24, 24]
        grads = [s.g_reducer, s.g_expander, s.g_combiner]
        blocks = [
            lambda b: s.held_reducer.at[b],
            lambda b: s.held_expander.at[b],
            lambda b: s.w_expander.at[:, 24 * b : 24 * b + 24, 3 * D :],
        ]
        outs = [whole(o.reducer), whole(o.expander), whole(o.combiner)]
        for j in range(3):
            lanes = slice(j * PIECE, (j + 1) * PIECE)
            counts += [48, 24]
            grads += [s.w_reducer.at[:, 0:HALF, lanes], s.w_expander.at[:, :, j * D : (j + 1) * D]]
            blocks.append(lambda b, lanes=lanes: s.w_reducer.at[:, HALF + 48 * b : HALF + 48 * b + 48, lanes])
            if j < 2:
                blocks.append(lambda b, j=j: s.wide.at[:, 192 * j + 24 * b : 192 * j + 24 * b + 24])
            else:
                blocks.append(lambda b: s.w_combiner.at[:, 24 * b : 24 * b + 24])
            outs += [relative_part(j), projector_part(j)]
        counts.append(8)
        grads.append(s.packs)
        blocks.append(lambda b: s.held_small.at[b])
        outs.append(whole(o.small))
        t = Scatter(p, counts, grads, blocks, outs, s.send2, s.recv2)
        t.begin(0)
    else:
        gives = [
            pltpu.make_async_copy(a, b, s.give.at[k])
            for k, (a, b) in enumerate(
                zip(
                    [s.g_reducer, s.g_expander, s.g_combiner, grad_relative, grad_projector],
                    [o.reducer, o.expander, o.combiner, o.relative, o.projector],
                )
            )
        ]
        gives[0].start()

    def middle(n):
        if remote:
            hooks(n, middle_plan(t))

    expander_gradient(s.low_t, slope, reduced_back, w.reducer, w.expander, flat(s.g_expander), uplift_sum, s.sum_back, middle)
    if remote:
        t.begin(1)
    else:
        gives[1].start()
    first_back(s.sum_back, n1, s.r1, vec, reduced_back, sums)
    branch_grads(mixture, reduced_back, w.combiner, flat(s.g_combiner), s.mixture_back)
    fetch(0, 0).start()
    give_result.wait()
    fetch(0, 1).start()
    if remote:
        for peer in p.peers():
            pl.semaphore_signal(s.ready, inc=1, device_id=peer, device_id_type=MESH)
        pl.semaphore_wait(s.ready, 6)
        t.begin(2)
    else:
        gives[2].start()
    top, bottom = activated.at[0:896], activated.at[896:1792]
    turned, score_back = activated.at[1792:2560], activated.at[2560:3072]
    tokens_t, back_t = slope.at[0:D], slope.at[D:]
    back_setup(s.feats, top, bottom)
    again = pltpu.make_async_copy(i.tokens, s.feats, s.load.at[0])
    again.start()
    again.wait()
    transposed(s.feats, tokens_t)
    if remote:
        run(before_plan(t))

    def project_part(j):
        projector_gradient(j, tokens_t, back_t, grad_projector, intercept_sum)

    late = {1: [(project_part, 0)], 3: [(project_part, 1)], 5: [(project_part, 2)]}
    if remote:
        for q, steps in late_plan(t).items():
            late[q] = late.get(q, []) + steps

    @pl.loop(0, PAIRS)
    def _(q):
        def done(e):
            @pl.when(q + 1 < PAIRS)
            def _():
                fetch(q + 1, e).start()

        attend_back(
            q, s.qkv, s.mixture_back, slots, lambda e: fetch(q, e).wait(), done, s.w_relative, top, bottom, score_back, s.two, turned, grad_relative, back_t
        )
        hooks(q, late)

    if remote:
        narrow(s.sums, intercept_sum, uplift_sum, s.packs.reshape(256, 128))
        t.begin(9)
    else:
        gives[3].start()
        gives[4].start()
    token_gradient(w.projector, back_t, s.sum_back, s.feats)
    give_tokens = pltpu.make_async_copy(s.feats, o.token_gradient, s.load.at[0])
    give_tokens.start()
    if remote:
        run(after_plan(t))
        t.end()
    else:
        for c in gives:
            c.wait()
    give_tokens.wait()


def middle_plan(t):
    return {8: [(t.s, 0)]}


def before_plan(t):
    return [(t.s, 1)]


def late_plan(t):
    return {
        0: [(t.x, 0), (t.s, 2)],
        1: [(t.begin, 3), (t.begin, 4), (t.f, 0)],
        2: [(t.x, 1), (t.s, 3), (t.s, 4)],
        3: [(t.begin, 5), (t.begin, 6), (t.f, 1), (t.x, 2), (t.z, 0)],
        4: [(t.x, 3), (t.x, 4), (t.s, 5), (t.s, 6), (t.f, 2)],
        5: [(t.begin, 7), (t.begin, 8), (t.f, 3), (t.f, 4), (t.x, 5), (t.x, 6), (t.z, 1), (t.z, 2)],
    }


def after_plan(t):
    return (
        [(t.s, 7), (t.s, 8), (t.s, 9), (t.f, 5), (t.f, 6), (t.x, 7), (t.x, 8), (t.x, 9), (t.z, 3), (t.z, 4), (t.z, 5), (t.z, 6)]
        + [(t.f, 7), (t.f, 8), (t.f, 9), (t.z, 7), (t.z, 8), (t.z, 9)]
    )


def run(steps):
    for step, w in steps:
        step(w)


def layer(tokens, coordinates, lengths, cotangent, weights, vectors, remote):
    ins = {"tokens": (tokens, HB), "coordinates": (coordinates, VM), "lengths": (lengths, SM), "cotangent": (cotangent, HB)}
    ins["frequency"] = (jnp.asarray(FREQUENCY), VM)
    ins.update({k: (weights[k], HB) for k in ORDER[1:]})
    ins.update({k: (v, VM) for k, v in vectors.items()})
    outs = {"result": ((PAGE, D), BF, HB), "token_gradient": ((PAGE, D), BF, HB), "probs": ((2 * PAIRS, PAGE, PAGE), BF, HB)}
    for k in ORDER[1:]:
        r, n = W_SHAPES[k]
        outs[k] = ((r, n), F32, VM) if remote else ((4, 8 * r, n), BF, HB)
    if remote:
        outs["small"] = ((8, 128), F32, VM)
    else:
        outs.update(sums=((8, D), F32, VM), uplift_sum=((1, FF), F32, VM), intercept_sum=((1, 3 * D), F32, VM))
    scratch = {"w_" + k: buf(4, 8 * r, n) for k, (r, n) in W_SHAPES.items()}
    scratch.update({"g_" + k: buf(4, 8 * W_SHAPES[k][0], W_SHAPES[k][1]) for k in ("combiner", "expander", "reducer")})
    scratch.update(
        feats=buf(PAGE, D), cotangent=buf(PAGE, D), qkv=buf(PAGE, 3 * D),
        wide=buf(4, HALF, D), low_t=buf(D, PAGE), mixture_back=buf(PAGE, D), two=buf(2 * PAGE, D, dtype=F32),
        sum_back=buf(PAGE, D, dtype=F32), r1=buf(PAGE, 128, dtype=F32), activated=buf(FF, PAGE), slope=buf(FF, PAGE),
        load=pltpu.SemaphoreType.DMA((7,)), keep=pltpu.SemaphoreType.DMA((2,)),
    )
    extra = {}
    if remote:
        scratch.update(
            held_reducer=buf(8, 4, 96, D), held_expander=buf(8, 4, 24, FF),
            held_small=buf(8, 4, 8, 128, dtype=F32), pack=buf(8, 128, dtype=F32), packs=buf(4, 64, 128, dtype=F32),
            vec=buf(8, D, dtype=F32), intercept=buf(1, 3 * D, dtype=F32), uplift=buf(1, FF, dtype=F32), sums=buf(8, D, dtype=F32),
            local=pltpu.SemaphoreType.DMA((6,)), send=pltpu.SemaphoreType.DMA((6, 31)), recv=pltpu.SemaphoreType.DMA((6, 32)),
            send2=pltpu.SemaphoreType.DMA((10, 10)), recv2=pltpu.SemaphoreType.DMA((10, 11)), ready=pltpu.SemaphoreType.REGULAR,
        )
        extra = dict(collective_id=0, has_side_effects=True)
    else:
        scratch["give"] = pltpu.SemaphoreType.DMA((5,))
    return call(functools.partial(layer_kernel, remote), ins, outs, scratch, "layer", **extra)


def finish_kernel(*refs):
    n = len(VECTORS)
    mats, small = refs[0:5], refs[5]
    for a, b in zip(mats, refs[6:11]):
        b[...] = a[...]
    for k, v in enumerate(VECTORS):
        refs[11 + k][...] = small[k : k + 1, 0 : COUNTS[v]].reshape(COUNTS[v])


def finish(mats, small):
    outs = [jax.ShapeDtypeStruct(m.shape, F32) for m in mats] + [jax.ShapeDtypeStruct((COUNTS[v],), F32) for v in VECTORS]
    got = pl.pallas_call(finish_kernel, out_shape=outs, in_specs=[VM] * 6, out_specs=[VM] * len(outs), name="finish")(*mats, small)
    return got[:5], dict(zip(VECTORS, got[5:]))


def whole_gather(v):
    return lax.all_gather(v, ("dp", "fsdp"), axis=0, tiled=True)


def whole_scatter(v):
    v = lax.psum_scatter(v.astype(F32), "dp", scatter_dimension=0, tiled=True)
    return lax.psum_scatter(v.astype(BF), "fsdp", scatter_dimension=0, tiled=True).astype(F32)


def cut(rows, sizes):
    parts = []
    at = 0
    for size in sizes:
        parts.append(rows[..., at : at + size])
        at += size
    return parts


def local(
    tokens, coordinates, lengths, cotangent, projector, intercept, relative, combiner, baseline,
    stretch, center, expander, uplift, reducer, offset, rescale, recenter, remote,
):
    vectors = dict(zip(VECTORS, (intercept, uplift, baseline, stretch, center, offset, rescale, recenter)))
    weights = dict(zip(ORDER[1:], (projector, relative, combiner, expander, reducer)))
    if remote:
        f = layer(tokens, coordinates, lengths, cotangent, weights, vectors, True)
        mats, small = finish([getattr(f, k) for k in ORDER[1:]], f.small)
        share = dict(zip(ORDER[1:], mats))
    else:
        sizes = [v.shape[0] for v in vectors.values()]
        rows = whole_gather(jnp.concatenate(list(vectors.values()))[None])
        wide = {k: v.reshape(1, -1).astype(F32) for k, v in zip(VECTORS, cut(rows, sizes))}
        table_rows = jnp.concatenate([wide[k] for k in VEC_ROWS] + [jnp.zeros((2, D), F32)])
        full = {k: whole_gather(m) for k, m in weights.items()}
        f = layer(
            tokens, coordinates, lengths, cotangent, full, {"vec": table_rows, "intercept": wide["intercept"], "uplift": wide["uplift"]}, False
        )
        change = {k: getattr(f, k).reshape(-1, W_SHAPES[k][1]) for k in ORDER[1:]}
        change["projector"] = change["projector"].reshape(D, 3, 3, PIECE).transpose(0, 2, 1, 3).reshape(D, 3 * D)
        share = {k: whole_scatter(v) for k, v in change.items()}
        sums = [f.intercept_sum[0], f.uplift_sum[0]] + [f.sums[k] for k in range(6)]
        stacked = jnp.concatenate([v.reshape(rows.shape[0], -1) for v in sums], axis=1)
        small = dict(zip(VECTORS, cut(whole_scatter(stacked)[0], sizes)))
    return (
        f.result, f.token_gradient, share["projector"], small["intercept"], share["relative"], share["combiner"], small["baseline"],
        small["stretch"], small["center"], share["expander"], small["uplift"], share["reducer"], small["offset"], small["rescale"],
        small["recenter"],
    )


def solution(mesh):
    rows, line = P(("dp", "fsdp"), None), P(("dp", "fsdp"))
    remote = (mesh.shape["dp"], mesh.shape["fsdp"]) == (NZ * NY, NX * NC)
    return jax.shard_map(
        functools.partial(local, remote=remote),
        mesh=mesh,
        in_specs=(rows, P(None, ("dp", "fsdp")), line, rows, rows, line, rows, rows, line, line, line, rows, line, rows, line, line, line),
        out_specs=(rows, rows, rows, line, rows, rows, line, line, line, rows, line, rows, line, line, line),
        check_vma=False,
    )
```

```python
import functools
import types

import jax
import jax.numpy as jnp
import numpy as np
from jax import lax
from jax.experimental import pallas as pl
from jax.experimental.pallas import tpu as pltpu
from jax.sharding import PartitionSpec as P

MESH = pl.DeviceIdType.MESH
NZ, NY, NX, NC = 4, 2, 2, 2


PAGE = 512
D = 768
FF = 3072
HALF = 384
PAIRS = 6
SCALE = 192.0 ** -0.5
EPSILON = 1e-12
NEGATIVE = -1e30
BF = jnp.bfloat16
F32 = jnp.float32
PIECE = 256
TALL = 128
SUM_BASELINE, SUM_STRETCH, SUM_CENTER, SUM_OFFSET, SUM_RESCALE, SUM_RECENTER = range(6)
VM = pl.BlockSpec(memory_space=pltpu.VMEM)
HB = pl.BlockSpec(memory_space=pl.ANY)
SM = pl.BlockSpec(memory_space=pltpu.SMEM)
BIG = 63 << 20
W_SHAPES = {"projector": (24, 2304), "relative": (48, 768), "combiner": (24, 768), "expander": (24, 3072), "reducer": (96, 768)}
VECTORS = ("intercept", "uplift", "baseline", "stretch", "center", "offset", "rescale", "recenter")
ORDER = ("small", "projector", "relative", "combiner", "expander", "reducer")
COUNTS = {"intercept": 72, "uplift": 96, "baseline": 24, "stretch": 24, "center": 24, "offset": 24, "rescale": 24, "recenter": 24}
FREQUENCY = np.exp(-np.log(10000.0) * np.arange(192) / 192).astype(np.float32)[:, None]
VEC_ROWS = VECTORS[2:]


class Place:
    def __init__(self):
        d = lax.axis_index("dp")
        f = lax.axis_index("fsdp")
        self.z, self.y = d // NY, d % NY
        self.x, self.c = f // NC, f % NC
        z, y, x, c = self.z, self.y, self.x, self.c
        self.y1, self.x1 = y + (1 - c) * (1 - 2 * y), x + c * (1 - 2 * x)
        self.y2, self.x2 = y + c * (1 - 2 * y), x + (1 - c) * (1 - 2 * x)
        self.yd, self.xd = 1 - y, 1 - x
        self.first = (z * NY + self.y1, self.x1 * NC + c)
        self.second = (z * NY + self.y2, self.x2 * NC + c)
        self.sibling = (z * NY + y, x * NC + 1 - c)

    def along_z(self, z):
        return (z * NY + self.y, self.x * NC + self.c)

    def peers(self):
        return [self.first, self.second, self.sibling] + [self.along_z((self.z + s) % NZ) for s in (1, 2, 3)]


def enter(place):
    barrier = pltpu.get_barrier_semaphore()
    peers = place.peers()
    for peer in peers:
        pl.semaphore_signal(barrier, inc=1, device_id=peer, device_id_type=MESH)
    pl.semaphore_wait(barrier, len(peers))


def nn(a, b):
    return jnp.dot(a, b, preferred_element_type=F32)


def nt(a, b):
    return lax.dot_general(a, b, (((1,), (1,)), ((), ())), preferred_element_type=F32)


def span(i, size):
    return pl.ds(pl.multiple_of(i * size, size), size)


def own_lanes(e, rows):
    lane = lax.broadcasted_iota(jnp.int32, (rows, 128), 1)
    return lane < 64 if e == 0 else lane >= 64


def only(e, v):
    return jnp.where(own_lanes(e, v.shape[0]), v, jnp.zeros_like(v))


def only_rows(e, v):
    row = lax.broadcasted_iota(jnp.int32, v.shape, 0)
    return jnp.where(row < 64 if e == 0 else row >= 64, v, jnp.zeros_like(v))


def project(tokens, projector, intercept, qkv):
    @pl.loop(0, 9)
    def _(n):
        cols = span(n, PIECE)
        qkv[:, cols] = (nn(tokens[...], projector[:, cols]) + intercept[:, cols]).astype(BF)


def table(relative, side, half, cols):
    return relative[2 * side : 2 * side + 2, half * 192 : (half + 1) * 192, cols].reshape(HALF, 128)


def turn(weights_of, feats, out, at, rows):
    ws, wc = weights_of
    c = feats[rows, :HALF].astype(F32)
    s = feats[rows, HALF:].astype(F32)
    out[rows, at : at + HALF] = (ws * s + wc * c).astype(BF)
    out[rows, at + HALF : at + 2 * HALF] = (wc * s - ws * c).astype(BF)


def mean(v):
    return jnp.sum(v, axis=1, keepdims=True) * (1.0 / D)


def first_norm(tokens, mixture, combiner, vec, hold, n1, r1, low):
    @pl.loop(0, 3)
    def _(n):
        cols = span(n, PIECE)
        hold[:, cols] = nn(mixture[...], combiner[:, cols])

    @pl.loop(0, PAGE // TALL)
    def _(i):
        rows = span(i, TALL)
        v = tokens[rows, :].astype(F32) + hold[rows, :] + vec.baseline[...]
        v = v - mean(v)
        r = lax.rsqrt(mean(v * v) + EPSILON)
        v = v * r
        n1[rows, :] = v
        r1[rows, :] = jnp.broadcast_to(r, (TALL, 128))
        low[rows, :] = (v * vec.stretch[...] + vec.center[...]).astype(BF)


def second_norm(n1, cotangent, vec, hold, reduced_back, second_back, result, sums):
    zero = jnp.zeros((8, D), F32)

    def fold(v):
        return jnp.sum(v.reshape(TALL // 8, 8, D), axis=0)

    def body(i, carry):
        rescale_sum, recenter_sum, offset_sum = carry
        rows = span(i, TALL)
        v = (n1[rows, :] * vec.stretch[...] + vec.center[...]) + hold[rows, :] + vec.offset[...]
        v = v - mean(v)
        r = lax.rsqrt(mean(v * v) + EPSILON)
        v = v * r
        g = cotangent[rows, :].astype(F32)
        result[rows, :] = (v * vec.rescale[...] + vec.recenter[...]).astype(BF)
        u = g * vec.rescale[...]
        back = r * (u - mean(u) - v * mean(u * v))
        second_back[rows, :] = back
        low = back.astype(BF)
        reduced_back[rows, :] = low
        return (rescale_sum + fold(g * v), recenter_sum + fold(g), offset_sum + fold(low.astype(F32)))

    a, b, c = lax.fori_loop(0, PAGE // TALL, body, (zero, zero, zero))
    for k, v in ((SUM_RESCALE, a), (SUM_RECENTER, b), (SUM_OFFSET, c)):
        sums[k : k + 1, :] = jnp.sum(v, axis=0, keepdims=True)


def first_back(total, n1, r1, vec, branch_back, sums):
    zero = jnp.zeros((8, D), F32)

    def fold(v):
        return jnp.sum(v.reshape(TALL // 8, 8, D), axis=0)

    def body(i, carry):
        stretch_sum, center_sum, baseline_sum = carry
        rows = span(i, TALL)
        b = total[rows, :]
        v = n1[rows, :]
        u = b * vec.stretch[...]
        back = r1[rows, :1] * (u - mean(u) - v * mean(u * v))
        total[rows, :] = back
        low = back.astype(BF)
        branch_back[rows, :] = low
        return (stretch_sum + fold(b * v), center_sum + fold(b), baseline_sum + fold(low.astype(F32)))

    a, b, c = lax.fori_loop(0, PAGE // TALL, body, (zero, zero, zero))
    for k, v in ((SUM_STRETCH, a), (SUM_CENTER, b), (SUM_BASELINE, c)):
        sums[k : k + 1, :] = jnp.sum(v, axis=0, keepdims=True)


def branch_grads(mixture, branch_back, combiner, grad_combiner, mixture_back):
    @pl.loop(0, 3)
    def _(n):
        cols = span(n, PIECE)
        grad_combiner[cols, :] = nn(mixture[:, cols].T, branch_back[...]).astype(BF)
        mixture_back[:, cols] = nt(branch_back[...], combiner[cols, :]).astype(BF)


def flat(ref):
    return ref.reshape(ref.shape[0] * ref.shape[1], ref.shape[2])


def name_refs(groups, refs):
    out = []
    at = 0
    for g in groups:
        out.append(types.SimpleNamespace(**dict(zip(g, refs[at : at + len(g)]))))
        at += len(g)
    return out


def call(kernel, ins, outs, scratch, name, **params):
    names = (tuple(ins), tuple(outs), tuple(scratch))
    got = pl.pallas_call(
        functools.partial(kernel, names),
        out_shape=[jax.ShapeDtypeStruct(s, d) for s, d, _ in outs.values()],
        in_specs=[sp for _, sp in ins.values()],
        out_specs=[sp for _, _, sp in outs.values()],
        scratch_shapes=list(scratch.values()),
        compiler_params=pltpu.CompilerParams(vmem_limit_bytes=BIG, **params),
        name=name,
    )(*[a for a, _ in ins.values()])
    return types.SimpleNamespace(**dict(zip(outs, got)))


def buf(*shape, dtype=BF):
    return pltpu.VMEM(shape, dtype)


class Gather:
    def __init__(self, place, shards, full, local, send, recv):
        self.p, self.shards, self.full = place, shards, full
        self.local, self.send, self.recv = local, send, recv
        self.sent = []

    def remote(self, w, src, dst, s, r, device):
        return pltpu.make_async_remote_copy(
            src_ref=src, dst_ref=dst, send_sem=self.send.at[w, s], recv_sem=self.recv.at[w, r], device_id=device, device_id_type=MESH
        )

    def go(self, make):
        self.remote(*make()).start()
        self.sent.append(make)

    def arrived(self, w, ref, r):
        self.remote(w, ref, ref, 0, r, self.p.sibling).wait_recv()

    def begin(self):
        p = self.p
        for w in range(len(self.shards)):
            pltpu.make_async_copy(self.shards[w], self.own(w, p.z), self.local.at[w]).start()
            for s in (1, 2, 3):
                self.go(lambda w=w, s=s: (w, self.shards[w], self.own(w, p.z), s - 1, p.z, p.along_z((p.z + s) % NZ)))

    def rows(self, w, y, x, c):
        count = self.shards[w].shape[0]
        return pl.ds(pl.multiple_of(((y * NX + x) * NC + c) * count, 8), count)

    def own(self, w, z):
        p = self.p
        return self.full[w].at[z, self.rows(w, p.y, p.x, p.c)]

    def block(self, w, at):
        p = self.p
        y, x = {"own": (p.y, p.x), "first": (p.y1, p.x1), "second": (p.y2, p.x2), "across": (p.yd, p.xd)}[at]
        return self.full[w].at[:, self.rows(w, y, x, p.c)]

    def pass_on(self, w, at, *moves):
        for s, r, device in moves:
            self.go(lambda s=s, r=r, device=device: (w, self.block(w, at), self.block(w, at), s, r, device))

    def a(self, w):
        p = self.p
        pltpu.make_async_copy(self.shards[w], self.own(w, p.z), self.local.at[w]).wait()
        for s in (1, 2, 3):
            zs = (p.z + s) % NZ
            self.arrived(w, self.own(w, zs), zs)
        self.pass_on(w, "own", (3, 4, p.first), (4, 5, p.second), (5, 7, p.sibling))

    def b(self, w):
        p = self.p
        self.arrived(w, self.block(w, "first"), 4)
        self.pass_on(w, "first", (6, 6, p.second), (7, 8, p.sibling))

    def c(self, w):
        p = self.p
        self.arrived(w, self.block(w, "second"), 5)
        self.pass_on(w, "second", (8, 9, p.sibling))
        self.arrived(w, self.block(w, "across"), 6)
        self.pass_on(w, "across", (9, 10, p.sibling))

    def d(self, w):
        for r in range(7, 11):
            self.arrived(w, self.block(w, "own"), r)

    def end(self):
        for make in self.sent:
            self.remote(*make()).wait_send()


class Gather2(Gather):
    def shard(self, w, at, z):
        p = self.p
        y, x = {"own": (p.y, p.x), "first": (p.y1, p.x1), "second": (p.y2, p.x2), "across": (p.yd, p.xd)}[at]
        return self.full[w].at[z, self.rows(w, y, x, p.c)]

    def level(self, k):
        return (self.p.z + k) % NZ

    def spread(self, w, k, source=None):
        p = self.p
        for j, (r, device) in enumerate(((4, p.first), (8, p.second), (16, p.sibling))):

            def make(j=j, r=r, device=device):
                z = self.level(k)
                ref = self.shard(w, "own", z)
                return w, ref if source is None else source, ref, 3 + 3 * k + j, r + z, device

            self.go(make)

    def begin(self, w):
        p = self.p
        pltpu.make_async_copy(self.shards[w], self.own(w, p.z), self.local.at[w]).start()
        for s in (1, 2, 3):
            self.go(lambda s=s: (w, self.shards[w], self.own(w, p.z), s - 1, p.z, p.along_z((p.z + s) % NZ)))
        self.spread(w, 0, self.shards[w])

    def a(self, w):
        pltpu.make_async_copy(self.shards[w], self.own(w, self.p.z), self.local.at[w]).wait()
        for k in (1, 2, 3):
            self.arrived(w, self.shard(w, "own", self.level(k)), self.level(k))
            self.spread(w, k)

    def b(self, w):
        p = self.p
        for k in range(NZ):
            self.arrived(w, self.shard(w, "first", self.level(k)), 4 + self.level(k))
            for j, (r, device) in enumerate(((12, p.second), (20, p.sibling))):

                def make(k=k, j=j, r=r, device=device):
                    z = self.level(k)
                    ref = self.shard(w, "first", z)
                    return w, ref, ref, 15 + 2 * k + j, r + z, device

                self.go(make)

    def hand(self, w, at, slot, r, s):
        for k in range(NZ):
            self.arrived(w, self.shard(w, at, self.level(k)), r + self.level(k))

            def make(k=k):
                z = self.level(k)
                ref = self.shard(w, at, z)
                return w, ref, ref, s + k, slot + z, self.p.sibling

            self.go(make)

    def c(self, w):
        self.hand(w, "second", 24, 8, 23)

    def e(self, w):
        self.hand(w, "across", 28, 12, 27)

    def d(self, w):
        for r in range(16, 32):
            self.arrived(w, self.own(w, 0), r)


def ramp(start, width):
    col = lax.broadcasted_iota(jnp.int32, (32, D), 1) + start
    mine = jnp.floor((col.astype(F32) + 0.5) * (1.0 / width)).astype(jnp.int32) == lax.broadcasted_iota(jnp.int32, (32, D), 0)
    col = lax.broadcasted_iota(jnp.int32, (128, D), 1) + start
    rest = col - jnp.floor((col.astype(F32) + 0.5) * (1.0 / width)).astype(jnp.int32) * width
    pick = jnp.where(rest == lax.broadcasted_iota(jnp.int32, (128, D), 0), 1.0, 0.0).astype(BF)
    return mine, pick


def widen(packs, vec, wide):
    k = 0
    for name, ref in (("intercept", wide.intercept), ("uplift", wide.uplift)):
        rows = packs[pl.ds(k, 32, stride=8), :].astype(BF)
        for start in range(0, 32 * COUNTS[name], D):
            mine, pick = ramp(start, COUNTS[name])
            ref[:, start : start + D] = jnp.sum(jnp.where(mine, nn(rows, pick), 0.0), axis=0, keepdims=True)
        k += 1
    mine, pick = ramp(0, 24)
    for j in range(6):
        rows = packs[pl.ds(k + j, 32, stride=8), :].astype(BF)
        vec[j : j + 1, :] = jnp.sum(jnp.where(mine, nn(rows, pick), 0.0), axis=0, keepdims=True)


def narrow(sums, intercept_sum, uplift_sum, packs):
    def one(v, mine, pick):
        v = jnp.where(mine, v, 0.0)
        high = v.astype(BF)
        return nt(high, pick) + nt((v - high.astype(F32)).astype(BF), pick)

    for k, (name, ref) in enumerate((("intercept", intercept_sum), ("uplift", uplift_sum))):
        total = jnp.zeros((32, 128), F32)
        for start in range(0, 32 * COUNTS[name], D):
            total += one(ref[:, start : start + D], *ramp(start, COUNTS[name]))
        packs[pl.ds(k, 32, stride=8), :] = total
    mine, pick = ramp(0, 24)
    for j in range(6):
        packs[pl.ds(2 + j, 32, stride=8), :] = one(sums[j : j + 1, :], mine, pick)


def sinusoids(frequency, coordinates, feats_t, feats):
    for c in (0, 1):
        angles = frequency[...] * coordinates[c : c + 1, :].astype(F32)
        feats_t[c * 192 : (c + 1) * 192, :] = jnp.cos(angles).astype(BF)
        feats_t[HALF + c * 192 : HALF + (c + 1) * 192, :] = jnp.sin(angles).astype(BF)
    for k in range(6):
        feats[:, k * 128 : (k + 1) * 128] = feats_t[k * 128 : (k + 1) * 128, :].T


class Scatter:
    ROLES = ("own", "first", "second", "across")

    def __init__(self, place, counts, grads, blocks, outs, send, recv):
        self.p, self.counts, self.grads, self.blocks, self.outs = place, counts, grads, blocks, outs
        self.send, self.recv = send, recv
        self.sent = []

    def remote(self, w, src, dst, s, r, device):
        return pltpu.make_async_remote_copy(
            src_ref=src, dst_ref=dst, send_sem=self.send.at[w, s], recv_sem=self.recv.at[w, r], device_id=device, device_id_type=MESH
        )

    def go(self, make):
        self.remote(*make()).start()
        self.sent.append(make)

    def arrived(self, w, ref, r):
        self.remote(w, ref, ref, 0, r, self.p.sibling).wait_recv()

    def at(self, role):
        p = self.p
        return {"own": (p.y, p.x), "first": (p.y1, p.x1), "second": (p.y2, p.x2), "across": (p.yd, p.xd)}[role]

    def part(self, w, y, x, c):
        count = self.counts[w]
        return self.grads[w].at[:, pl.ds(pl.multiple_of(((y * NX + x) * NC + c) * count, 8), count)]

    def begin(self, w):
        theirs = {"own": "own", "first": "second", "second": "first", "across": "across"}
        for b in (3, 2, 1, 0):
            role = theirs[self.ROLES[b]]
            self.go(lambda b=b, role=role: (w, self.part(w, *self.at(role), 1 - self.p.c), self.blocks[w](b), b, b, self.p.sibling))

    def add(self, w, b, other):
        mine = self.blocks[w](b)

        @pl.loop(0, NZ)
        def _(k):
            mine[k] = (mine[k].astype(F32) + other[k].astype(F32)).astype(mine.dtype)

    def s(self, w):
        block = self.blocks[w]
        for b in (3, 2, 1, 0):
            self.arrived(w, block(b), b)
            self.add(w, b, self.part(w, *self.at(self.ROLES[b]), self.p.c))
            if b >= 2:
                self.go(lambda b=b: (w, block(b), block(7 - b), 7 - b, 7 - b, self.p.second))

    def x(self, w):
        block = self.blocks[w]
        self.arrived(w, block(4), 4)
        self.add(w, 1, block(4))
        self.go(lambda: (w, block(1), block(6), 6, 6, self.p.first))
        self.arrived(w, block(5), 5)
        self.add(w, 0, block(5))

    def f(self, w):
        p = self.p
        block = self.blocks[w]
        self.arrived(w, block(6), 6)
        self.add(w, 0, block(6))
        for s in (1, 2, 3):

            def make(s=s):
                zt = (p.z + s) % NZ
                return w, block(0).at[zt], block(7).at[p.z], 6 + s, 7 + p.z, p.along_z(zt)

            self.go(make)

    def z(self, w):
        p = self.p
        total = self.blocks[w](0)[p.z].astype(F32)
        for s in (1, 2, 3):
            zs = (p.z + s) % NZ
            self.arrived(w, self.blocks[w](7).at[zs], 7 + zs)
            total += self.blocks[w](7)[zs].astype(F32)
        self.outs[w](total)

    def end(self):
        for make in self.sent:
            self.remote(*make()).wait_send()


def pool_at(n):
    return pl.ds(pl.multiple_of((n >> 1) * 512, 512), 512), pl.ds(pl.multiple_of((n & 1) * PIECE, PIECE), PIECE)


def attend(p, qkv, relative, feats, live, places, slots, mixture):
    lanes = span(p, 128)
    q2 = qkv[:, lanes]
    k2 = qkv[:, span(p + PAIRS, 128)]
    v2 = qkv[:, span(p + 2 * PAIRS, 128)]
    every = slice(None)
    mixed = []
    for e in (0, 1):
        left, right = places[2 * e], places[2 * e + 1]
        q = only(e, q2)
        k = only(e, k2)
        turn((nt(q, table(relative, 0, 0, lanes)), nt(q, table(relative, 0, 1, lanes))), feats, left, 0, every)
        turn((nt(k, table(relative, 1, 0, lanes)), nt(k, table(relative, 1, 1, lanes))), feats, right, 0, every)
    for e in (0, 1):
        left, right = places[2 * e], places[2 * e + 1]
        scores = (nt(left[...], feats[...]) + nt(only(e, q2), k2) + nt(feats[...], right[...])) * SCALE
        key = lax.broadcasted_iota(jnp.int32, scores.shape, 1)
        scores = jnp.where(key < live, scores, NEGATIVE)
        powers = jnp.exp(scores - jnp.max(scores, axis=1, keepdims=True))
        share = (powers / jnp.sum(powers, axis=1, keepdims=True)).astype(BF)
        slots[e][...] = share
        mixed.append(nn(share, v2))
    mixture[:, lanes] = jnp.where(own_lanes(0, PAGE), mixed[0], mixed[1]).astype(BF)


def feed_pool(low, expander, uplift, activated, slope):
    @pl.loop(0, FF // PIECE)
    def _(n):
        cols = span(n, PIECE)
        v = nn(low[...], expander[:, cols]) + uplift[:, cols]
        half = 0.5 * lax.erf(v * (0.5 ** 0.5)) + 0.5
        activated[pool_at(n)] = (v * half).astype(BF)
        slope[pool_at(n)] = (half + v * (jnp.exp(v * v * -0.5) * 0.3989422804014327)).astype(BF)


def reduce_pool(activated, reducer, hold):
    @pl.loop(0, 3)
    def _(n):
        cols = span(n, PIECE)
        total = nn(activated[0:512, :], reducer[0:512, cols])
        for j in range(1, 6):
            total += nn(activated[512 * j : 512 * (j + 1), :], reducer[512 * j : 512 * (j + 1), cols])
        hold[:, cols] = total


def reducer_gradient(activated, reduced_back, grad_reducer):
    @pl.loop(0, FF // PIECE)
    def _(n):
        grad_reducer[span(n, PIECE), :] = nn(activated[pool_at(n)].T, reduced_back[...]).astype(BF)


def expander_gradient(low_t, slope, reduced_back, reducer, expander, grad_expander, uplift_sum, hook):
    @pl.loop(0, FF // PIECE)
    def _(n):
        cols = span(n, PIECE)
        inner = (nt(reduced_back[...], reducer[cols, :]) * slope[pool_at(n)].astype(F32)).astype(BF)
        slope[pool_at(n)] = inner
        uplift_sum[:, cols] = jnp.sum(inner.astype(F32), axis=0, keepdims=True)
        grad_expander[:, cols] = nn(low_t[...], inner).astype(BF)
        hook(n)


def expander_back(slope, expander, total):
    @pl.loop(0, 3)
    def _(n):
        cols = span(n, PIECE)
        part = nt(slope[0:512, :], expander[cols, 0:512])
        for j in range(1, 6):
            part += nt(slope[512 * j : 512 * (j + 1), :], expander[cols, 512 * j : 512 * (j + 1)])
        total[:, cols] += part


def back_setup(feats, top, bottom):
    for k in range(6):
        block = feats[:, k * 128 : (k + 1) * 128].T
        for h in (0, 1):
            kind, coordinate, at = (2 * k + h) // 6, (2 * k + h) // 3 % 2, (2 * k + h) % 3
            row = coordinate * HALF + kind * 192 + at * 64
            for out in (top, bottom):
                out[row : row + 64, :] = block[h * 64 : (h + 1) * 64, :]


def attend_back(p, qkv, mixture_back, slots, ready, done, relative, top, bottom, score_backs, two, grad_relative, back_t):
    lanes = span(p, 128)
    q2 = qkv[:, lanes]
    k2 = qkv[:, span(p + PAIRS, 128)]
    v2 = qkv[:, span(p + 2 * PAIRS, 128)]
    m2 = mixture_back[:, lanes]
    top[D:, :] = k2.T
    bottom[D:, :] = q2.T
    mt = m2.T
    values = []
    for e in (0, 1):
        back = nt(only(e, m2), v2)
        ready(e)
        share = slots[e][...].astype(F32)
        score_backs[e][...] = (share * (back - jnp.sum(share * back, axis=1, keepdims=True)) * SCALE).astype(BF)
        values.append(nn(mt, slots[e][...]))
        done(e)
    row = lax.broadcasted_iota(jnp.int32, (128, PAGE), 0)
    back_t[span(p + 2 * PAIRS, 128), :] = jnp.where(row < 64, values[0], values[1]).astype(BF)
    for side, source, dot, t2 in ((0, top, nt, q2), (1, bottom, nn, k2)):
        text = []
        for e in (0, 1):
            total = None
            for c in (0, 1):
                rows = slice(c * HALF, (c + 1) * HALF) if c == 0 else slice(HALF, D + 128)
                lifted = dot(source[rows, :], score_backs[e][...])
                cos = top[c * HALF : c * HALF + 192, :].astype(F32)
                sin = top[c * HALF + 192 : (c + 1) * HALF, :].astype(F32)
                g1, g2 = lifted[0:192], lifted[192:HALF]
                turned = jnp.concatenate([(g1 * sin - g2 * cos).astype(BF), (g1 * cos + g2 * sin).astype(BF)], axis=0)
                part = nn(relative[2 * side + c, :, lanes].T, turned)
                if c == 1:
                    part = part + lifted[HALF:]
                total = part if total is None else total + part
                grad = nn(turned, only(e, t2))
                kept = two.at[c * HALF : (c + 1) * HALF, 128 * side : 128 * (side + 1)]
                if e == 0:
                    kept[...] = grad
                else:
                    grad_relative[2 * side + c, :, lanes] = (kept[...] + grad).astype(BF)
            text.append(total)
        back_t[span(p + side * PAIRS, 128), :] = jnp.where(row < 64, text[0], text[1]).astype(BF)


def projector_gradient(j, tokens_t, back_t, grad_projector, intercept_sum):
    @pl.loop(0, 3)
    def _(k):
        cols = pl.ds(pl.multiple_of(k * D + j * PIECE, PIECE), PIECE)
        b = back_t[cols, :]
        intercept_sum[:, cols] = nt(jnp.ones((8, PAGE), BF), b)[0:1, :]
        grad_projector[:, :, span(3 * j + k, PIECE)] = nt(tokens_t[...], b).astype(BF).reshape(4, 192, PIECE)


def token_gradient(projector, back_t, sum_back, out):
    @pl.loop(0, 3)
    def _(n):
        cols = span(n, PIECE)
        out[:, cols] = (sum_back[:, cols] + nn(projector[cols, :], back_t[...]).T).astype(BF)


def transposed(src, dst):
    for k in range(6):
        dst[k * 128 : (k + 1) * 128, :] = src[:, k * 128 : (k + 1) * 128].T


def layer_kernel(remote, names, *refs):
    i, o, s = name_refs(names, refs)
    full = [getattr(s, "w_" + w) for w in ORDER[1:]]
    shards = [getattr(i, w) for w in ORDER[1:]]
    take_tokens = pltpu.make_async_copy(i.tokens, s.mixture_back, s.load.at[0])
    take_cotangent = pltpu.make_async_copy(i.cotangent, s.cotangent, s.load.at[1])
    take_tokens.start()
    if remote:
        p = Place()
        enter(p)
        s.pack[...] = jnp.zeros((8, 128), F32)
        for k, v in enumerate(VECTORS):
            n = COUNTS[v]
            s.pack[k : k + 1, 0:n] = getattr(i, v)[...].astype(F32).reshape(1, n)
        g = Gather2(p, [s.pack] + shards, [s.packs] + full, s.local, s.send, s.recv)
        for k in range(6):
            g.begin(k)
        vec_ref, intercept, uplift = s.vec, s.intercept, s.uplift
    else:
        takes = [pltpu.make_async_copy(a, flat(b), s.load.at[2 + k]) for k, (a, b) in enumerate(zip(shards, full))]
        for t in takes:
            t.start()
        vec_ref, intercept, uplift = i.vec, i.intercept, i.uplift
    w = types.SimpleNamespace(**{n: flat(ref) for n, ref in zip(ORDER[1:], full)})
    vec = types.SimpleNamespace(**{v: vec_ref.at[k : k + 1] for k, v in enumerate(VEC_ROWS)})
    live = i.lengths[0]
    wide = flat(s.wide)
    low, mixture, reduced_back = (wide.at[k * PAGE : (k + 1) * PAGE] for k in range(3))
    n1, hold = s.two.at[0:PAGE], s.two.at[PAGE : 2 * PAGE]
    places = [flat(s.g_reducer).at[k * PAGE : (k + 1) * PAGE] for k in range(4)]
    activated, slope = s.activated, s.slope

    sinusoids(i.frequency, i.coordinates, s.low_t, s.feats)
    if remote:
        g.a(0)
        g.a(1); g.b(0)
        g.a(2); g.b(1); g.c(0); g.e(0)
        g.a(3); g.b(2); g.c(1); g.e(1); g.d(0)
        widen(s.packs.reshape(256, 128), s.vec, types.SimpleNamespace(intercept=s.intercept, uplift=s.uplift))
        g.a(4); g.b(3); g.c(2); g.e(2); g.d(1)
        early = {0: [(g.c, 4)], 1: [(g.d, 3)], 2: [(g.b, 5)], 3: [(g.e, 4)], 4: [(g.c, 5)]}
    else:
        for t in takes:
            t.wait()
        early = {}
    take_tokens.wait()
    project(s.mixture_back, w.projector, intercept, s.qkv)
    if remote:
        g.a(5); g.b(4); g.c(3); g.e(3); g.d(2)

    slots = [s.low_t.at[0:PAGE], s.cotangent.at[:, 0:PAGE]]

    def keep(q, e):
        return pltpu.make_async_copy(slots[e], o.probs.at[2 * q + e], s.keep.at[e])

    def fetch(q, e):
        return pltpu.make_async_copy(o.probs.at[2 * q + e], slots[e], s.keep.at[e])

    def hooks(q, table_of):
        for k, steps in table_of.items():

            @pl.when(q == k)
            def _(steps=steps):
                run(steps)

    @pl.loop(0, PAIRS)
    def _(q):
        @pl.when(q >= 1)
        def _():
            keep(q - 1, 0).wait()
            keep(q - 1, 1).wait()

        attend(q, s.qkv, s.w_relative, s.feats, live, places, slots, mixture)
        keep(q, 0).start()
        keep(q, 1).start()
        hooks(q, early)

    keep(PAIRS - 1, 0).wait()
    keep(PAIRS - 1, 1).wait()
    take_cotangent.start()

    first_norm(s.mixture_back, mixture, w.combiner, vec, hold, n1, s.r1, low)
    if remote:
        g.d(4)
    feed_pool(low, w.expander, uplift, activated, slope)
    if remote:
        g.e(5)
    transposed(low, s.low_t)
    if remote:
        g.d(5)
    take_cotangent.wait()
    reduce_pool(activated, w.reducer, hold)
    second_norm(n1, s.cotangent, vec, hold, reduced_back, s.sum_back, s.cotangent, o.sums if not remote else s.sums)
    give_result = pltpu.make_async_copy(s.cotangent, o.result, s.load.at[1])
    give_result.start()
    sums, uplift_sum, intercept_sum = (s.sums, s.uplift, s.intercept) if remote else (o.sums, o.uplift_sum, o.intercept_sum)
    reducer_gradient(activated, reduced_back, flat(s.g_reducer))
    grad_relative = s.w_reducer.at[:, 0:HALF]
    grad_projector = s.w_expander.at[:, :, 0 : 3 * D]
    if remote:
        g.end()

        def whole(ref):
            def put(v):
                ref[...] = v

            return put

        def relative_part(j):
            def put(v):
                o.relative[:, j * PIECE : (j + 1) * PIECE] = v

            return put

        def projector_part(j):
            def put(v):
                for k in range(3):
                    o.projector[:, k * D + j * PIECE : k * D + (j + 1) * PIECE] = v[:, k * PIECE : (k + 1) * PIECE]

            return put

        counts = [96, 24, 24]
        grads = [s.g_reducer, s.g_expander, s.g_combiner]
        blocks = [
            lambda b: s.held_reducer.at[b],
            lambda b: s.held_expander.at[b],
            lambda b: s.w_expander.at[:, 24 * b : 24 * b + 24, 3 * D :],
        ]
        outs = [whole(o.reducer), whole(o.expander), whole(o.combiner)]
        for j in range(3):
            lanes = slice(j * PIECE, (j + 1) * PIECE)
            counts += [48, 24]
            grads += [s.w_reducer.at[:, 0:HALF, lanes], s.w_expander.at[:, :, j * D : (j + 1) * D]]
            blocks.append(lambda b, lanes=lanes: s.w_reducer.at[:, HALF + 48 * b : HALF + 48 * b + 48, lanes])
            if j < 2:
                blocks.append(lambda b, j=j: s.wide.at[:, 192 * j + 24 * b : 192 * j + 24 * b + 24])
            else:
                blocks.append(lambda b: s.w_combiner.at[:, 24 * b : 24 * b + 24])
            outs += [relative_part(j), projector_part(j)]
        counts.append(8)
        grads.append(s.packs)
        blocks.append(lambda b: s.held_small.at[b])
        outs.append(whole(o.small))
        t = Scatter(p, counts, grads, blocks, outs, s.send2, s.recv2)
        t.begin(0)
    else:
        gives = [
            pltpu.make_async_copy(a, b, s.give.at[k])
            for k, (a, b) in enumerate(
                zip(
                    [s.g_reducer, s.g_expander, s.g_combiner, grad_relative, grad_projector],
                    [o.reducer, o.expander, o.combiner, o.relative, o.projector],
                )
            )
        ]
        gives[0].start()

    def middle(n):
        if remote:
            hooks(n, middle_plan(t))

    expander_gradient(s.low_t, slope, reduced_back, w.reducer, w.expander, flat(s.g_expander), uplift_sum, middle)
    if remote:
        t.begin(1)
    else:
        gives[1].start()
    expander_back(slope, w.expander, s.sum_back)
    first_back(s.sum_back, n1, s.r1, vec, reduced_back, sums)
    if remote:
        t.s(1)
    branch_grads(mixture, reduced_back, w.combiner, flat(s.g_combiner), s.mixture_back)
    fetch(0, 0).start()
    give_result.wait()
    fetch(0, 1).start()
    if remote:
        for peer in p.peers():
            pl.semaphore_signal(s.ready, inc=1, device_id=peer, device_id_type=MESH)
        pl.semaphore_wait(s.ready, 6)
        t.begin(2)
    else:
        gives[2].start()
    top, bottom = activated.at[0:896], activated.at[896:1792]
    score_backs = [activated.at[1792:2304], activated.at[2304:2816]]
    tokens_t, back_t = slope.at[0:D], slope.at[D:]
    back_setup(s.feats, top, bottom)
    again = pltpu.make_async_copy(i.tokens, s.feats, s.load.at[0])
    again.start()
    again.wait()
    transposed(s.feats, tokens_t)
    if remote:
        run(before_plan(t))

    def project_part(j):
        projector_gradient(j, tokens_t, back_t, grad_projector, intercept_sum)

    late = {1: [(project_part, 0)], 3: [(project_part, 1)], 5: [(project_part, 2)]}
    if remote:
        for q, steps in late_plan(t).items():
            late[q] = late.get(q, []) + steps

    @pl.loop(0, PAIRS)
    def _(q):
        def done(e):
            @pl.when(q + 1 < PAIRS)
            def _():
                fetch(q + 1, e).start()

        attend_back(
            q, s.qkv, s.mixture_back, slots, lambda e: fetch(q, e).wait(), done, s.w_relative, top, bottom, score_backs, s.two, grad_relative, back_t
        )
        hooks(q, late)

    if remote:
        narrow(s.sums, intercept_sum, uplift_sum, s.packs.reshape(256, 128))
        t.begin(9)
        t.s(7)
        t.s(8)
    else:
        gives[3].start()
        gives[4].start()
    token_gradient(w.projector, back_t, s.sum_back, s.feats)
    give_tokens = pltpu.make_async_copy(s.feats, o.token_gradient, s.load.at[0])
    give_tokens.start()
    if remote:
        run(after_plan(t))
        t.end()
    else:
        for c in gives:
            c.wait()
    give_tokens.wait()


def middle_plan(t):
    return {5: [(t.s, 0)]}


def before_plan(t):
    return [(t.s, 2)]


def late_plan(t):
    return {
        0: [(t.x, 0)],
        1: [(t.begin, 3), (t.begin, 4)],
        2: [(t.s, 3), (t.s, 4), (t.f, 0), (t.x, 1)],
        3: [(t.begin, 5), (t.begin, 6), (t.x, 2)],
        4: [(t.s, 5), (t.s, 6), (t.f, 1), (t.x, 3), (t.x, 4)],
        5: [(t.begin, 7), (t.begin, 8)],
    }


def after_plan(t):
    return (
        [(t.x, 5), (t.x, 6), (t.f, 2), (t.f, 3), (t.f, 4), (t.x, 7), (t.x, 8), (t.s, 9), (t.z, 0), (t.z, 1), (t.f, 5), (t.f, 6), (t.x, 9)]
        + [(t.z, 2), (t.z, 3), (t.z, 4), (t.f, 7), (t.f, 8), (t.f, 9)] + [(t.z, k) for k in (5, 6, 7, 8, 9)]
    )


def run(steps):
    for step, w in steps:
        step(w)


def layer(tokens, coordinates, lengths, cotangent, weights, vectors, remote):
    ins = {"tokens": (tokens, HB), "coordinates": (coordinates, VM), "lengths": (lengths, SM), "cotangent": (cotangent, HB)}
    ins["frequency"] = (jnp.asarray(FREQUENCY), VM)
    ins.update({k: (weights[k], HB) for k in ORDER[1:]})
    ins.update({k: (v, VM) for k, v in vectors.items()})
    outs = {"result": ((PAGE, D), BF, HB), "token_gradient": ((PAGE, D), BF, HB), "probs": ((2 * PAIRS, PAGE, PAGE), BF, HB)}
    for k in ORDER[1:]:
        r, n = W_SHAPES[k]
        outs[k] = ((r, n), F32, VM) if remote else ((4, 8 * r, n), BF, HB)
    if remote:
        outs["small"] = ((8, 128), F32, VM)
    else:
        outs.update(sums=((8, D), F32, VM), uplift_sum=((1, FF), F32, VM), intercept_sum=((1, 3 * D), F32, VM))
    scratch = {"w_" + k: buf(4, 8 * r, n) for k, (r, n) in W_SHAPES.items()}
    scratch.update({"g_" + k: buf(4, 8 * W_SHAPES[k][0], W_SHAPES[k][1]) for k in ("combiner", "expander", "reducer")})
    scratch.update(
        feats=buf(PAGE, D), cotangent=buf(PAGE, D), qkv=buf(PAGE, 3 * D),
        wide=buf(4, HALF, D), low_t=buf(D, PAGE), mixture_back=buf(PAGE, D), two=buf(2 * PAGE, D, dtype=F32),
        sum_back=buf(PAGE, D, dtype=F32), r1=buf(PAGE, 128, dtype=F32), activated=buf(FF, PAGE), slope=buf(FF, PAGE),
        load=pltpu.SemaphoreType.DMA((7,)), keep=pltpu.SemaphoreType.DMA((2,)),
    )
    extra = {}
    if remote:
        scratch.update(
            held_reducer=buf(8, 4, 96, D), held_expander=buf(8, 4, 24, FF),
            held_small=buf(8, 4, 8, 128, dtype=F32), pack=buf(8, 128, dtype=F32), packs=buf(4, 64, 128, dtype=F32),
            vec=buf(8, D, dtype=F32), intercept=buf(1, 3 * D, dtype=F32), uplift=buf(1, FF, dtype=F32), sums=buf(8, D, dtype=F32),
            local=pltpu.SemaphoreType.DMA((6,)), send=pltpu.SemaphoreType.DMA((6, 31)), recv=pltpu.SemaphoreType.DMA((6, 32)),
            send2=pltpu.SemaphoreType.DMA((10, 10)), recv2=pltpu.SemaphoreType.DMA((10, 11)), ready=pltpu.SemaphoreType.REGULAR,
        )
        extra = dict(collective_id=0, has_side_effects=True)
    else:
        scratch["give"] = pltpu.SemaphoreType.DMA((5,))
    return call(functools.partial(layer_kernel, remote), ins, outs, scratch, "layer", **extra)


def finish_kernel(*refs):
    mats, small, outs, rest = refs[0:7], refs[7], refs[8:15], refs[15:]
    for a, b in zip(mats, outs):
        b[...] = a[...]
    for k, v in enumerate(VECTORS):
        rest[k][...] = small[k : k + 1, 0 : COUNTS[v]].reshape(COUNTS[v])


def finish(mats, small):
    outs = [jax.ShapeDtypeStruct(m.shape, m.dtype) for m in mats] + [jax.ShapeDtypeStruct((COUNTS[v],), F32) for v in VECTORS]
    got = pl.pallas_call(finish_kernel, out_shape=outs, in_specs=[VM] * 8, out_specs=[VM] * 15, name="finish")(*mats, small)
    return got[:7], dict(zip(VECTORS, got[7:]))


def whole_gather(v):
    return lax.all_gather(v, ("dp", "fsdp"), axis=0, tiled=True)


def whole_scatter(v):
    v = lax.psum_scatter(v.astype(F32), "dp", scatter_dimension=0, tiled=True)
    return lax.psum_scatter(v.astype(BF), "fsdp", scatter_dimension=0, tiled=True).astype(F32)


def cut(rows, sizes):
    parts = []
    at = 0
    for size in sizes:
        parts.append(rows[..., at : at + size])
        at += size
    return parts


def local(
    tokens, coordinates, lengths, cotangent, projector, intercept, relative, combiner, baseline,
    stretch, center, expander, uplift, reducer, offset, rescale, recenter, remote,
):
    vectors = dict(zip(VECTORS, (intercept, uplift, baseline, stretch, center, offset, rescale, recenter)))
    weights = dict(zip(ORDER[1:], (projector, relative, combiner, expander, reducer)))
    if remote:
        f = layer(tokens, coordinates, lengths, cotangent, weights, vectors, True)
        (*mats, result, token_change), small = finish([getattr(f, k) for k in ORDER[1:]] + [f.result, f.token_gradient], f.small)
        share = dict(zip(ORDER[1:], mats))
    else:
        sizes = [v.shape[0] for v in vectors.values()]
        rows = whole_gather(jnp.concatenate(list(vectors.values()))[None])
        wide = {k: v.reshape(1, -1).astype(F32) for k, v in zip(VECTORS, cut(rows, sizes))}
        table_rows = jnp.concatenate([wide[k] for k in VEC_ROWS] + [jnp.zeros((2, D), F32)])
        full = {k: whole_gather(m) for k, m in weights.items()}
        f = layer(
            tokens, coordinates, lengths, cotangent, full, {"vec": table_rows, "intercept": wide["intercept"], "uplift": wide["uplift"]}, False
        )
        change = {k: getattr(f, k).reshape(-1, W_SHAPES[k][1]) for k in ORDER[1:]}
        change["projector"] = change["projector"].reshape(D, 3, 3, PIECE).transpose(0, 2, 1, 3).reshape(D, 3 * D)
        share = {k: whole_scatter(v) for k, v in change.items()}
        sums = [f.intercept_sum[0], f.uplift_sum[0]] + [f.sums[k] for k in range(6)]
        stacked = jnp.concatenate([v.reshape(rows.shape[0], -1) for v in sums], axis=1)
        small = dict(zip(VECTORS, cut(whole_scatter(stacked)[0], sizes)))
        result, token_change = f.result, f.token_gradient
    return (
        result, token_change, share["projector"], small["intercept"], share["relative"], share["combiner"], small["baseline"],
        small["stretch"], small["center"], share["expander"], small["uplift"], share["reducer"], small["offset"], small["rescale"],
        small["recenter"],
    )


def solution(mesh):
    rows, line = P(("dp", "fsdp"), None), P(("dp", "fsdp"))
    remote = (mesh.shape["dp"], mesh.shape["fsdp"]) == (NZ * NY, NX * NC)
    return jax.shard_map(
        functools.partial(local, remote=remote),
        mesh=mesh,
        in_specs=(rows, P(None, ("dp", "fsdp")), line, rows, rows, line, rows, rows, line, line, line, rows, line, rows, line, line, line),
        out_specs=(rows, rows, rows, line, rows, rows, line, line, line, rows, line, rows, line, line, line),
        check_vma=False,
    )
```

```python
import functools
import types

import jax
import jax.numpy as jnp
import numpy as np
from jax import lax
from jax.experimental import pallas as pl
from jax.experimental.pallas import tpu as pltpu
from jax.sharding import PartitionSpec as P

MESH = pl.DeviceIdType.MESH
NZ, NY, NX, NC = 4, 2, 2, 2


PAGE = 512
D = 768
FF = 3072
HALF = 384
PAIRS = 6
SCALE = 192.0 ** -0.5
EPSILON = 1e-12
NEGATIVE = -1e30
BF = jnp.bfloat16
F32 = jnp.float32
PIECE = 256
TALL = 128
SUM_BASELINE, SUM_STRETCH, SUM_CENTER, SUM_OFFSET, SUM_RESCALE, SUM_RECENTER = range(6)
VM = pl.BlockSpec(memory_space=pltpu.VMEM)
HB = pl.BlockSpec(memory_space=pl.ANY)
SM = pl.BlockSpec(memory_space=pltpu.SMEM)
BIG = 63 << 20
W_SHAPES = {"projector": (24, 2304), "relative": (48, 768), "combiner": (24, 768), "expander": (24, 3072), "reducer": (96, 768)}
VECTORS = ("intercept", "uplift", "baseline", "stretch", "center", "offset", "rescale", "recenter")
ORDER = ("small", "projector", "relative", "combiner", "expander", "reducer")
COUNTS = {"intercept": 72, "uplift": 96, "baseline": 24, "stretch": 24, "center": 24, "offset": 24, "rescale": 24, "recenter": 24}
FREQUENCY = np.exp(-np.log(10000.0) * np.arange(192) / 192).astype(np.float32)[:, None]
VEC_ROWS = VECTORS[2:]


class Place:
    def __init__(self):
        d = lax.axis_index("dp")
        f = lax.axis_index("fsdp")
        self.z, self.y = d // NY, d % NY
        self.x, self.c = f // NC, f % NC
        z, y, x, c = self.z, self.y, self.x, self.c
        self.y1, self.x1 = y + (1 - c) * (1 - 2 * y), x + c * (1 - 2 * x)
        self.y2, self.x2 = y + c * (1 - 2 * y), x + (1 - c) * (1 - 2 * x)
        self.yd, self.xd = 1 - y, 1 - x
        self.first = (z * NY + self.y1, self.x1 * NC + c)
        self.second = (z * NY + self.y2, self.x2 * NC + c)
        self.sibling = (z * NY + y, x * NC + 1 - c)

    def along_z(self, z):
        return (z * NY + self.y, self.x * NC + self.c)

    def peers(self):
        return [self.first, self.second, self.sibling] + [self.along_z((self.z + s) % NZ) for s in (1, 2, 3)]


def enter(place):
    barrier = pltpu.get_barrier_semaphore()
    peers = place.peers()
    for peer in peers:
        pl.semaphore_signal(barrier, inc=1, device_id=peer, device_id_type=MESH)
    pl.semaphore_wait(barrier, len(peers))


def nn(a, b):
    return jnp.dot(a, b, preferred_element_type=F32)


def nt(a, b):
    return lax.dot_general(a, b, (((1,), (1,)), ((), ())), preferred_element_type=F32)


def span(i, size):
    return pl.ds(pl.multiple_of(i * size, size), size)


def own_lanes(e, rows):
    lane = lax.broadcasted_iota(jnp.int32, (rows, 128), 1)
    return lane < 64 if e == 0 else lane >= 64


def only(e, v):
    return jnp.where(own_lanes(e, v.shape[0]), v, jnp.zeros_like(v))


def only_rows(e, v):
    row = lax.broadcasted_iota(jnp.int32, v.shape, 0)
    return jnp.where(row < 64 if e == 0 else row >= 64, v, jnp.zeros_like(v))


def project(tokens, projector, intercept, qkv):
    @pl.loop(0, 9)
    def _(n):
        cols = span(n, PIECE)
        qkv[:, cols] = (nn(tokens[...], projector[:, cols]) + intercept[:, cols]).astype(BF)


def table(relative, side, half, cols):
    return relative[2 * side : 2 * side + 2, half * 192 : (half + 1) * 192, cols].reshape(HALF, 128)


def turn(weights, feats, out, rows):
    ws, wc = weights[:, :HALF], weights[:, HALF:]
    c = feats[rows, :HALF].astype(F32)
    s = feats[rows, HALF:].astype(F32)
    out[rows, :HALF] = (ws * s + wc * c).astype(BF)
    out[rows, HALF:] = (wc * s - ws * c).astype(BF)


def mean(v):
    return jnp.sum(v, axis=1, keepdims=True) * (1.0 / D)


def first_norm(tokens, mixture, combiner, vec, hold, n1, r1, low):
    @pl.loop(0, 3)
    def _(n):
        cols = span(n, PIECE)
        hold[:, cols] = nn(mixture[...], combiner[:, cols])

    @pl.loop(0, PAGE // TALL)
    def _(i):
        rows = span(i, TALL)
        v = tokens[rows, :].astype(F32) + hold[rows, :] + vec.baseline[...]
        v = v - mean(v)
        r = lax.rsqrt(mean(v * v) + EPSILON)
        v = v * r
        n1[rows, :] = v
        r1[rows, :] = jnp.broadcast_to(r, (TALL, 128))
        low[rows, :] = (v * vec.stretch[...] + vec.center[...]).astype(BF)


def second_norm(n1, cotangent, vec, hold, reduced_back, second_back, result, sums):
    zero = jnp.zeros((8, D), F32)

    def fold(v):
        return jnp.sum(v.reshape(TALL // 8, 8, D), axis=0)

    def body(i, carry):
        rescale_sum, recenter_sum, offset_sum = carry
        rows = span(i, TALL)
        v = (n1[rows, :] * vec.stretch[...] + vec.center[...]) + hold[rows, :] + vec.offset[...]
        v = v - mean(v)
        r = lax.rsqrt(mean(v * v) + EPSILON)
        v = v * r
        g = cotangent[rows, :].astype(F32)
        result[rows, :] = (v * vec.rescale[...] + vec.recenter[...]).astype(BF)
        u = g * vec.rescale[...]
        back = r * (u - mean(u) - v * mean(u * v))
        second_back[rows, :] = back
        low = back.astype(BF)
        reduced_back[rows, :] = low
        return (rescale_sum + fold(g * v), recenter_sum + fold(g), offset_sum + fold(low.astype(F32)))

    a, b, c = lax.fori_loop(0, PAGE // TALL, body, (zero, zero, zero))
    for k, v in ((SUM_RESCALE, a), (SUM_RECENTER, b), (SUM_OFFSET, c)):
        sums[k : k + 1, :] = jnp.sum(v, axis=0, keepdims=True)


def first_back(total, n1, r1, vec, branch_back, sums):
    zero = jnp.zeros((8, D), F32)

    def fold(v):
        return jnp.sum(v.reshape(TALL // 8, 8, D), axis=0)

    def body(i, carry):
        stretch_sum, center_sum, baseline_sum = carry
        rows = span(i, TALL)
        b = total[rows, :]
        v = n1[rows, :]
        u = b * vec.stretch[...]
        back = r1[rows, :1] * (u - mean(u) - v * mean(u * v))
        total[rows, :] = back
        low = back.astype(BF)
        branch_back[rows, :] = low
        return (stretch_sum + fold(b * v), center_sum + fold(b), baseline_sum + fold(low.astype(F32)))

    a, b, c = lax.fori_loop(0, PAGE // TALL, body, (zero, zero, zero))
    for k, v in ((SUM_STRETCH, a), (SUM_CENTER, b), (SUM_BASELINE, c)):
        sums[k : k + 1, :] = jnp.sum(v, axis=0, keepdims=True)


def branch_grads(mixture, branch_back, combiner, grad_combiner, mixture_back):
    @pl.loop(0, 3)
    def _(n):
        cols = span(n, PIECE)
        grad_combiner[cols, :] = nn(mixture[:, cols].T, branch_back[...]).astype(BF)
        mixture_back[:, cols] = nt(branch_back[...], combiner[cols, :]).astype(BF)


def flat(ref):
    return ref.reshape(ref.shape[0] * ref.shape[1], ref.shape[2])


def name_refs(groups, refs):
    out = []
    at = 0
    for g in groups:
        out.append(types.SimpleNamespace(**dict(zip(g, refs[at : at + len(g)]))))
        at += len(g)
    return out


def call(kernel, ins, outs, scratch, name, **params):
    names = (tuple(ins), tuple(outs), tuple(scratch))
    got = pl.pallas_call(
        functools.partial(kernel, names),
        out_shape=[jax.ShapeDtypeStruct(s, d) for s, d, _ in outs.values()],
        in_specs=[sp for _, sp in ins.values()],
        out_specs=[sp for _, _, sp in outs.values()],
        scratch_shapes=list(scratch.values()),
        compiler_params=pltpu.CompilerParams(vmem_limit_bytes=BIG, **params),
        name=name,
    )(*[a for a, _ in ins.values()])
    return types.SimpleNamespace(**dict(zip(outs, got)))


def buf(*shape, dtype=BF):
    return pltpu.VMEM(shape, dtype)


class Gather:
    def __init__(self, place, shards, full, local, send, recv):
        self.p, self.shards, self.full = place, shards, full
        self.local, self.send, self.recv = local, send, recv
        self.sent = []

    def remote(self, w, src, dst, s, r, device):
        return pltpu.make_async_remote_copy(
            src_ref=src, dst_ref=dst, send_sem=self.send.at[w, s], recv_sem=self.recv.at[w, r], device_id=device, device_id_type=MESH
        )

    def go(self, make):
        self.remote(*make()).start()
        self.sent.append(make)

    def arrived(self, w, ref, r):
        self.remote(w, ref, ref, 0, r, self.p.sibling).wait_recv()

    def begin(self):
        p = self.p
        for w in range(len(self.shards)):
            pltpu.make_async_copy(self.shards[w], self.own(w, p.z), self.local.at[w]).start()
            for s in (1, 2, 3):
                self.go(lambda w=w, s=s: (w, self.shards[w], self.own(w, p.z), s - 1, p.z, p.along_z((p.z + s) % NZ)))

    def rows(self, w, y, x, c):
        count = self.shards[w].shape[0]
        return pl.ds(pl.multiple_of(((y * NX + x) * NC + c) * count, 8), count)

    def own(self, w, z):
        p = self.p
        return self.full[w].at[z, self.rows(w, p.y, p.x, p.c)]

    def block(self, w, at):
        p = self.p
        y, x = {"own": (p.y, p.x), "first": (p.y1, p.x1), "second": (p.y2, p.x2), "across": (p.yd, p.xd)}[at]
        return self.full[w].at[:, self.rows(w, y, x, p.c)]

    def pass_on(self, w, at, *moves):
        for s, r, device in moves:
            self.go(lambda s=s, r=r, device=device: (w, self.block(w, at), self.block(w, at), s, r, device))

    def a(self, w):
        p = self.p
        pltpu.make_async_copy(self.shards[w], self.own(w, p.z), self.local.at[w]).wait()
        for s in (1, 2, 3):
            zs = (p.z + s) % NZ
            self.arrived(w, self.own(w, zs), zs)
        self.pass_on(w, "own", (3, 4, p.first), (4, 5, p.second), (5, 7, p.sibling))

    def b(self, w):
        p = self.p
        self.arrived(w, self.block(w, "first"), 4)
        self.pass_on(w, "first", (6, 6, p.second), (7, 8, p.sibling))

    def c(self, w):
        p = self.p
        self.arrived(w, self.block(w, "second"), 5)
        self.pass_on(w, "second", (8, 9, p.sibling))
        self.arrived(w, self.block(w, "across"), 6)
        self.pass_on(w, "across", (9, 10, p.sibling))

    def d(self, w):
        for r in range(7, 11):
            self.arrived(w, self.block(w, "own"), r)

    def end(self):
        for make in self.sent:
            self.remote(*make()).wait_send()


class Gather2(Gather):
    def shard(self, w, at, z):
        p = self.p
        y, x = {"own": (p.y, p.x), "first": (p.y1, p.x1), "second": (p.y2, p.x2), "across": (p.yd, p.xd)}[at]
        return self.full[w].at[z, self.rows(w, y, x, p.c)]

    def level(self, k):
        return (self.p.z + k) % NZ

    def spread(self, w, k, source=None):
        p = self.p
        for j, (r, device) in enumerate(((4, p.first), (8, p.second), (16, p.sibling))):

            def make(j=j, r=r, device=device):
                z = self.level(k)
                ref = self.shard(w, "own", z)
                return w, ref if source is None else source, ref, 3 + 3 * k + j, r + z, device

            self.go(make)

    def begin(self, w):
        p = self.p
        pltpu.make_async_copy(self.shards[w], self.own(w, p.z), self.local.at[w]).start()
        for s in (1, 2, 3):
            self.go(lambda s=s: (w, self.shards[w], self.own(w, p.z), s - 1, p.z, p.along_z((p.z + s) % NZ)))
        self.spread(w, 0, self.shards[w])

    def a(self, w):
        pltpu.make_async_copy(self.shards[w], self.own(w, self.p.z), self.local.at[w]).wait()
        for k in (1, 2, 3):
            self.arrived(w, self.shard(w, "own", self.level(k)), self.level(k))
            self.spread(w, k)

    def b(self, w, ks=range(NZ)):
        p = self.p
        for k in ks:
            self.arrived(w, self.shard(w, "first", self.level(k)), 4 + self.level(k))
            for j, (r, device) in enumerate(((12, p.second), (20, p.sibling))):

                def make(k=k, j=j, r=r, device=device):
                    z = self.level(k)
                    ref = self.shard(w, "first", z)
                    return w, ref, ref, 15 + 2 * k + j, r + z, device

                self.go(make)

    def b_part(self, w):
        return lambda k: self.b(w, [k])

    def hand(self, w, at, slot, r, s):
        for k in range(NZ):
            self.arrived(w, self.shard(w, at, self.level(k)), r + self.level(k))

            def make(k=k):
                z = self.level(k)
                ref = self.shard(w, at, z)
                return w, ref, ref, s + k, slot + z, self.p.sibling

            self.go(make)

    def c(self, w):
        self.hand(w, "second", 24, 8, 23)

    def e(self, w):
        self.hand(w, "across", 28, 12, 27)

    def d(self, w):
        for r in range(16, 32):
            self.arrived(w, self.own(w, 0), r)


def ramp(start, width):
    col = lax.broadcasted_iota(jnp.int32, (32, D), 1) + start
    mine = jnp.floor((col.astype(F32) + 0.5) * (1.0 / width)).astype(jnp.int32) == lax.broadcasted_iota(jnp.int32, (32, D), 0)
    col = lax.broadcasted_iota(jnp.int32, (128, D), 1) + start
    rest = col - jnp.floor((col.astype(F32) + 0.5) * (1.0 / width)).astype(jnp.int32) * width
    pick = jnp.where(rest == lax.broadcasted_iota(jnp.int32, (128, D), 0), 1.0, 0.0).astype(BF)
    return mine, pick


def widen(packs, vec, wide):
    k = 0
    for name, ref in (("intercept", wide.intercept), ("uplift", wide.uplift)):
        rows = packs[pl.ds(k, 32, stride=8), :].astype(BF)
        for start in range(0, 32 * COUNTS[name], D):
            mine, pick = ramp(start, COUNTS[name])
            ref[:, start : start + D] = jnp.sum(jnp.where(mine, nn(rows, pick), 0.0), axis=0, keepdims=True)
        k += 1
    mine, pick = ramp(0, 24)
    for j in range(6):
        rows = packs[pl.ds(k + j, 32, stride=8), :].astype(BF)
        vec[j : j + 1, :] = jnp.sum(jnp.where(mine, nn(rows, pick), 0.0), axis=0, keepdims=True)


def narrow(sums, intercept_sum, uplift_sum, packs):
    def one(v, mine, pick):
        v = jnp.where(mine, v, 0.0)
        high = v.astype(BF)
        return nt(high, pick) + nt((v - high.astype(F32)).astype(BF), pick)

    for k, (name, ref) in enumerate((("intercept", intercept_sum), ("uplift", uplift_sum))):
        total = jnp.zeros((32, 128), F32)
        for start in range(0, 32 * COUNTS[name], D):
            total += one(ref[:, start : start + D], *ramp(start, COUNTS[name]))
        packs[pl.ds(k, 32, stride=8), :] = total
    mine, pick = ramp(0, 24)
    for j in range(6):
        packs[pl.ds(2 + j, 32, stride=8), :] = one(sums[j : j + 1, :], mine, pick)


def sinusoids(frequency, coordinates, feats_t, feats):
    for c in (0, 1):
        angles = frequency[...] * coordinates[c : c + 1, :].astype(F32)
        feats_t[c * 192 : (c + 1) * 192, :] = jnp.cos(angles).astype(BF)
        feats_t[HALF + c * 192 : HALF + (c + 1) * 192, :] = jnp.sin(angles).astype(BF)
    for k in range(6):
        feats[:, k * 128 : (k + 1) * 128] = feats_t[k * 128 : (k + 1) * 128, :].T


class Scatter:
    ROLES = ("own", "first", "second", "across")

    def __init__(self, place, counts, grads, blocks, outs, send, recv):
        self.p, self.counts, self.grads, self.blocks, self.outs = place, counts, grads, blocks, outs
        self.send, self.recv = send, recv
        self.sent = []

    def remote(self, w, src, dst, s, r, device):
        return pltpu.make_async_remote_copy(
            src_ref=src, dst_ref=dst, send_sem=self.send.at[w, s], recv_sem=self.recv.at[w, r], device_id=device, device_id_type=MESH
        )

    def go(self, make):
        self.remote(*make()).start()
        self.sent.append(make)

    def arrived(self, w, ref, r):
        self.remote(w, ref, ref, 0, r, self.p.sibling).wait_recv()

    def at(self, role):
        p = self.p
        return {"own": (p.y, p.x), "first": (p.y1, p.x1), "second": (p.y2, p.x2), "across": (p.yd, p.xd)}[role]

    def part(self, w, y, x, c):
        count = self.counts[w]
        return self.grads[w].at[:, pl.ds(pl.multiple_of(((y * NX + x) * NC + c) * count, 8), count)]

    def begin(self, w):
        theirs = {"own": "own", "first": "second", "second": "first", "across": "across"}
        for b in (3, 2, 1, 0):
            role = theirs[self.ROLES[b]]
            self.go(lambda b=b, role=role: (w, self.part(w, *self.at(role), 1 - self.p.c), self.blocks[w](b), b, b, self.p.sibling))

    def add(self, w, b, other):
        mine = self.blocks[w](b)

        @pl.loop(0, NZ)
        def _(k):
            mine[k] = (mine[k].astype(F32) + other[k].astype(F32)).astype(mine.dtype)

    def s(self, w):
        block = self.blocks[w]
        for b in (3, 2, 1, 0):
            self.arrived(w, block(b), b)
            self.add(w, b, self.part(w, *self.at(self.ROLES[b]), self.p.c))
            if b >= 2:
                self.go(lambda b=b: (w, block(b), block(7 - b), 7 - b, 7 - b, self.p.second))

    def x(self, w):
        block = self.blocks[w]
        self.arrived(w, block(4), 4)
        self.add(w, 1, block(4))
        self.go(lambda: (w, block(1), block(6), 6, 6, self.p.first))
        self.arrived(w, block(5), 5)
        self.add(w, 0, block(5))

    def f(self, w):
        p = self.p
        block = self.blocks[w]
        self.arrived(w, block(6), 6)
        self.add(w, 0, block(6))
        for s in (1, 2, 3):

            def make(s=s):
                zt = (p.z + s) % NZ
                return w, block(0).at[zt], block(7).at[p.z], 6 + s, 7 + p.z, p.along_z(zt)

            self.go(make)

    def z(self, w):
        p = self.p
        total = self.blocks[w](0)[p.z].astype(F32)
        for s in (1, 2, 3):
            zs = (p.z + s) % NZ
            self.arrived(w, self.blocks[w](7).at[zs], 7 + zs)
            total += self.blocks[w](7)[zs].astype(F32)
        self.outs[w](total)

    def end(self):
        for make in self.sent:
            self.remote(*make()).wait_send()


def pool_at(n):
    return pl.ds(pl.multiple_of((n >> 1) * 512, 512), 512), pl.ds(pl.multiple_of((n & 1) * PIECE, PIECE), PIECE)


def attend(p, qkv, relative, feats, live, places, slots, mixture):
    lanes = span(p, 128)
    q2 = qkv[:, lanes]
    k2 = qkv[:, span(p + PAIRS, 128)]
    v2 = qkv[:, span(p + 2 * PAIRS, 128)]
    every = slice(None)
    mixed = []
    tables = [jnp.concatenate([table(relative, side, half, lanes) for half in (0, 1)], axis=0) for side in (0, 1)]
    for e in (0, 1):
        left, right = places[2 * e], places[2 * e + 1]
        q = only(e, q2)
        k = only(e, k2)
        turn(nt(q, tables[0]), feats, left, every)
        turn(nt(k, tables[1]), feats, right, every)
    for e in (0, 1):
        left, right = places[2 * e], places[2 * e + 1]
        scores = (nt(left[...], feats[...]) + nt(only(e, q2), k2) + nt(feats[...], right[...])) * SCALE
        key = lax.broadcasted_iota(jnp.int32, scores.shape, 1)
        scores = jnp.where(key < live, scores, NEGATIVE)
        powers = jnp.exp(scores - jnp.max(scores, axis=1, keepdims=True))
        share = (powers / jnp.sum(powers, axis=1, keepdims=True)).astype(BF)
        slots[e][...] = share
        mixed.append(nn(share, v2))
    mixture[:, lanes] = jnp.where(own_lanes(0, PAGE), mixed[0], mixed[1]).astype(BF)


def feed_pool(low, expander, uplift, activated, slope):
    @pl.loop(0, FF // PIECE)
    def _(n):
        cols = span(n, PIECE)
        v = nn(low[...], expander[:, cols]) + uplift[:, cols]
        half = 0.5 * lax.erf(v * (0.5 ** 0.5)) + 0.5
        activated[pool_at(n)] = (v * half).astype(BF)
        slope[pool_at(n)] = (half + v * (jnp.exp(v * v * -0.5) * 0.3989422804014327)).astype(BF)


def reduce_pool(activated, reducer, hold):
    @pl.loop(0, 3)
    def _(n):
        cols = span(n, PIECE)
        total = nn(activated[0:512, :], reducer[0:512, cols])
        for j in range(1, 6):
            total += nn(activated[512 * j : 512 * (j + 1), :], reducer[512 * j : 512 * (j + 1), cols])
        hold[:, cols] = total


def reducer_gradient(activated, reduced_back, grad_reducer):
    @pl.loop(0, FF // PIECE)
    def _(n):
        grad_reducer[span(n, PIECE), :] = nn(activated[pool_at(n)].T, reduced_back[...]).astype(BF)


def expander_gradient(low_t, slope, reduced_back, reducer, expander, grad_expander, uplift_sum, hook):
    @pl.loop(0, FF // PIECE)
    def _(n):
        cols = span(n, PIECE)
        inner = (nt(reduced_back[...], reducer[cols, :]) * slope[pool_at(n)].astype(F32)).astype(BF)
        slope[pool_at(n)] = inner
        uplift_sum[:, cols] = jnp.sum(inner.astype(F32), axis=0, keepdims=True)
        grad_expander[:, cols] = nn(low_t[...], inner).astype(BF)
        hook(n)


def expander_back(slope, expander, total):
    @pl.loop(0, 3)
    def _(n):
        cols = span(n, PIECE)
        part = nt(slope[0:512, :], expander[cols, 0:512])
        for j in range(1, 6):
            part += nt(slope[512 * j : 512 * (j + 1), :], expander[cols, 512 * j : 512 * (j + 1)])
        total[:, cols] += part


def back_setup(feats, top, bottom):
    for k in range(6):
        block = feats[:, k * 128 : (k + 1) * 128].T
        for h in (0, 1):
            kind, coordinate, at = (2 * k + h) // 6, (2 * k + h) // 3 % 2, (2 * k + h) % 3
            row = coordinate * HALF + kind * 192 + at * 64
            for out in (top, bottom):
                out[row : row + 64, :] = block[h * 64 : (h + 1) * 64, :]


def attend_back(p, qkv, mixture_back, slots, ready, done, relative, top, bottom, score_backs, two, grad_relative, back_t):
    lanes = span(p, 128)
    q2 = qkv[:, lanes]
    k2 = qkv[:, span(p + PAIRS, 128)]
    v2 = qkv[:, span(p + 2 * PAIRS, 128)]
    m2 = mixture_back[:, lanes]
    top[D:, :] = k2.T
    bottom[D:, :] = q2.T
    mt = m2.T
    values = []
    for e in (0, 1):
        back = nt(only(e, m2), v2)
        ready(e)
        share = slots[e][...].astype(F32)
        score_backs[e][...] = (share * (back - jnp.sum(share * back, axis=1, keepdims=True)) * SCALE).astype(BF)
        values.append(nn(mt, slots[e][...]))
        done(e)
    row = lax.broadcasted_iota(jnp.int32, (128, PAGE), 0)
    back_t[span(p + 2 * PAIRS, 128), :] = jnp.where(row < 64, values[0], values[1]).astype(BF)
    for side, source, dot, t2 in ((0, top, nt, q2), (1, bottom, nn, k2)):
        text = []
        backward = jnp.concatenate([relative[2 * side + c, :, lanes].T for c in (0, 1)], axis=1)
        for e in (0, 1):
            both = []
            for c in (0, 1):
                rows = slice(c * HALF, (c + 1) * HALF) if c == 0 else slice(HALF, D + 128)
                lifted = dot(source[rows, :], score_backs[e][...])
                cos = top[c * HALF : c * HALF + 192, :].astype(F32)
                sin = top[c * HALF + 192 : (c + 1) * HALF, :].astype(F32)
                g1, g2 = lifted[0:192], lifted[192:HALF]
                both += [(g1 * sin - g2 * cos).astype(BF), (g1 * cos + g2 * sin).astype(BF)]
            turned = jnp.concatenate(both, axis=0)
            text.append(nn(backward, turned) + lifted[HALF:])
            grad = nn(turned, only(e, t2))
            kept = two.at[0:D, 128 * side : 128 * (side + 1)]
            if e == 0:
                kept[...] = grad
            else:
                grad_relative[2 * side : 2 * side + 2, :, lanes] = (kept[...] + grad).astype(BF).reshape(2, HALF, 128)
        back_t[span(p + side * PAIRS, 128), :] = jnp.where(row < 64, text[0], text[1]).astype(BF)


def projector_gradient(j, tokens_t, back_t, grad_projector, intercept_sum):
    @pl.loop(0, 3)
    def _(k):
        cols = pl.ds(pl.multiple_of(k * D + j * PIECE, PIECE), PIECE)
        b = back_t[cols, :]
        intercept_sum[:, cols] = nt(jnp.ones((8, PAGE), BF), b)[0:1, :]
        grad_projector[:, :, span(3 * j + k, PIECE)] = nt(tokens_t[...], b).astype(BF).reshape(4, 192, PIECE)


def token_gradient(projector, back_t, sum_back, out):
    @pl.loop(0, 3)
    def _(n):
        cols = span(n, PIECE)
        out[:, cols] = (sum_back[:, cols] + nn(projector[cols, :], back_t[...]).T).astype(BF)


def transposed(src, dst):
    for k in range(6):
        dst[k * 128 : (k + 1) * 128, :] = src[:, k * 128 : (k + 1) * 128].T


def layer_kernel(remote, names, *refs):
    i, o, s = name_refs(names, refs)
    full = [getattr(s, "w_" + w) for w in ORDER[1:]]
    shards = [getattr(i, w) for w in ORDER[1:]]
    take_tokens = pltpu.make_async_copy(i.tokens, s.mixture_back, s.load.at[0])
    take_cotangent = pltpu.make_async_copy(i.cotangent, s.cotangent, s.load.at[1])
    take_tokens.start()
    if remote:
        p = Place()
        enter(p)
        s.pack[...] = jnp.zeros((8, 128), F32)
        for k, v in enumerate(VECTORS):
            n = COUNTS[v]
            s.pack[k : k + 1, 0:n] = getattr(i, v)[...].astype(F32).reshape(1, n)
        g = Gather2(p, [s.pack] + shards, [s.packs] + full, s.local, s.send, s.recv)
        for k in range(6):
            g.begin(k)
        vec_ref, intercept, uplift = s.vec, s.intercept, s.uplift
    else:
        takes = [pltpu.make_async_copy(a, flat(b), s.load.at[2 + k]) for k, (a, b) in enumerate(zip(shards, full))]
        for t in takes:
            t.start()
        vec_ref, intercept, uplift = i.vec, i.intercept, i.uplift
    w = types.SimpleNamespace(**{n: flat(ref) for n, ref in zip(ORDER[1:], full)})
    vec = types.SimpleNamespace(**{v: vec_ref.at[k : k + 1] for k, v in enumerate(VEC_ROWS)})
    live = i.lengths[0]
    wide = flat(s.wide)
    low, mixture, reduced_back = (wide.at[k * PAGE : (k + 1) * PAGE] for k in range(3))
    n1, hold = s.two.at[0:PAGE], s.two.at[PAGE : 2 * PAGE]
    places = [flat(s.g_reducer).at[k * PAGE : (k + 1) * PAGE] for k in range(4)]
    activated, slope = s.activated, s.slope

    sinusoids(i.frequency, i.coordinates, s.low_t, s.feats)
    if remote:
        g.a(0)
        g.a(1); g.b(0)
        g.a(2); g.b(1); g.c(0); g.e(0); g.d(0)
        g.a(3); g.b(2); g.c(1)
        widen(s.packs.reshape(256, 128), s.vec, types.SimpleNamespace(intercept=s.intercept, uplift=s.uplift))
        g.a(4); g.e(1); g.b(3); g.c(2); g.d(1)
        part = g.b_part(5)
        early = {0: [(g.c, 3), (part, 0)], 1: [(part, 1), (part, 2)], 2: [(part, 3), (g.c, 4), (g.e, 3)], 3: [(g.d, 3)], 4: [(g.c, 5), (g.e, 4)]}
    else:
        for t in takes:
            t.wait()
        early = {}
    take_tokens.wait()
    project(s.mixture_back, w.projector, intercept, s.qkv)
    if remote:
        g.e(2); g.a(5); g.b(4); g.d(2)

    slots = [s.low_t.at[0:PAGE], s.cotangent.at[:, 0:PAGE]]

    def keep(q, e):
        return pltpu.make_async_copy(slots[e], o.probs.at[2 * q + e], s.keep.at[e])

    def fetch(q, e):
        return pltpu.make_async_copy(o.probs.at[2 * q + e], slots[e], s.keep.at[e])

    def hooks(q, table_of):
        for k, steps in table_of.items():

            @pl.when(q == k)
            def _(steps=steps):
                run(steps)

    @pl.loop(0, PAIRS)
    def _(q):
        @pl.when(q >= 1)
        def _():
            keep(q - 1, 0).wait()
            keep(q - 1, 1).wait()

        attend(q, s.qkv, s.w_relative, s.feats, live, places, slots, mixture)
        keep(q, 0).start()
        keep(q, 1).start()
        hooks(q, early)

    keep(PAIRS - 1, 0).wait()
    keep(PAIRS - 1, 1).wait()
    take_cotangent.start()

    first_norm(s.mixture_back, mixture, w.combiner, vec, hold, n1, s.r1, low)
    if remote:
        g.d(4)
    feed_pool(low, w.expander, uplift, activated, slope)
    if remote:
        g.e(5)
    transposed(low, s.low_t)
    if remote:
        g.d(5)
    take_cotangent.wait()
    reduce_pool(activated, w.reducer, hold)
    second_norm(n1, s.cotangent, vec, hold, reduced_back, s.sum_back, s.cotangent, o.sums if not remote else s.sums)
    give_result = pltpu.make_async_copy(s.cotangent, o.result, s.load.at[1])
    give_result.start()
    sums, uplift_sum, intercept_sum = (s.sums, s.uplift, s.intercept) if remote else (o.sums, o.uplift_sum, o.intercept_sum)
    reducer_gradient(activated, reduced_back, flat(s.g_reducer))
    grad_relative = s.w_reducer.at[:, 0:HALF]
    grad_projector = s.w_expander.at[:, :, 0 : 3 * D]
    if remote:
        g.end()

        def whole(ref):
            def put(v):
                ref[...] = v

            return put

        def relative_part(j):
            def put(v):
                o.relative[:, j * PIECE : (j + 1) * PIECE] = v

            return put

        def projector_part(j):
            def put(v):
                for k in range(3):
                    o.projector[:, k * D + j * PIECE : k * D + (j + 1) * PIECE] = v[:, k * PIECE : (k + 1) * PIECE]

            return put

        counts = [96, 24, 24]
        grads = [s.g_reducer, s.g_expander, s.g_combiner]
        blocks = [
            lambda b: s.held_reducer.at[b],
            lambda b: s.held_expander.at[b],
            lambda b: s.w_expander.at[:, 24 * b : 24 * b + 24, 3 * D :],
        ]
        outs = [whole(o.reducer), whole(o.expander), whole(o.combiner)]
        for j in range(3):
            lanes = slice(j * PIECE, (j + 1) * PIECE)
            counts += [48, 24]
            grads += [s.w_reducer.at[:, 0:HALF, lanes], s.w_expander.at[:, :, j * D : (j + 1) * D]]
            blocks.append(lambda b, lanes=lanes: s.w_reducer.at[:, HALF + 48 * b : HALF + 48 * b + 48, lanes])
            if j < 2:
                blocks.append(lambda b, j=j: s.wide.at[:, 192 * j + 24 * b : 192 * j + 24 * b + 24])
            else:
                blocks.append(lambda b: s.w_combiner.at[:, 24 * b : 24 * b + 24])
            outs += [relative_part(j), projector_part(j)]
        counts.append(8)
        grads.append(s.packs)
        blocks.append(lambda b: s.held_small.at[b])
        outs.append(whole(o.small))
        t = Scatter(p, counts, grads, blocks, outs, s.send2, s.recv2)
        t.begin(0)
    else:
        gives = [
            pltpu.make_async_copy(a, b, s.give.at[k])
            for k, (a, b) in enumerate(
                zip(
                    [s.g_reducer, s.g_expander, s.g_combiner, grad_relative, grad_projector],
                    [o.reducer, o.expander, o.combiner, o.relative, o.projector],
                )
            )
        ]
        gives[0].start()

    def middle(n):
        if remote:
            hooks(n, middle_plan(t))

    expander_gradient(s.low_t, slope, reduced_back, w.reducer, w.expander, flat(s.g_expander), uplift_sum, middle)
    if remote:
        t.begin(1)
    else:
        gives[1].start()
    expander_back(slope, w.expander, s.sum_back)
    first_back(s.sum_back, n1, s.r1, vec, reduced_back, sums)
    if remote:
        t.s(1)
    branch_grads(mixture, reduced_back, w.combiner, flat(s.g_combiner), s.mixture_back)
    fetch(0, 0).start()
    give_result.wait()
    fetch(0, 1).start()
    if remote:
        for peer in p.peers():
            pl.semaphore_signal(s.ready, inc=1, device_id=peer, device_id_type=MESH)
        pl.semaphore_wait(s.ready, 6)
        t.begin(2)
    else:
        gives[2].start()
    top, bottom = activated.at[0:896], activated.at[896:1792]
    score_backs = [activated.at[1792:2304], activated.at[2304:2816]]
    tokens_t, back_t = slope.at[0:D], slope.at[D:]
    back_setup(s.feats, top, bottom)
    again = pltpu.make_async_copy(i.tokens, s.feats, s.load.at[0])
    again.start()
    again.wait()
    transposed(s.feats, tokens_t)
    if remote:
        run(before_plan(t))

    def project_part(j):
        projector_gradient(j, tokens_t, back_t, grad_projector, intercept_sum)

    late = {1: [(project_part, 0)], 3: [(project_part, 1)], 5: [(project_part, 2)]}
    if remote:
        for q, steps in late_plan(t).items():
            late[q] = late.get(q, []) + steps

    @pl.loop(0, PAIRS)
    def _(q):
        def done(e):
            @pl.when(q + 1 < PAIRS)
            def _():
                fetch(q + 1, e).start()

        attend_back(
            q, s.qkv, s.mixture_back, slots, lambda e: fetch(q, e).wait(), done, s.w_relative, top, bottom, score_backs, s.two, grad_relative, back_t
        )
        hooks(q, late)

    if remote:
        narrow(s.sums, intercept_sum, uplift_sum, s.packs.reshape(256, 128))
        t.begin(9)
        t.s(7)
        t.s(8)
    else:
        gives[3].start()
        gives[4].start()
    token_gradient(w.projector, back_t, s.sum_back, s.feats)
    give_tokens = pltpu.make_async_copy(s.feats, o.token_gradient, s.load.at[0])
    give_tokens.start()
    if remote:
        run(after_plan(t))
        t.end()
    else:
        for c in gives:
            c.wait()
    give_tokens.wait()


def middle_plan(t):
    return {5: [(t.s, 0)]}


def before_plan(t):
    return [(t.s, 2)]


def late_plan(t):
    return {
        0: [(t.x, 0)],
        1: [(t.begin, 3), (t.begin, 4)],
        2: [(t.s, 3), (t.s, 4), (t.f, 0), (t.x, 1)],
        3: [(t.begin, 5), (t.begin, 6), (t.x, 2)],
        4: [(t.s, 5), (t.s, 6), (t.f, 1), (t.x, 3), (t.x, 4)],
        5: [(t.begin, 7), (t.begin, 8)],
    }


def after_plan(t):
    return (
        [(t.x, 5), (t.x, 6), (t.f, 2), (t.f, 3), (t.f, 4), (t.x, 7), (t.x, 8), (t.s, 9), (t.z, 0), (t.z, 1), (t.f, 5), (t.f, 6), (t.x, 9)]
        + [(t.z, 2), (t.z, 3), (t.z, 4), (t.f, 7), (t.f, 8), (t.f, 9)] + [(t.z, k) for k in (5, 6, 7, 8, 9)]
    )


def run(steps):
    for step, w in steps:
        step(w)


def layer(tokens, coordinates, lengths, cotangent, weights, vectors, remote):
    ins = {"tokens": (tokens, HB), "coordinates": (coordinates, VM), "lengths": (lengths, SM), "cotangent": (cotangent, HB)}
    ins["frequency"] = (jnp.asarray(FREQUENCY), VM)
    ins.update({k: (weights[k], HB) for k in ORDER[1:]})
    ins.update({k: (v, VM) for k, v in vectors.items()})
    outs = {"result": ((PAGE, D), BF, HB), "token_gradient": ((PAGE, D), BF, HB), "probs": ((2 * PAIRS, PAGE, PAGE), BF, HB)}
    for k in ORDER[1:]:
        r, n = W_SHAPES[k]
        outs[k] = ((r, n), F32, VM) if remote else ((4, 8 * r, n), BF, HB)
    if remote:
        outs["small"] = ((8, 128), F32, VM)
    else:
        outs.update(sums=((8, D), F32, VM), uplift_sum=((1, FF), F32, VM), intercept_sum=((1, 3 * D), F32, VM))
    scratch = {"w_" + k: buf(4, 8 * r, n) for k, (r, n) in W_SHAPES.items()}
    scratch.update({"g_" + k: buf(4, 8 * W_SHAPES[k][0], W_SHAPES[k][1]) for k in ("combiner", "expander", "reducer")})
    scratch.update(
        feats=buf(PAGE, D), cotangent=buf(PAGE, D), qkv=buf(PAGE, 3 * D),
        wide=buf(4, HALF, D), low_t=buf(D, PAGE), mixture_back=buf(PAGE, D), two=buf(2 * PAGE, D, dtype=F32),
        sum_back=buf(PAGE, D, dtype=F32), r1=buf(PAGE, 128, dtype=F32), activated=buf(FF, PAGE), slope=buf(FF, PAGE),
        load=pltpu.SemaphoreType.DMA((7,)), keep=pltpu.SemaphoreType.DMA((2,)),
    )
    extra = {}
    if remote:
        scratch.update(
            held_reducer=buf(8, 4, 96, D), held_expander=buf(8, 4, 24, FF),
            held_small=buf(8, 4, 8, 128, dtype=F32), pack=buf(8, 128, dtype=F32), packs=buf(4, 64, 128, dtype=F32),
            vec=buf(8, D, dtype=F32), intercept=buf(1, 3 * D, dtype=F32), uplift=buf(1, FF, dtype=F32), sums=buf(8, D, dtype=F32),
            local=pltpu.SemaphoreType.DMA((6,)), send=pltpu.SemaphoreType.DMA((6, 31)), recv=pltpu.SemaphoreType.DMA((6, 32)),
            send2=pltpu.SemaphoreType.DMA((10, 10)), recv2=pltpu.SemaphoreType.DMA((10, 11)), ready=pltpu.SemaphoreType.REGULAR,
        )
        extra = dict(collective_id=0, has_side_effects=True)
    else:
        scratch["give"] = pltpu.SemaphoreType.DMA((5,))
    return call(functools.partial(layer_kernel, remote), ins, outs, scratch, "layer", **extra)


def finish_kernel(*refs):
    mats, small, outs, rest = refs[0:7], refs[7], refs[8:15], refs[15:]
    for a, b in zip(mats, outs):
        b[...] = a[...]
    for k, v in enumerate(VECTORS):
        rest[k][...] = small[k : k + 1, 0 : COUNTS[v]].reshape(COUNTS[v])


def finish(mats, small):
    outs = [jax.ShapeDtypeStruct(m.shape, m.dtype) for m in mats] + [jax.ShapeDtypeStruct((COUNTS[v],), F32) for v in VECTORS]
    got = pl.pallas_call(finish_kernel, out_shape=outs, in_specs=[VM] * 8, out_specs=[VM] * 15, name="finish")(*mats, small)
    return got[:7], dict(zip(VECTORS, got[7:]))


def whole_gather(v):
    return lax.all_gather(v, ("dp", "fsdp"), axis=0, tiled=True)


def whole_scatter(v):
    v = lax.psum_scatter(v.astype(F32), "dp", scatter_dimension=0, tiled=True)
    return lax.psum_scatter(v.astype(BF), "fsdp", scatter_dimension=0, tiled=True).astype(F32)


def cut(rows, sizes):
    parts = []
    at = 0
    for size in sizes:
        parts.append(rows[..., at : at + size])
        at += size
    return parts


def local(
    tokens, coordinates, lengths, cotangent, projector, intercept, relative, combiner, baseline,
    stretch, center, expander, uplift, reducer, offset, rescale, recenter, remote,
):
    vectors = dict(zip(VECTORS, (intercept, uplift, baseline, stretch, center, offset, rescale, recenter)))
    weights = dict(zip(ORDER[1:], (projector, relative, combiner, expander, reducer)))
    if remote:
        f = layer(tokens, coordinates, lengths, cotangent, weights, vectors, True)
        (*mats, result, token_change), small = finish([getattr(f, k) for k in ORDER[1:]] + [f.result, f.token_gradient], f.small)
        share = dict(zip(ORDER[1:], mats))
    else:
        sizes = [v.shape[0] for v in vectors.values()]
        rows = whole_gather(jnp.concatenate(list(vectors.values()))[None])
        wide = {k: v.reshape(1, -1).astype(F32) for k, v in zip(VECTORS, cut(rows, sizes))}
        table_rows = jnp.concatenate([wide[k] for k in VEC_ROWS] + [jnp.zeros((2, D), F32)])
        full = {k: whole_gather(m) for k, m in weights.items()}
        f = layer(
            tokens, coordinates, lengths, cotangent, full, {"vec": table_rows, "intercept": wide["intercept"], "uplift": wide["uplift"]}, False
        )
        change = {k: getattr(f, k).reshape(-1, W_SHAPES[k][1]) for k in ORDER[1:]}
        change["projector"] = change["projector"].reshape(D, 3, 3, PIECE).transpose(0, 2, 1, 3).reshape(D, 3 * D)
        share = {k: whole_scatter(v) for k, v in change.items()}
        sums = [f.intercept_sum[0], f.uplift_sum[0]] + [f.sums[k] for k in range(6)]
        stacked = jnp.concatenate([v.reshape(rows.shape[0], -1) for v in sums], axis=1)
        small = dict(zip(VECTORS, cut(whole_scatter(stacked)[0], sizes)))
        result, token_change = f.result, f.token_gradient
    return (
        result, token_change, share["projector"], small["intercept"], share["relative"], share["combiner"], small["baseline"],
        small["stretch"], small["center"], share["expander"], small["uplift"], share["reducer"], small["offset"], small["rescale"],
        small["recenter"],
    )


def solution(mesh):
    rows, line = P(("dp", "fsdp"), None), P(("dp", "fsdp"))
    remote = (mesh.shape["dp"], mesh.shape["fsdp"]) == (NZ * NY, NX * NC)
    return jax.shard_map(
        functools.partial(local, remote=remote),
        mesh=mesh,
        in_specs=(rows, P(None, ("dp", "fsdp")), line, rows, rows, line, rows, rows, line, line, line, rows, line, rows, line, line, line),
        out_specs=(rows, rows, rows, line, rows, rows, line, line, line, rows, line, rows, line, line, line),
        check_vma=False,
    )
```

```python
import functools
import types

import jax
import jax.numpy as jnp
import numpy as np
from jax import lax
from jax.experimental import pallas as pl
from jax.experimental.pallas import tpu as pltpu
from jax.sharding import PartitionSpec as P

MESH = pl.DeviceIdType.MESH
NZ, NY, NX, NC = 4, 2, 2, 2


PAGE = 512
D = 768
FF = 3072
HALF = 384
PAIRS = 6
SCALE = 192.0 ** -0.5
EPSILON = 1e-12
NEGATIVE = -1e30
BF = jnp.bfloat16
F32 = jnp.float32
PIECE = 256
TALL = 256
SUM_BASELINE, SUM_STRETCH, SUM_CENTER, SUM_OFFSET, SUM_RESCALE, SUM_RECENTER = range(6)
VM = pl.BlockSpec(memory_space=pltpu.VMEM)
HB = pl.BlockSpec(memory_space=pl.ANY)
SM = pl.BlockSpec(memory_space=pltpu.SMEM)
BIG = 63 << 20
W_SHAPES = {"projector": (24, 2304), "relative": (48, 768), "combiner": (24, 768), "expander": (24, 3072), "reducer": (96, 768)}
VECTORS = ("intercept", "uplift", "baseline", "stretch", "center", "offset", "rescale", "recenter")
ORDER = ("small", "projector", "relative", "combiner", "expander", "reducer")
COUNTS = {"intercept": 72, "uplift": 96, "baseline": 24, "stretch": 24, "center": 24, "offset": 24, "rescale": 24, "recenter": 24}
FREQUENCY = np.exp(-np.log(10000.0) * np.arange(192) / 192).astype(np.float32)[:, None]
VEC_ROWS = VECTORS[2:]


class Place:
    def __init__(self):
        d = lax.axis_index("dp")
        f = lax.axis_index("fsdp")
        self.z, self.y = d // NY, d % NY
        self.x, self.c = f // NC, f % NC
        z, y, x, c = self.z, self.y, self.x, self.c
        self.y1, self.x1 = y + (1 - c) * (1 - 2 * y), x + c * (1 - 2 * x)
        self.y2, self.x2 = y + c * (1 - 2 * y), x + (1 - c) * (1 - 2 * x)
        self.yd, self.xd = 1 - y, 1 - x
        self.first = (z * NY + self.y1, self.x1 * NC + c)
        self.second = (z * NY + self.y2, self.x2 * NC + c)
        self.sibling = (z * NY + y, x * NC + 1 - c)

    def along_z(self, z):
        return (z * NY + self.y, self.x * NC + self.c)

    def peers(self):
        return [self.first, self.second, self.sibling] + [self.along_z((self.z + s) % NZ) for s in (1, 2, 3)]


def enter(place):
    barrier = pltpu.get_barrier_semaphore()
    peers = place.peers()
    for peer in peers:
        pl.semaphore_signal(barrier, inc=1, device_id=peer, device_id_type=MESH)
    pl.semaphore_wait(barrier, len(peers))


def nn(a, b):
    return jnp.dot(a, b, preferred_element_type=F32)


def nt(a, b):
    return lax.dot_general(a, b, (((1,), (1,)), ((), ())), preferred_element_type=F32)


def span(i, size):
    return pl.ds(pl.multiple_of(i * size, size), size)


def own_lanes(e, rows):
    lane = lax.broadcasted_iota(jnp.int32, (rows, 128), 1)
    return lane < 64 if e == 0 else lane >= 64


def only(e, v):
    return jnp.where(own_lanes(e, v.shape[0]), v, jnp.zeros_like(v))


def only_rows(e, v):
    row = lax.broadcasted_iota(jnp.int32, v.shape, 0)
    return jnp.where(row < 64 if e == 0 else row >= 64, v, jnp.zeros_like(v))


def project(tokens, projector, intercept, qkv):
    @pl.loop(0, 9)
    def _(n):
        cols = span(n, PIECE)
        qkv[:, cols] = (nn(tokens[...], projector[:, cols]) + intercept[:, cols]).astype(BF)


def table(relative, side, half, cols):
    return relative[2 * side : 2 * side + 2, half * 192 : (half + 1) * 192, cols].reshape(HALF, 128)


def turn(weights, feats, out, rows):
    ws, wc = weights[:, :HALF], weights[:, HALF:]
    c = feats[rows, :HALF].astype(F32)
    s = feats[rows, HALF:].astype(F32)
    out[rows, :HALF] = (ws * s + wc * c).astype(BF)
    out[rows, HALF:] = (wc * s - ws * c).astype(BF)


def mean(v):
    return jnp.sum(v, axis=1, keepdims=True) * (1.0 / D)


def first_norm(tokens, mixture, combiner, vec, hold, n1, r1, low):
    @pl.loop(0, 3)
    def _(n):
        cols = span(n, PIECE)
        hold[:, cols] = nn(mixture[...], combiner[:, cols])

    @pl.loop(0, PAGE // TALL)
    def _(i):
        rows = span(i, TALL)
        v = tokens[rows, :].astype(F32) + hold[rows, :] + vec.baseline[...]
        v = v - mean(v)
        r = lax.rsqrt(mean(v * v) + EPSILON)
        v = v * r
        n1[rows, :] = v
        r1[rows, :] = jnp.broadcast_to(r, (TALL, 128))
        low[rows, :] = (v * vec.stretch[...] + vec.center[...]).astype(BF)


def second_norm(n1, cotangent, vec, hold, reduced_back, second_back, result, sums):
    zero = jnp.zeros((8, D), F32)

    def fold(v):
        return jnp.sum(v.reshape(TALL // 8, 8, D), axis=0)

    def body(i, carry):
        rescale_sum, recenter_sum, offset_sum = carry
        rows = span(i, TALL)
        v = (n1[rows, :] * vec.stretch[...] + vec.center[...]) + hold[rows, :] + vec.offset[...]
        v = v - mean(v)
        r = lax.rsqrt(mean(v * v) + EPSILON)
        v = v * r
        g = cotangent[rows, :].astype(F32)
        result[rows, :] = (v * vec.rescale[...] + vec.recenter[...]).astype(BF)
        u = g * vec.rescale[...]
        back = r * (u - mean(u) - v * mean(u * v))
        second_back[rows, :] = back
        low = back.astype(BF)
        reduced_back[rows, :] = low
        return (rescale_sum + fold(g * v), recenter_sum + fold(g), offset_sum + fold(low.astype(F32)))

    a, b, c = lax.fori_loop(0, PAGE // TALL, body, (zero, zero, zero))
    for k, v in ((SUM_RESCALE, a), (SUM_RECENTER, b), (SUM_OFFSET, c)):
        sums[k : k + 1, :] = jnp.sum(v, axis=0, keepdims=True)


def first_back(total, n1, r1, vec, branch_back, sums):
    zero = jnp.zeros((8, D), F32)

    def fold(v):
        return jnp.sum(v.reshape(TALL // 8, 8, D), axis=0)

    def body(i, carry):
        stretch_sum, center_sum, baseline_sum = carry
        rows = span(i, TALL)
        b = total[rows, :]
        v = n1[rows, :]
        u = b * vec.stretch[...]
        back = r1[rows, :1] * (u - mean(u) - v * mean(u * v))
        total[rows, :] = back
        low = back.astype(BF)
        branch_back[rows, :] = low
        return (stretch_sum + fold(b * v), center_sum + fold(b), baseline_sum + fold(low.astype(F32)))

    a, b, c = lax.fori_loop(0, PAGE // TALL, body, (zero, zero, zero))
    for k, v in ((SUM_STRETCH, a), (SUM_CENTER, b), (SUM_BASELINE, c)):
        sums[k : k + 1, :] = jnp.sum(v, axis=0, keepdims=True)


def branch_grads(mixture, branch_back, combiner, grad_combiner, mixture_back):
    @pl.loop(0, 3)
    def _(n):
        cols = span(n, PIECE)
        grad_combiner[cols, :] = nn(mixture[:, cols].T, branch_back[...]).astype(BF)
        mixture_back[:, cols] = nt(branch_back[...], combiner[cols, :]).astype(BF)


def flat(ref):
    return ref.reshape(ref.shape[0] * ref.shape[1], ref.shape[2])


def name_refs(groups, refs):
    out = []
    at = 0
    for g in groups:
        out.append(types.SimpleNamespace(**dict(zip(g, refs[at : at + len(g)]))))
        at += len(g)
    return out


def call(kernel, ins, outs, scratch, name, **params):
    names = (tuple(ins), tuple(outs), tuple(scratch))
    got = pl.pallas_call(
        functools.partial(kernel, names),
        out_shape=[jax.ShapeDtypeStruct(s, d) for s, d, _ in outs.values()],
        in_specs=[sp for _, sp in ins.values()],
        out_specs=[sp for _, _, sp in outs.values()],
        scratch_shapes=list(scratch.values()),
        compiler_params=pltpu.CompilerParams(vmem_limit_bytes=BIG, **params),
        name=name,
    )(*[a for a, _ in ins.values()])
    return types.SimpleNamespace(**dict(zip(outs, got)))


def buf(*shape, dtype=BF):
    return pltpu.VMEM(shape, dtype)


class Gather:
    def __init__(self, place, shards, full, local, send, recv):
        self.p, self.shards, self.full = place, shards, full
        self.local, self.send, self.recv = local, send, recv
        self.sent = []

    def remote(self, w, src, dst, s, r, device):
        return pltpu.make_async_remote_copy(
            src_ref=src, dst_ref=dst, send_sem=self.send.at[w, s], recv_sem=self.recv.at[w, r], device_id=device, device_id_type=MESH
        )

    def go(self, make):
        self.remote(*make()).start()
        self.sent.append(make)

    def arrived(self, w, ref, r):
        self.remote(w, ref, ref, 0, r, self.p.sibling).wait_recv()

    def begin(self):
        p = self.p
        for w in range(len(self.shards)):
            pltpu.make_async_copy(self.shards[w], self.own(w, p.z), self.local.at[w]).start()
            for s in (1, 2, 3):
                self.go(lambda w=w, s=s: (w, self.shards[w], self.own(w, p.z), s - 1, p.z, p.along_z((p.z + s) % NZ)))

    def rows(self, w, y, x, c):
        count = self.shards[w].shape[0]
        return pl.ds(pl.multiple_of(((y * NX + x) * NC + c) * count, 8), count)

    def own(self, w, z):
        p = self.p
        return self.full[w].at[z, self.rows(w, p.y, p.x, p.c)]

    def block(self, w, at):
        p = self.p
        y, x = {"own": (p.y, p.x), "first": (p.y1, p.x1), "second": (p.y2, p.x2), "across": (p.yd, p.xd)}[at]
        return self.full[w].at[:, self.rows(w, y, x, p.c)]

    def pass_on(self, w, at, *moves):
        for s, r, device in moves:
            self.go(lambda s=s, r=r, device=device: (w, self.block(w, at), self.block(w, at), s, r, device))

    def a(self, w):
        p = self.p
        pltpu.make_async_copy(self.shards[w], self.own(w, p.z), self.local.at[w]).wait()
        for s in (1, 2, 3):
            zs = (p.z + s) % NZ
            self.arrived(w, self.own(w, zs), zs)
        self.pass_on(w, "own", (3, 4, p.first), (4, 5, p.second), (5, 7, p.sibling))

    def b(self, w):
        p = self.p
        self.arrived(w, self.block(w, "first"), 4)
        self.pass_on(w, "first", (6, 6, p.second), (7, 8, p.sibling))

    def c(self, w):
        p = self.p
        self.arrived(w, self.block(w, "second"), 5)
        self.pass_on(w, "second", (8, 9, p.sibling))
        self.arrived(w, self.block(w, "across"), 6)
        self.pass_on(w, "across", (9, 10, p.sibling))

    def d(self, w):
        for r in range(7, 11):
            self.arrived(w, self.block(w, "own"), r)

    def end(self):
        for make in self.sent:
            self.remote(*make()).wait_send()


class Gather2(Gather):
    def shard(self, w, at, z):
        p = self.p
        y, x = {"own": (p.y, p.x), "first": (p.y1, p.x1), "second": (p.y2, p.x2), "across": (p.yd, p.xd)}[at]
        return self.full[w].at[z, self.rows(w, y, x, p.c)]

    def level(self, k):
        return (self.p.z + k) % NZ

    def spread(self, w, k, source=None):
        p = self.p
        for j, (r, device) in enumerate(((4, p.first), (8, p.second), (16, p.sibling))):

            def make(j=j, r=r, device=device):
                z = self.level(k)
                ref = self.shard(w, "own", z)
                return w, ref if source is None else source, ref, 3 + 3 * k + j, r + z, device

            self.go(make)

    def begin(self, w):
        p = self.p
        pltpu.make_async_copy(self.shards[w], self.own(w, p.z), self.local.at[w]).start()
        for s in (1, 2, 3):
            self.go(lambda s=s: (w, self.shards[w], self.own(w, p.z), s - 1, p.z, p.along_z((p.z + s) % NZ)))
        self.spread(w, 0, self.shards[w])

    def a(self, w):
        pltpu.make_async_copy(self.shards[w], self.own(w, self.p.z), self.local.at[w]).wait()
        for k in (1, 2, 3):
            self.arrived(w, self.shard(w, "own", self.level(k)), self.level(k))
            self.spread(w, k)

    def b(self, w, ks=range(NZ)):
        p = self.p
        for k in ks:
            self.arrived(w, self.shard(w, "first", self.level(k)), 4 + self.level(k))
            for j, (r, device) in enumerate(((12, p.second), (20, p.sibling))):

                def make(k=k, j=j, r=r, device=device):
                    z = self.level(k)
                    ref = self.shard(w, "first", z)
                    return w, ref, ref, 15 + 2 * k + j, r + z, device

                self.go(make)

    def b_part(self, w):
        return lambda k: self.b(w, [k])

    def hand(self, w, at, slot, r, s):
        for k in range(NZ):
            self.arrived(w, self.shard(w, at, self.level(k)), r + self.level(k))

            def make(k=k):
                z = self.level(k)
                ref = self.shard(w, at, z)
                return w, ref, ref, s + k, slot + z, self.p.sibling

            self.go(make)

    def c(self, w):
        self.hand(w, "second", 24, 8, 23)

    def e(self, w):
        self.hand(w, "across", 28, 12, 27)

    def d(self, w):
        for r in range(16, 32):
            self.arrived(w, self.own(w, 0), r)


def ramp(start, width):
    col = lax.broadcasted_iota(jnp.int32, (32, D), 1) + start
    mine = jnp.floor((col.astype(F32) + 0.5) * (1.0 / width)).astype(jnp.int32) == lax.broadcasted_iota(jnp.int32, (32, D), 0)
    col = lax.broadcasted_iota(jnp.int32, (128, D), 1) + start
    rest = col - jnp.floor((col.astype(F32) + 0.5) * (1.0 / width)).astype(jnp.int32) * width
    pick = jnp.where(rest == lax.broadcasted_iota(jnp.int32, (128, D), 0), 1.0, 0.0).astype(BF)
    return mine, pick


def widen(packs, vec, wide):
    k = 0
    for name, ref in (("intercept", wide.intercept), ("uplift", wide.uplift)):
        rows = packs[pl.ds(k, 32, stride=8), :].astype(BF)
        for start in range(0, 32 * COUNTS[name], D):
            mine, pick = ramp(start, COUNTS[name])
            ref[:, start : start + D] = jnp.sum(jnp.where(mine, nn(rows, pick), 0.0), axis=0, keepdims=True)
        k += 1
    mine, pick = ramp(0, 24)
    for j in range(6):
        rows = packs[pl.ds(k + j, 32, stride=8), :].astype(BF)
        vec[j : j + 1, :] = jnp.sum(jnp.where(mine, nn(rows, pick), 0.0), axis=0, keepdims=True)


def narrow(sums, intercept_sum, uplift_sum, packs):
    def one(v, mine, pick):
        v = jnp.where(mine, v, 0.0)
        high = v.astype(BF)
        return nt(high, pick) + nt((v - high.astype(F32)).astype(BF), pick)

    for k, (name, ref) in enumerate((("intercept", intercept_sum), ("uplift", uplift_sum))):
        total = jnp.zeros((32, 128), F32)
        for start in range(0, 32 * COUNTS[name], D):
            total += one(ref[:, start : start + D], *ramp(start, COUNTS[name]))
        packs[pl.ds(k, 32, stride=8), :] = total
    mine, pick = ramp(0, 24)
    for j in range(6):
        packs[pl.ds(2 + j, 32, stride=8), :] = one(sums[j : j + 1, :], mine, pick)


def sinusoids(frequency, coordinates, feats_t, feats):
    for c in (0, 1):
        angles = frequency[...] * coordinates[c : c + 1, :].astype(F32)
        feats_t[c * 192 : (c + 1) * 192, :] = jnp.cos(angles).astype(BF)
        feats_t[HALF + c * 192 : HALF + (c + 1) * 192, :] = jnp.sin(angles).astype(BF)
    for k in range(6):
        feats[:, k * 128 : (k + 1) * 128] = feats_t[k * 128 : (k + 1) * 128, :].T


class Scatter:
    ROLES = ("own", "first", "second", "across")

    def __init__(self, place, counts, grads, blocks, outs, send, recv):
        self.p, self.counts, self.grads, self.blocks, self.outs = place, counts, grads, blocks, outs
        self.send, self.recv = send, recv
        self.sent = []

    def remote(self, w, src, dst, s, r, device):
        return pltpu.make_async_remote_copy(
            src_ref=src, dst_ref=dst, send_sem=self.send.at[w, s], recv_sem=self.recv.at[w, r], device_id=device, device_id_type=MESH
        )

    def go(self, make):
        self.remote(*make()).start()
        self.sent.append(make)

    def arrived(self, w, ref, r):
        self.remote(w, ref, ref, 0, r, self.p.sibling).wait_recv()

    def at(self, role):
        p = self.p
        return {"own": (p.y, p.x), "first": (p.y1, p.x1), "second": (p.y2, p.x2), "across": (p.yd, p.xd)}[role]

    def part(self, w, y, x, c):
        count = self.counts[w]
        return self.grads[w].at[:, pl.ds(pl.multiple_of(((y * NX + x) * NC + c) * count, 8), count)]

    def begin(self, w):
        theirs = {"own": "own", "first": "second", "second": "first", "across": "across"}
        for b in (3, 2, 1, 0):
            role = theirs[self.ROLES[b]]
            self.go(lambda b=b, role=role: (w, self.part(w, *self.at(role), 1 - self.p.c), self.blocks[w](b), b, b, self.p.sibling))

    def add(self, w, b, other):
        mine = self.blocks[w](b)

        @pl.loop(0, NZ)
        def _(k):
            mine[k] = (mine[k].astype(F32) + other[k].astype(F32)).astype(mine.dtype)

    def s(self, w):
        block = self.blocks[w]
        for b in (3, 2, 1, 0):
            self.arrived(w, block(b), b)
            self.add(w, b, self.part(w, *self.at(self.ROLES[b]), self.p.c))
            if b >= 2:
                self.go(lambda b=b: (w, block(b), block(7 - b), 7 - b, 7 - b, self.p.second))

    def x(self, w):
        block = self.blocks[w]
        self.arrived(w, block(4), 4)
        self.add(w, 1, block(4))
        self.go(lambda: (w, block(1), block(6), 6, 6, self.p.first))
        self.arrived(w, block(5), 5)
        self.add(w, 0, block(5))

    def f(self, w):
        p = self.p
        block = self.blocks[w]
        self.arrived(w, block(6), 6)
        self.add(w, 0, block(6))
        for s in (1, 2, 3):

            def make(s=s):
                zt = (p.z + s) % NZ
                return w, block(0).at[zt], block(7).at[p.z], 6 + s, 7 + p.z, p.along_z(zt)

            self.go(make)

    def z(self, w):
        p = self.p
        total = self.blocks[w](0)[p.z].astype(F32)
        for s in (1, 2, 3):
            zs = (p.z + s) % NZ
            self.arrived(w, self.blocks[w](7).at[zs], 7 + zs)
            total += self.blocks[w](7)[zs].astype(F32)
        self.outs[w](total)

    def end(self):
        for make in self.sent:
            self.remote(*make()).wait_send()


def pool_at(n):
    return pl.ds(pl.multiple_of((n >> 1) * 512, 512), 512), pl.ds(pl.multiple_of((n & 1) * PIECE, PIECE), PIECE)


def attend(p, qkv, relative, feats, live, places, slots, mixture):
    lanes = span(p, 128)
    q2 = qkv[:, lanes]
    k2 = qkv[:, span(p + PAIRS, 128)]
    v2 = qkv[:, span(p + 2 * PAIRS, 128)]
    every = slice(None)
    mixed = []
    tables = [jnp.concatenate([table(relative, side, half, lanes) for half in (0, 1)], axis=0) for side in (0, 1)]
    for e in (0, 1):
        left, right = places[2 * e], places[2 * e + 1]
        q = only(e, q2)
        k = only(e, k2)
        turn(nt(q, tables[0]), feats, left, every)
        turn(nt(k, tables[1]), feats, right, every)
    for e in (0, 1):
        left, right = places[2 * e], places[2 * e + 1]
        scores = (nt(left[...], feats[...]) + nt(only(e, q2), k2) + nt(feats[...], right[...])) * SCALE
        key = lax.broadcasted_iota(jnp.int32, scores.shape, 1)
        scores = jnp.where(key < live, scores, NEGATIVE)
        powers = jnp.exp(scores - jnp.max(scores, axis=1, keepdims=True))
        share = (powers / jnp.sum(powers, axis=1, keepdims=True)).astype(BF)
        slots[e][...] = share
        mixed.append(nn(share, v2))
    mixture[:, lanes] = jnp.where(own_lanes(0, PAGE), mixed[0], mixed[1]).astype(BF)


def feed_pool(low, expander, uplift, activated, slope):
    @pl.loop(0, FF // PIECE)
    def _(n):
        cols = span(n, PIECE)
        v = nn(low[...], expander[:, cols]) + uplift[:, cols]
        half = 0.5 * lax.erf(v * (0.5 ** 0.5)) + 0.5
        activated[pool_at(n)] = (v * half).astype(BF)
        slope[pool_at(n)] = (half + v * (jnp.exp(v * v * -0.5) * 0.3989422804014327)).astype(BF)


def reduce_pool(activated, reducer, hold):
    @pl.loop(0, 3)
    def _(n):
        cols = span(n, PIECE)
        total = nn(activated[0:512, :], reducer[0:512, cols])
        for j in range(1, 6):
            total += nn(activated[512 * j : 512 * (j + 1), :], reducer[512 * j : 512 * (j + 1), cols])
        hold[:, cols] = total


def reducer_gradient(activated, reduced_back, grad_reducer):
    @pl.loop(0, FF // PIECE)
    def _(n):
        grad_reducer[span(n, PIECE), :] = nn(activated[pool_at(n)].T, reduced_back[...]).astype(BF)


def expander_gradient(low_t, slope, reduced_back, reducer, expander, grad_expander, uplift_sum, hook):
    @pl.loop(0, FF // PIECE)
    def _(n):
        cols = span(n, PIECE)
        inner = (nt(reduced_back[...], reducer[cols, :]) * slope[pool_at(n)].astype(F32)).astype(BF)
        slope[pool_at(n)] = inner
        uplift_sum[:, cols] = jnp.sum(inner.astype(F32), axis=0, keepdims=True)
        grad_expander[:, cols] = nn(low_t[...], inner).astype(BF)
        hook(n)


def expander_back(slope, expander, total):
    @pl.loop(0, 3)
    def _(n):
        cols = span(n, PIECE)
        part = nt(slope[0:512, :], expander[cols, 0:512])
        for j in range(1, 6):
            part += nt(slope[512 * j : 512 * (j + 1), :], expander[cols, 512 * j : 512 * (j + 1)])
        total[:, cols] += part


def back_setup(feats, top, bottom):
    for k in range(6):
        block = feats[:, k * 128 : (k + 1) * 128].T
        for h in (0, 1):
            kind, coordinate, at = (2 * k + h) // 6, (2 * k + h) // 3 % 2, (2 * k + h) % 3
            row = coordinate * HALF + kind * 192 + at * 64
            for out in (top, bottom):
                out[row : row + 64, :] = block[h * 64 : (h + 1) * 64, :]


def attend_back(p, qkv, mixture_back, slots, ready, done, relative, top, bottom, score_backs, two, grad_relative, back_t):
    lanes = span(p, 128)
    q2 = qkv[:, lanes]
    k2 = qkv[:, span(p + PAIRS, 128)]
    v2 = qkv[:, span(p + 2 * PAIRS, 128)]
    m2 = mixture_back[:, lanes]
    top[D:, :] = k2.T
    bottom[D:, :] = q2.T
    mt = m2.T
    values = []
    for e in (0, 1):
        back = nt(only(e, m2), v2)
        ready(e)
        share = slots[e][...].astype(F32)
        score_backs[e][...] = (share * (back - jnp.sum(share * back, axis=1, keepdims=True)) * SCALE).astype(BF)
        values.append(nn(mt, slots[e][...]))
        done(e)
    row = lax.broadcasted_iota(jnp.int32, (128, PAGE), 0)
    back_t[span(p + 2 * PAIRS, 128), :] = jnp.where(row < 64, values[0], values[1]).astype(BF)
    for side, source, dot, t2 in ((0, top, nt, q2), (1, bottom, nn, k2)):
        text = []
        backward = jnp.concatenate([relative[2 * side + c, :, lanes].T for c in (0, 1)], axis=1)
        for e in (0, 1):
            both = []
            for c in (0, 1):
                rows = slice(c * HALF, (c + 1) * HALF) if c == 0 else slice(HALF, D + 128)
                lifted = dot(source[rows, :], score_backs[e][...])
                cos = top[c * HALF : c * HALF + 192, :].astype(F32)
                sin = top[c * HALF + 192 : (c + 1) * HALF, :].astype(F32)
                g1, g2 = lifted[0:192], lifted[192:HALF]
                both += [(g1 * sin - g2 * cos).astype(BF), (g1 * cos + g2 * sin).astype(BF)]
            turned = jnp.concatenate(both, axis=0)
            text.append(nn(backward, turned) + lifted[HALF:])
            grad = nn(turned, only(e, t2))
            kept = two.at[0:D, 128 * side : 128 * (side + 1)]
            if e == 0:
                kept[...] = grad
            else:
                grad_relative[2 * side : 2 * side + 2, :, lanes] = (kept[...] + grad).astype(BF).reshape(2, HALF, 128)
        back_t[span(p + side * PAIRS, 128), :] = jnp.where(row < 64, text[0], text[1]).astype(BF)


def projector_gradient(j, tokens_t, back_t, grad_projector, intercept_sum):
    @pl.loop(0, 3)
    def _(k):
        cols = pl.ds(pl.multiple_of(k * D + j * PIECE, PIECE), PIECE)
        b = back_t[cols, :]
        intercept_sum[:, cols] = nt(jnp.ones((8, PAGE), BF), b)[0:1, :]
        grad_projector[:, :, span(3 * j + k, PIECE)] = nt(tokens_t[...], b).astype(BF).reshape(4, 192, PIECE)


def token_gradient(projector, back_t, sum_back, out):
    @pl.loop(0, 3)
    def _(n):
        cols = span(n, PIECE)
        out[:, cols] = (sum_back[:, cols] + nn(projector[cols, :], back_t[...]).T).astype(BF)


def transposed(src, dst):
    for k in range(6):
        dst[k * 128 : (k + 1) * 128, :] = src[:, k * 128 : (k + 1) * 128].T


def layer_kernel(remote, names, *refs):
    i, o, s = name_refs(names, refs)
    full = [getattr(s, "w_" + w) for w in ORDER[1:]]
    shards = [getattr(i, w) for w in ORDER[1:]]
    take_tokens = pltpu.make_async_copy(i.tokens, s.mixture_back, s.load.at[0])
    take_cotangent = pltpu.make_async_copy(i.cotangent, s.cotangent, s.load.at[1])
    take_tokens.start()
    if remote:
        p = Place()
        enter(p)
        s.pack[...] = jnp.zeros((8, 128), F32)
        for k, v in enumerate(VECTORS):
            n = COUNTS[v]
            s.pack[k : k + 1, 0:n] = getattr(i, v)[...].astype(F32).reshape(1, n)
        g = Gather2(p, [s.pack] + shards, [s.packs] + full, s.local, s.send, s.recv)
        for k in range(6):
            g.begin(k)
        vec_ref, intercept, uplift = s.vec, s.intercept, s.uplift
    else:
        takes = [pltpu.make_async_copy(a, flat(b), s.load.at[2 + k]) for k, (a, b) in enumerate(zip(shards, full))]
        for t in takes:
            t.start()
        vec_ref, intercept, uplift = i.vec, i.intercept, i.uplift
    w = types.SimpleNamespace(**{n: flat(ref) for n, ref in zip(ORDER[1:], full)})
    vec = types.SimpleNamespace(**{v: vec_ref.at[k : k + 1] for k, v in enumerate(VEC_ROWS)})
    live = i.lengths[0]
    wide = flat(s.wide)
    low, mixture, reduced_back = (wide.at[k * PAGE : (k + 1) * PAGE] for k in range(3))
    n1, hold = s.two.at[0:PAGE], s.two.at[PAGE : 2 * PAGE]
    places = [flat(s.g_reducer).at[k * PAGE : (k + 1) * PAGE] for k in range(4)]
    activated, slope = s.activated, s.slope

    sinusoids(i.frequency, i.coordinates, s.low_t, s.feats)
    if remote:
        g.a(0)
        g.a(1); g.b(0)
        g.a(2); g.b(1); g.c(0); g.e(0); g.d(0)
        g.a(3); g.b(2); g.c(1)
        widen(s.packs.reshape(256, 128), s.vec, types.SimpleNamespace(intercept=s.intercept, uplift=s.uplift))
        g.a(4); g.e(1); g.b(3); g.c(2); g.d(1)
        part = g.b_part(5)
        early = {0: [(g.c, 3), (part, 0)], 1: [(part, 1), (part, 2)], 2: [(part, 3), (g.c, 4), (g.e, 3)], 3: [(g.d, 3)], 4: [(g.c, 5), (g.e, 4)]}
    else:
        for t in takes:
            t.wait()
        early = {}
    take_tokens.wait()
    project(s.mixture_back, w.projector, intercept, s.qkv)
    if remote:
        g.e(2); g.a(5); g.b(4); g.d(2)

    slots = [s.low_t.at[0:PAGE], s.cotangent.at[:, 0:PAGE]]

    def keep(q, e):
        return pltpu.make_async_copy(slots[e], o.probs.at[2 * q + e], s.keep.at[e])

    def fetch(q, e):
        return pltpu.make_async_copy(o.probs.at[2 * q + e], slots[e], s.keep.at[e])

    def hooks(q, table_of):
        for k, steps in table_of.items():

            @pl.when(q == k)
            def _(steps=steps):
                run(steps)

    @pl.loop(0, PAIRS)
    def _(q):
        @pl.when(q >= 1)
        def _():
            keep(q - 1, 0).wait()
            keep(q - 1, 1).wait()

        attend(q, s.qkv, s.w_relative, s.feats, live, places, slots, mixture)
        keep(q, 0).start()
        keep(q, 1).start()
        hooks(q, early)

    keep(PAIRS - 1, 0).wait()
    keep(PAIRS - 1, 1).wait()
    take_cotangent.start()

    first_norm(s.mixture_back, mixture, w.combiner, vec, hold, n1, s.r1, low)
    if remote:
        g.d(4)
    feed_pool(low, w.expander, uplift, activated, slope)
    if remote:
        g.e(5)
    transposed(low, s.low_t)
    if remote:
        g.d(5)
    take_cotangent.wait()
    reduce_pool(activated, w.reducer, hold)
    second_norm(n1, s.cotangent, vec, hold, reduced_back, s.sum_back, s.cotangent, o.sums if not remote else s.sums)
    give_result = pltpu.make_async_copy(s.cotangent, o.result, s.load.at[1])
    give_result.start()
    sums, uplift_sum, intercept_sum = (s.sums, s.uplift, s.intercept) if remote else (o.sums, o.uplift_sum, o.intercept_sum)
    reducer_gradient(activated, reduced_back, flat(s.g_reducer))
    grad_relative = s.w_reducer.at[:, 0:HALF]
    grad_projector = s.w_expander.at[:, :, 0 : 3 * D]
    if remote:
        g.end()

        def whole(ref):
            def put(v):
                ref[...] = v

            return put

        def relative_part(j):
            def put(v):
                o.relative[:, j * PIECE : (j + 1) * PIECE] = v

            return put

        def projector_part(j):
            def put(v):
                for k in range(3):
                    o.projector[:, k * D + j * PIECE : k * D + (j + 1) * PIECE] = v[:, k * PIECE : (k + 1) * PIECE]

            return put

        counts = [96, 24, 24]
        grads = [s.g_reducer, s.g_expander, s.g_combiner]
        blocks = [
            lambda b: s.held_reducer.at[b],
            lambda b: s.held_expander.at[b],
            lambda b: s.w_expander.at[:, 24 * b : 24 * b + 24, 3 * D :],
        ]
        outs = [whole(o.reducer), whole(o.expander), whole(o.combiner)]
        for j in range(3):
            lanes = slice(j * PIECE, (j + 1) * PIECE)
            counts += [48, 24]
            grads += [s.w_reducer.at[:, 0:HALF, lanes], s.w_expander.at[:, :, j * D : (j + 1) * D]]
            blocks.append(lambda b, lanes=lanes: s.w_reducer.at[:, HALF + 48 * b : HALF + 48 * b + 48, lanes])
            if j < 2:
                blocks.append(lambda b, j=j: s.wide.at[:, 192 * j + 24 * b : 192 * j + 24 * b + 24])
            else:
                blocks.append(lambda b: s.w_combiner.at[:, 24 * b : 24 * b + 24])
            outs += [relative_part(j), projector_part(j)]
        counts.append(8)
        grads.append(s.packs)
        blocks.append(lambda b: s.held_small.at[b])
        outs.append(whole(o.small))
        t = Scatter(p, counts, grads, blocks, outs, s.send2, s.recv2)
        t.begin(0)
    else:
        gives = [
            pltpu.make_async_copy(a, b, s.give.at[k])
            for k, (a, b) in enumerate(
                zip(
                    [s.g_reducer, s.g_expander, s.g_combiner, grad_relative, grad_projector],
                    [o.reducer, o.expander, o.combiner, o.relative, o.projector],
                )
            )
        ]
        gives[0].start()

    def middle(n):
        if remote:
            hooks(n, middle_plan(t))

    expander_gradient(s.low_t, slope, reduced_back, w.reducer, w.expander, flat(s.g_expander), uplift_sum, middle)
    if remote:
        t.begin(1)
    else:
        gives[1].start()
    expander_back(slope, w.expander, s.sum_back)
    first_back(s.sum_back, n1, s.r1, vec, reduced_back, sums)
    if remote:
        t.s(1)
    branch_grads(mixture, reduced_back, w.combiner, flat(s.g_combiner), s.mixture_back)
    fetch(0, 0).start()
    give_result.wait()
    fetch(0, 1).start()
    if remote:
        for peer in p.peers():
            pl.semaphore_signal(s.ready, inc=1, device_id=peer, device_id_type=MESH)
        pl.semaphore_wait(s.ready, 6)
        t.begin(2)
    else:
        gives[2].start()
    top, bottom = activated.at[0:896], activated.at[896:1792]
    score_backs = [activated.at[1792:2304], activated.at[2304:2816]]
    tokens_t, back_t = slope.at[0:D], slope.at[D:]
    back_setup(s.feats, top, bottom)
    again = pltpu.make_async_copy(i.tokens, s.feats, s.load.at[0])
    again.start()
    again.wait()
    transposed(s.feats, tokens_t)
    if remote:
        run(before_plan(t))

    def project_part(j):
        projector_gradient(j, tokens_t, back_t, grad_projector, intercept_sum)

    late = {1: [(project_part, 0)], 3: [(project_part, 1)], 5: [(project_part, 2)]}
    if remote:
        for q, steps in late_plan(t).items():
            late[q] = late.get(q, []) + steps

    @pl.loop(0, PAIRS)
    def _(q):
        def done(e):
            @pl.when(q + 1 < PAIRS)
            def _():
                fetch(q + 1, e).start()

        attend_back(
            q, s.qkv, s.mixture_back, slots, lambda e: fetch(q, e).wait(), done, s.w_relative, top, bottom, score_backs, s.two, grad_relative, back_t
        )
        hooks(q, late)

    if remote:
        t.s(7)
        t.s(8)
        narrow(s.sums, intercept_sum, uplift_sum, s.packs.reshape(256, 128))
        t.begin(9)
    else:
        gives[3].start()
        gives[4].start()
    token_gradient(w.projector, back_t, s.sum_back, s.feats)
    give_tokens = pltpu.make_async_copy(s.feats, o.token_gradient, s.load.at[0])
    give_tokens.start()
    if remote:
        run(after_plan(t))
        t.end()
    else:
        for c in gives:
            c.wait()
    give_tokens.wait()


def middle_plan(t):
    return {4: [(t.s, 0)]}


def before_plan(t):
    return [(t.s, 2)]


def late_plan(t):
    return {
        0: [(t.x, 0)],
        1: [(t.begin, 3), (t.begin, 4)],
        2: [(t.s, 3), (t.s, 4), (t.f, 0), (t.x, 1)],
        3: [(t.begin, 5), (t.begin, 6), (t.x, 2)],
        4: [(t.s, 5), (t.s, 6), (t.f, 1), (t.x, 3), (t.x, 4)],
        5: [(t.begin, 7), (t.begin, 8)],
    }


def after_plan(t):
    return (
        [(t.x, 5), (t.x, 6), (t.f, 2), (t.f, 3), (t.f, 4), (t.x, 7), (t.x, 8), (t.s, 9), (t.z, 0), (t.z, 1), (t.f, 5), (t.f, 6), (t.x, 9)]
        + [(t.z, 2), (t.z, 3), (t.z, 4), (t.f, 7), (t.f, 8), (t.f, 9)] + [(t.z, k) for k in (5, 6, 7, 8, 9)]
    )


def run(steps):
    for step, w in steps:
        step(w)


def layer(tokens, coordinates, lengths, cotangent, weights, vectors, remote):
    ins = {"tokens": (tokens, HB), "coordinates": (coordinates, VM), "lengths": (lengths, SM), "cotangent": (cotangent, HB)}
    ins["frequency"] = (jnp.asarray(FREQUENCY), VM)
    ins.update({k: (weights[k], HB) for k in ORDER[1:]})
    ins.update({k: (v, VM) for k, v in vectors.items()})
    outs = {"result": ((PAGE, D), BF, HB), "token_gradient": ((PAGE, D), BF, HB), "probs": ((2 * PAIRS, PAGE, PAGE), BF, HB)}
    for k in ORDER[1:]:
        r, n = W_SHAPES[k]
        outs[k] = ((r, n), F32, VM) if remote else ((4, 8 * r, n), BF, HB)
    if remote:
        outs["small"] = ((8, 128), F32, VM)
    else:
        outs.update(sums=((8, D), F32, VM), uplift_sum=((1, FF), F32, VM), intercept_sum=((1, 3 * D), F32, VM))
    scratch = {"w_" + k: buf(4, 8 * r, n) for k, (r, n) in W_SHAPES.items()}
    scratch.update({"g_" + k: buf(4, 8 * W_SHAPES[k][0], W_SHAPES[k][1]) for k in ("combiner", "expander", "reducer")})
    scratch.update(
        feats=buf(PAGE, D), cotangent=buf(PAGE, D), qkv=buf(PAGE, 3 * D),
        wide=buf(4, HALF, D), low_t=buf(D, PAGE), mixture_back=buf(PAGE, D), two=buf(2 * PAGE, D, dtype=F32),
        sum_back=buf(PAGE, D, dtype=F32), r1=buf(PAGE, 128, dtype=F32), activated=buf(FF, PAGE), slope=buf(FF, PAGE),
        load=pltpu.SemaphoreType.DMA((7,)), keep=pltpu.SemaphoreType.DMA((2,)),
    )
    extra = {}
    if remote:
        scratch.update(
            held_reducer=buf(8, 4, 96, D), held_expander=buf(8, 4, 24, FF),
            held_small=buf(8, 4, 8, 128, dtype=F32), pack=buf(8, 128, dtype=F32), packs=buf(4, 64, 128, dtype=F32),
            vec=buf(8, D, dtype=F32), intercept=buf(1, 3 * D, dtype=F32), uplift=buf(1, FF, dtype=F32), sums=buf(8, D, dtype=F32),
            local=pltpu.SemaphoreType.DMA((6,)), send=pltpu.SemaphoreType.DMA((6, 31)), recv=pltpu.SemaphoreType.DMA((6, 32)),
            send2=pltpu.SemaphoreType.DMA((10, 10)), recv2=pltpu.SemaphoreType.DMA((10, 11)), ready=pltpu.SemaphoreType.REGULAR,
        )
        extra = dict(collective_id=0, has_side_effects=True)
    else:
        scratch["give"] = pltpu.SemaphoreType.DMA((5,))
    return call(functools.partial(layer_kernel, remote), ins, outs, scratch, "layer", **extra)


def finish_kernel(*refs):
    mats, small, outs, rest = refs[0:7], refs[7], refs[8:15], refs[15:]
    for a, b in zip(mats, outs):
        b[...] = a[...]
    for k, v in enumerate(VECTORS):
        rest[k][...] = small[k : k + 1, 0 : COUNTS[v]].reshape(COUNTS[v])


def finish(mats, small):
    outs = [jax.ShapeDtypeStruct(m.shape, m.dtype) for m in mats] + [jax.ShapeDtypeStruct((COUNTS[v],), F32) for v in VECTORS]
    got = pl.pallas_call(finish_kernel, out_shape=outs, in_specs=[VM] * 8, out_specs=[VM] * 15, name="finish")(*mats, small)
    return got[:7], dict(zip(VECTORS, got[7:]))


def whole_gather(v):
    return lax.all_gather(v, ("dp", "fsdp"), axis=0, tiled=True)


def whole_scatter(v):
    v = lax.psum_scatter(v.astype(F32), "dp", scatter_dimension=0, tiled=True)
    return lax.psum_scatter(v.astype(BF), "fsdp", scatter_dimension=0, tiled=True).astype(F32)


def cut(rows, sizes):
    parts = []
    at = 0
    for size in sizes:
        parts.append(rows[..., at : at + size])
        at += size
    return parts


def local(
    tokens, coordinates, lengths, cotangent, projector, intercept, relative, combiner, baseline,
    stretch, center, expander, uplift, reducer, offset, rescale, recenter, remote,
):
    vectors = dict(zip(VECTORS, (intercept, uplift, baseline, stretch, center, offset, rescale, recenter)))
    weights = dict(zip(ORDER[1:], (projector, relative, combiner, expander, reducer)))
    if remote:
        f = layer(tokens, coordinates, lengths, cotangent, weights, vectors, True)
        (*mats, result, token_change), small = finish([getattr(f, k) for k in ORDER[1:]] + [f.result, f.token_gradient], f.small)
        share = dict(zip(ORDER[1:], mats))
    else:
        sizes = [v.shape[0] for v in vectors.values()]
        rows = whole_gather(jnp.concatenate(list(vectors.values()))[None])
        wide = {k: v.reshape(1, -1).astype(F32) for k, v in zip(VECTORS, cut(rows, sizes))}
        table_rows = jnp.concatenate([wide[k] for k in VEC_ROWS] + [jnp.zeros((2, D), F32)])
        full = {k: whole_gather(m) for k, m in weights.items()}
        f = layer(
            tokens, coordinates, lengths, cotangent, full, {"vec": table_rows, "intercept": wide["intercept"], "uplift": wide["uplift"]}, False
        )
        change = {k: getattr(f, k).reshape(-1, W_SHAPES[k][1]) for k in ORDER[1:]}
        change["projector"] = change["projector"].reshape(D, 3, 3, PIECE).transpose(0, 2, 1, 3).reshape(D, 3 * D)
        share = {k: whole_scatter(v) for k, v in change.items()}
        sums = [f.intercept_sum[0], f.uplift_sum[0]] + [f.sums[k] for k in range(6)]
        stacked = jnp.concatenate([v.reshape(rows.shape[0], -1) for v in sums], axis=1)
        small = dict(zip(VECTORS, cut(whole_scatter(stacked)[0], sizes)))
        result, token_change = f.result, f.token_gradient
    return (
        result, token_change, share["projector"], small["intercept"], share["relative"], share["combiner"], small["baseline"],
        small["stretch"], small["center"], share["expander"], small["uplift"], share["reducer"], small["offset"], small["rescale"],
        small["recenter"],
    )


def solution(mesh):
    rows, line = P(("dp", "fsdp"), None), P(("dp", "fsdp"))
    remote = (mesh.shape["dp"], mesh.shape["fsdp"]) == (NZ * NY, NX * NC)
    return jax.shard_map(
        functools.partial(local, remote=remote),
        mesh=mesh,
        in_specs=(rows, P(None, ("dp", "fsdp")), line, rows, rows, line, rows, rows, line, line, line, rows, line, rows, line, line, line),
        out_specs=(rows, rows, rows, line, rows, rows, line, line, line, rows, line, rows, line, line, line),
        check_vma=False,
    )
```
